128 devices in a mesh: dp: 64 (over y, x, z), tensor: 2 (over core).
Axes of the slice: x: 4, y: 4, z: 4, core: 2. Of those that a mesh axis runs over, the one named last changes fastest.
Arguments:
- tokens: bfloat16 [8192, 1024], P('dp', 'tensor'), may hold values from -6 to 6
- segment_ids: int32 [8192], P('dp'), may hold values from 0 to 7, never falling along the last dimension, each value on 1 to 2048 neighbouring positions
- valid_mask: int32 [8192], P('dp'), may hold values 0 or 1
- norm1_gain: bfloat16 [1024], replicated, may hold values from 0.099609375 to 1.8984375
- in_weight: bfloat16 [3, 1024, 1024], P(None, 'dp', 'tensor'), may hold values from -0.1875 to 0.1875
- conv_weight: bfloat16 [3, 1024], replicated, may hold values from -3.5 to 3.5
- out_weight: bfloat16 [1024, 1024], P('tensor', 'dp'), may hold values from -0.1875 to 0.1875
- norm2_gain: bfloat16 [1024], replicated, may hold values from 0.099609375 to 1.8984375
- gate_weight: bfloat16 [1024, 4608], P('dp', 'tensor'), may hold values from -0.1875 to 0.1875
- up_weight: bfloat16 [1024, 4608], P('dp', 'tensor'), may hold values from -0.1875 to 0.1875
- down_weight: bfloat16 [4608, 1024], P('tensor', 'dp'), may hold values from -0.09375 to 0.09375
- out_cotangent: bfloat16 [8192, 1024], P('dp', 'tensor'), may hold values from -6 to 6
Outputs:
- mixed_out: bfloat16 [8192, 1024], P('dp', 'tensor')
- tokens_grad: float32 [8192, 1024], P('dp', 'tensor')
- norm1_gain_grad: float32 [1024], replicated
- in_weight_grad: float32 [3, 1024, 1024], P(None, 'dp', 'tensor')
- conv_weight_grad: float32 [3, 1024], replicated
- out_weight_grad: float32 [1024, 1024], P('tensor', 'dp')
- norm2_gain_grad: float32 [1024], replicated
- gate_weight_grad: float32 [1024, 4608], P('dp', 'tensor')
- up_weight_grad: float32 [1024, 4608], P('dp', 'tensor')
- down_weight_grad: float32 [4608, 1024], P('tensor', 'dp')
The draws below stay inside these ranges and needn't reach their ends.
All inputs are finite; a program needn't handle non-finite values. No bound on the sum of `valid_mask` on one device may be relied on, other than what follows from the above.
Results may differ from the reference program's by a relative error of at most 0.02.
Values may be sent and summed in bfloat16 or wider, within the bound.
A program may use at most 128 MiB of HBM per device.

```python
import math
import jax
import jax.numpy as jnp
import numpy as np
from jax import lax

D = 1024
FF = 4608
KW = 3
MAXLEN = 2048
TOKENS = 8192
SEQS = 8


def place_ends(values, key, least, largest):
    dims = values.shape
    index_at = [jax.random.randint(jax.random.fold_in(key, axis), (), 0, dims[axis]) for axis in range(len(dims))]
    values = values.at[tuple(index_at)].set(least)
    longest = dims.index(max(dims))
    index_at[longest] = (index_at[longest] + 1) % dims[longest]
    return values.at[tuple(index_at)].set(largest)


def block_levels(stream_key, dims, split, smallest, largest):
    factor_of, own = 1.0, jax.random.fold_in(stream_key, 6)
    for dim, shards_of in split:
        draws = jnp.exp(jax.random.uniform(jax.random.fold_in(own, dim), (shards_of,), jnp.float32, smallest / len(split), largest / len(split)))
        factor_of = factor_of * jnp.repeat(draws, dims[dim] // shards_of).reshape([-1 if axis == dim else 1 for axis in range(len(dims))])
    return factor_of


def profile(amount, total, most, slope):
    weights = [(1 << 20) // math.isqrt(rank ** slope) + 1 for rank in range(2, amount + 1)]
    surplus, counts = total - most - (amount - 1), [1] * (amount - 1)
    while surplus > 0:
        movable = [i for i in range(amount - 1) if counts[i] < most]
        mass, budget = sum([weights[i] for i in movable]), surplus
        for i in movable:
            extra = min(most - counts[i], max(1, budget * weights[i] // mass), surplus)
            counts[i] = counts[i] + extra
            surplus = surplus - extra
    return np.array([most] + counts)


def uneven(key, amount, total, bound, slope):
    if amount == 2:
        one = jax.random.randint(key, (), max(1, total - bound), min(bound, total - 1) + 1)
        return jnp.stack([one, total - one])
    lengths = jnp.asarray(profile(amount, total, bound, slope), jnp.int32)
    twos = (amount - 1) // 2
    source_of, taker = lengths[1:1 + 2 * twos:2], lengths[2:2 + 2 * twos:2]
    room = jnp.minimum(source_of - 1, bound - taker)
    passed = jax.random.randint(jax.random.fold_in(key, 1), (twos,), 0, 1 << 20) % (room + 1)
    lengths = lengths.at[1:1 + 2 * twos:2].set(source_of - passed).at[2:2 + 2 * twos:2].set(taker + passed)
    return lengths[jax.random.permutation(jax.random.fold_in(key, 2), amount)]


def bell_draw(key, extent, deviation, limit, split=(), kind=jnp.bfloat16):
    loudness = block_levels(key, extent, split, -0.22, 0.18) if split else 1.0
    values = jax.random.normal(key, extent, jnp.float32) * deviation * loudness
    return jnp.minimum(jnp.maximum(values, -limit), limit).astype(kind)


def setup_inputs(seed: int = 0) -> dict:
    keys = jax.random.split(jax.random.key(seed), 13)
    tokens = bell_draw(keys[0], (TOKENS, D), 1.0, 6.0, ((0, 64), (1, 2)))
    segment_ids = jnp.searchsorted(jnp.cumsum(uneven(keys[1], SEQS, TOKENS, MAXLEN, 2)), jnp.arange(TOKENS), side="right").astype(jnp.int32)
    valid_mask = place_ends((jax.random.randint(keys[2], (TOKENS,), 0, 8) < 7).astype(jnp.int32), jax.random.fold_in(keys[2], 1), 0, 1)
    norm1_gain = jnp.clip(1.0 + 0.18 * jax.random.normal(keys[3], (D,), jnp.float32), 0.099609375, 1.8984375).astype(jnp.bfloat16)
    in_weight = bell_draw(keys[4], (3, D, D), D ** -0.5, 0.1875, ((1, 64), (2, 2)))
    conv_weight = bell_draw(keys[5], (KW, D), KW ** -0.5, 3.5)
    out_weight = bell_draw(keys[6], (D, D), D ** -0.5, 0.1875, ((0, 2), (1, 64)))
    norm2_gain = jnp.clip(1.0 + 0.18 * jax.random.normal(keys[7], (D,), jnp.float32), 0.099609375, 1.8984375).astype(jnp.bfloat16)
    gate_weight = bell_draw(keys[8], (D, FF), D ** -0.5, 0.1875, ((0, 64), (1, 2)))
    up_weight = bell_draw(keys[9], (D, FF), D ** -0.5, 0.1875, ((0, 64), (1, 2)))
    down_weight = bell_draw(keys[10], (FF, D), FF ** -0.5, 0.09375, ((0, 2), (1, 64)))
    out_cotangent = bell_draw(keys[11], (TOKENS, D), 1.0, 6.0, ((0, 64), (1, 2)))
    return dict(tokens=tokens, segment_ids=segment_ids, valid_mask=valid_mask, norm1_gain=norm1_gain, in_weight=in_weight, conv_weight=conv_weight, out_weight=out_weight, norm2_gain=norm2_gain, gate_weight=gate_weight, up_weight=up_weight, down_weight=down_weight, out_cotangent=out_cotangent)


EPSILON = 1e-05

@jax.custom_vjp
def low(v):
    return lax.optimization_barrier(v.astype(jnp.bfloat16)).astype(jnp.float32)

@jax.custom_vjp
def low_back(v):
    return v

def low_keep(v):
    return (low(v), None)

def low_pass(kept, grad):
    return (grad,)

def back_keep(v):
    return (v, None)

def back_low(kept, grad):
    return (low(grad),)
low.defvjp(low_keep, low_pass)
low_back.defvjp(back_keep, back_low)

def matmul_high(left_side, right_side):
    return jnp.dot(left_side, right_side, precision=lax.Precision.HIGHEST, preferred_element_type=jnp.float32)

def rms_scale(values):
    return lax.rsqrt(lax.optimization_barrier(jnp.mean(values * values, axis=1, keepdims=True)) + EPSILON)

def tap_masks(seg_ext, valid_ext, margin, row_count):
    keep_list = []
    for offset in range(margin + 1):
        current_seg = seg_ext[margin:margin + row_count]
        earlier_seg = seg_ext[margin - offset:margin - offset + row_count]
        same_seg = (current_seg == earlier_seg).astype(jnp.int32)
        live_pair = valid_ext[margin:margin + row_count] * valid_ext[margin - offset:margin - offset + row_count] * same_seg
        keep_list.append(live_pair.astype(jnp.float32))
    return keep_list

def block_forward(keep_list, ext_tokens, gain_one, in_w, conv_w, out_w, gain_two, gate_w, up_w, down_w):
    margin = len(keep_list) - 1
    row_count = ext_tokens.shape[0] - margin
    normed_one = low(ext_tokens * rms_scale(ext_tokens) * gain_one)
    b_part = low_back(matmul_high(normed_one, in_w[0]))
    c_part = low_back(matmul_high(normed_one, in_w[1]))
    v_part = low_back(matmul_high(normed_one, in_w[2]))
    mixed = low(b_part * v_part)
    conv_sum = jnp.zeros((row_count, mixed.shape[1]), jnp.float32)
    for offset in range(margin + 1):
        conv_sum = conv_sum + conv_w[offset] * mixed[margin - offset:margin - offset + row_count] * keep_list[offset][:, None]
    gated_val = low(c_part[margin:] * conv_sum)
    residual = ext_tokens[margin:] + low_back(matmul_high(gated_val, out_w))
    normed_two = low(residual * rms_scale(residual) * gain_two)
    gate_val = low_back(matmul_high(normed_two, gate_w))
    up_val = low_back(matmul_high(normed_two, up_w))
    hidden = low(jax.nn.silu(gate_val) * up_val)
    return residual + matmul_high(hidden, down_w)

def reference(tokens, segment_ids, valid_mask, norm1_gain, in_weight, conv_weight, out_weight, norm2_gain, gate_weight, up_weight, down_weight, out_cotangent):
    margin = KW - 1
    block_len = math.gcd(TOKENS, 4096)
    block_count = TOKENS // block_len
    tok_pad = jnp.concatenate([jnp.zeros((margin, D), jnp.float32), tokens.astype(jnp.float32)], axis=0)
    seg_pad = jnp.concatenate([jnp.full((margin,), -1, jnp.int32), segment_ids.astype(jnp.int32)])
    valid_pad = jnp.concatenate([jnp.zeros((margin,), jnp.int32), valid_mask.astype(jnp.int32)])
    cotangent = out_cotangent.astype(jnp.float32)
    weights = tuple((weight_arg.astype(jnp.float32) for weight_arg in (norm1_gain, in_weight, conv_weight, out_weight, norm2_gain, gate_weight, up_weight, down_weight)))

    def one_block(grad_total, block_index):
        row_start = block_index * block_len
        ext_tokens = lax.dynamic_slice_in_dim(tok_pad, row_start, block_len + margin, 0)
        seg_ext = lax.dynamic_slice_in_dim(seg_pad, row_start, block_len + margin, 0)
        valid_ext = lax.dynamic_slice_in_dim(valid_pad, row_start, block_len + margin, 0)
        grad_block = lax.dynamic_slice_in_dim(cotangent, row_start, block_len, 0)
        keep_list = tap_masks(seg_ext, valid_ext, margin, block_len)

        def forward_fn(*inputs):
            return block_forward(keep_list, *inputs)
        result, pullback = jax.vjp(forward_fn, ext_tokens, *weights)
        block_grads = pullback(grad_block)
        grad_total = tuple((running + addend for running, addend in zip(grad_total, block_grads[1:])))
        return (grad_total, (result, block_grads[0]))
    zero_grads = tuple((jnp.zeros_like(weight_arg) for weight_arg in weights))
    grad_sums, (results, ext_grads) = lax.scan(one_block, zero_grads, jnp.arange(block_count, dtype=jnp.int32))
    mixed_out = results.reshape(TOKENS, D).astype(jnp.bfloat16)
    core_grads = ext_grads[:, margin:]
    core_grads = core_grads.at[:-1, block_len - margin:].add(ext_grads[1:, :margin])
    tokens_grad = core_grads.reshape(TOKENS, D)
    return (mixed_out, tokens_grad, grad_sums[0], grad_sums[1], grad_sums[2], grad_sums[3], grad_sums[4], grad_sums[5], grad_sums[6], grad_sums[7])
```

```python
import jax
import jax.numpy as jnp
from jax import lax
from jax.experimental import pallas as pl
from jax.experimental.pallas import tpu as pltpu
from jax.sharding import PartitionSpec as P

D = 1024
EPS = 1e-05
R = 4
BF = jnp.bfloat16
F32 = jnp.float32
TOK = 128
GT = 512
HALF = 512
CH = 128
HID = 576
HP = 640
WIDTHS = (512, 2 * HP, HP)
NCOPY = 230


def nn(a, b):
    return lax.dot_general(a, b, (((1,), (0,)), ((), ())), preferred_element_type=F32)


def nt(a, b):
    return lax.dot_general(a, b, (((1,), (1,)), ((), ())), preferred_element_type=F32)


def tn(a, b):
    return lax.dot_general(a, b, (((0,), (0,)), ((), ())), preferred_element_type=F32)


def add_into(dst, *others):
    total = dst[...].astype(F32)
    for other in others:
        total = total + other[...].astype(F32)
    dst[...] = total.astype(dst.dtype)


class Wire:
    def __init__(self, send_sems, recv_sems):
        self.send_sems, self.recv_sems, self.started = send_sems, recv_sems, []

    def send(self, src, dst, device):
        k = len(self.started)
        copy = pltpu.make_async_remote_copy(
            src_ref=src,
            dst_ref=dst,
            send_sem=self.send_sems.at[k],
            recv_sem=self.recv_sems.at[k],
            device_id=device,
            device_id_type=pl.DeviceIdType.MESH,
        )
        copy.start()
        self.started.append(copy)
        return copy

    def finish(self):
        for copy in self.started:
            copy.wait_send()


def ring_ag(wire, i, plus, minus, blk):
    prev, nxt = (i + R - 1) % R, (i + 1) % R
    c1 = wire.send(blk(i, None), blk(i, None), plus)
    c2 = wire.send(blk(i, None), blk(i, None), minus)
    yield
    c1.wait_recv()
    c3 = wire.send(blk(prev, 0), blk(prev, 0), plus)
    c2.wait_recv()
    c4 = wire.send(blk(nxt, 1), blk(nxt, 1), minus)
    yield
    c3.wait_recv()
    c4.wait_recv()
    yield


def ring_rs(wire, i, plus, minus, blk, recv):
    prev, nxt, far = (i + R - 1) % R, (i + 1) % R, (i + 2) % R
    c1 = wire.send(blk(far, 0), recv[0], plus)
    c2 = wire.send(blk(far, 1), recv[1], minus)
    c3 = wire.send(blk(nxt, 1), recv[2], plus)
    c4 = wire.send(blk(prev, 0), recv[3], minus)
    yield
    c1.wait_recv()
    add_into(blk(nxt, 0), recv[0])
    c5 = wire.send(blk(nxt, 0), recv[4], plus)
    c2.wait_recv()
    add_into(blk(prev, 1), recv[1])
    c6 = wire.send(blk(prev, 1), recv[5], minus)
    yield
    for c in (c3, c4, c5, c6):
        c.wait_recv()
    yield


def together(*gens):
    for _ in zip(*gens):
        yield


def kernel(
    tok_ref,
    dy_ref,
    code_ref,
    vec_ref,
    pack0,
    pack1,
    pack2,
    mix_out,
    tg_out,
    small_out,
    g0_out,
    g1_out,
    g2_out,
    w0,
    w1,
    w2,
    g0,
    g1,
    g2,
    ra0,
    ra1,
    ra2,
    rb0,
    rb1,
    rb2,
    oa0,
    oa1,
    oa2,
    codes,
    n1,
    dyf,
    n2,
    dhb,
    zpart,
    zrc,
    zp,
    zr,
    stat_s,
    stat_r,
    hat1,
    hat2,
    h2s,
    dh2s,
    bcv,
    dbcv,
    zc,
    gat,
    mx,
    cd,
    q1,
    q2,
    halo_s,
    halo_r,
    uu,
    dab,
    red,
    send_sems,
    recv_sems,
):
    dp = lax.axis_index("dp")
    core = lax.axis_index("tensor")
    y, x, z = dp // 16, (dp // 4) % 4, dp % 4
    group = dp // 4

    def dev(yy, xx, zz):
        return (yy * 16 + xx * 4 + zz, core)

    def up(v, k=1):
        return (v + k) % R

    peer = (dp, 1 - core)
    xs = [None] + [dev(y, up(x, k), z) for k in (1, 2, 3)]
    ys = [None] + [dev(up(y, k), x, z) for k in (1, 2, 3)]
    zs = [None] + [dev(y, x, up(z, k)) for k in (1, 2, 3)]
    after = ((dp + 4) % 64, core)
    before = ((dp + 60) % 64, core)

    barrier = pltpu.get_barrier_semaphore()
    others = [peer, after, before] + xs[1:] + ys[1:] + zs[1:]
    for other in others:
        pl.semaphore_signal(barrier, inc=1, device_id=other, device_id_type=pl.DeviceIdType.MESH)
    pl.semaphore_wait(barrier, len(others))

    wire = Wire(send_sems, recv_sems)
    packs, ws, gs = (pack0, pack1, pack2), (w0, w1, w2), (g0, g1, g2)
    ras, rbs, oas = (ra0, ra1, ra2), (rb0, rb1, rb2), (oa0, oa1, oa2)
    my_cols = pl.ds(pl.multiple_of(core * HALF, HALF), HALF)
    peer_cols = pl.ds(pl.multiple_of((1 - core) * HALF, HALF), HALF)

    def rows_of(j, count=TOK):
        return pl.ds(pl.multiple_of(j * count, count), count)

    def scatter_weights(c):
        mine = pl.ds(pl.multiple_of(z * 16, 16), 16)
        slab = ws[c].at[y, x, mine, :]
        copies = [wire.send(packs[c].at[up(z, k)], slab, zs[k]) for k in (1, 2, 3)]
        ws[c][y, x, mine, :] = packs[c][z]
        return copies

    def ag_plane(c):
        w = ws[c]

        def part(base, h):
            return pl.ds(base, 32) if h is None else pl.ds(base + 16 * h, 16)

        yield from together(
            ring_ag(wire, x, xs[1], xs[3], lambda j, h: w.at[y, j, part(0, h), :]),
            ring_ag(wire, y, ys[1], ys[3], lambda j, h: w.at[j, x, part(32, h), :]),
        )
        yield from together(
            ring_ag(wire, y, ys[1], ys[3], lambda j, h: w.at[j, :, part(0, h), :]),
            ring_ag(wire, x, xs[1], xs[3], lambda j, h: w.at[:, j, part(32, h), :]),
        )

    def rs_plane(c):
        g, ra, rb = gs[c], ras[c], rbs[c]

        def part(base, h):
            return pl.ds(base + 16 * h, 16)

        yield from together(
            ring_rs(wire, y, ys[1], ys[3], lambda j, h: g.at[j, :, part(0, h), :], [ra.at[0, k] for k in range(6)]),
            ring_rs(wire, x, xs[1], xs[3], lambda j, h: g.at[:, j, part(32, h), :], [ra.at[1, k] for k in range(6)]),
        )
        for h, (u, v) in ((0, (3, 4)), (1, (2, 5))):
            add_into(g.at[y, :, part(0, h), :], ra.at[0, u], ra.at[0, v])
            add_into(g.at[:, x, part(32, h), :], ra.at[1, u], ra.at[1, v])
        yield from together(
            ring_rs(wire, x, xs[1], xs[3], lambda j, h: g.at[y, j, part(0, h), :], [rb.at[0, k] for k in range(6)]),
            ring_rs(wire, y, ys[1], ys[3], lambda j, h: g.at[j, x, part(32, h), :], [rb.at[1, k] for k in range(6)]),
        )
        for h, (u, v) in ((0, (3, 4)), (1, (2, 5))):
            add_into(g.at[y, x, part(0, h), :], rb.at[0, u], rb.at[0, v])
            add_into(g.at[y, x, part(32, h), :], rb.at[1, u], rb.at[1, v])
        yield

    def gather_grads(c):
        def rows(j):
            return gs[c].at[y, x, pl.ds(pl.multiple_of(j * 16, 16), 16), :]

        copies = [wire.send(rows(up(z, k)), oas[c].at[z], zs[k]) for k in (1, 2, 3)]
        oas[c][z] = rows(z)[...]
        return copies

    def ag_group(n):
        def blk(j, h):
            base, count = (0, TOK) if h is None else (h * (TOK // 2), TOK // 2)
            return n.at[pl.ds(pl.multiple_of(j * TOK + base, TOK // 2), count), my_cols]

        def both(j, h, device):
            return wire.send(blk(j, h), blk(j, h), device)

        prev, nxt, far = up(z, 3), up(z), up(z, 2)
        c1 = both(z, None, zs[1])
        c2 = both(z, None, zs[3])
        got = [both(z, None, peer)]
        yield
        c1.wait_recv()
        c3 = both(prev, 0, zs[1])
        got.append(both(prev, None, peer))
        c2.wait_recv()
        c4 = both(nxt, 1, zs[3])
        got.append(both(nxt, None, peer))
        yield
        c3.wait_recv()
        got.append(both(far, 0, peer))
        c4.wait_recv()
        got.append(both(far, 1, peer))
        yield
        for c in got:
            c.wait_recv()
        yield

    def rs_group(k):
        part, rc, p = zpart.at[k], zrc.at[k], zp.at[k]
        c = wire.send(part.at[:, peer_cols], rc, peer)
        yield
        c.wait_recv()
        p[...] = (part[:, my_cols].astype(F32) + rc[...].astype(F32)).astype(BF)

        def blk(j, h):
            return p.at[pl.ds(pl.multiple_of(j * TOK + h * (TOK // 2), TOK // 2), TOK // 2), :]

        yield from ring_rs(wire, z, zs[1], zs[3], blk, [zr.at[k, i] for i in range(6)])

    def rs_result(k):
        def half(h, u, v):
            own = zp[k, pl.ds(pl.multiple_of(z * TOK + h * (TOK // 2), TOK // 2), TOK // 2), :]
            return own.astype(F32) + zr[k, u].astype(F32) + zr[k, v].astype(F32)

        return jnp.concatenate([half(0, 3, 4), half(1, 2, 5)], axis=0)

    def chip_sum(k, values):
        stat_s[k] = jnp.broadcast_to(jnp.sum(values, axis=1, keepdims=True), (TOK, CH))
        c = wire.send(stat_s.at[k], stat_r.at[k], peer)
        c.wait_recv()
        return (stat_s[k] + stat_r[k])[:, :1]

    dealt0 = scatter_weights(0)
    tok = tok_ref[...].astype(F32)
    r1 = lax.rsqrt(chip_sum(0, tok * tok) * (1.0 / D) + EPS)
    gain1 = vec_ref[pl.ds(0, 1), my_cols]
    gain2 = vec_ref[pl.ds(1, 1), my_cols]
    hat1[...] = tok * r1
    n1[rows_of(z), my_cols] = (hat1[...] * gain1).astype(BF)
    ag_n1 = ag_group(n1)
    next(ag_n1)
    codes[z] = code_ref[...]
    code_copies = [wire.send(code_ref, codes.at[z], zs[k]) for k in (1, 2, 3)]
    for c in dealt0:
        c.wait_recv()
    ag0 = ag_plane(0)
    next(ag0)
    dealt1 = scatter_weights(1)
    dealt2 = scatter_weights(2)
    next(ag_n1)
    next(ag0)
    next(ag0)
    for c in dealt1:
        c.wait_recv()
    ag1 = ag_plane(1)
    next(ag0)
    next(ag1)
    next(ag_n1)
    dyf[rows_of(z), my_cols] = dy_ref[...]
    ag_dy = ag_group(dyf)
    next(ag_dy)
    next(ag0)
    for c in dealt2:
        c.wait_recv()
    ag2 = ag_plane(2)
    next(ag2)
    next(ag1)
    next(ag_n1)
    next(ag0)

    ch_cols = pl.ds(pl.multiple_of(core * HALF + z * CH, CH), CH)
    taps = [vec_ref[pl.ds(2 + k, 1), ch_cols] for k in range(3)]
    bcv[...] = nn(n1[...], w0[...].reshape(D, 512)[:, : 3 * CH])
    mx[pl.ds(8, GT), :] = (bcv[:, 0:CH] * bcv[:, 2 * CH : 3 * CH]).astype(BF).astype(F32)
    for c in code_copies:
        c.wait_recv()
    cd[pl.ds(8, GT), :] = codes[...].reshape(GT, CH).astype(F32)
    halo_s[0, 0] = mx[pl.ds(GT, 8), :]
    halo_s[0, 1] = cd[pl.ds(GT, 8), :]
    c = wire.send(halo_s.at[0], halo_r.at[0], after)
    next(ag1)
    next(ag2)
    next(ag_dy)
    c.wait_recv()
    first = group == 0
    mx[pl.ds(0, 8), :] = halo_r[0, 0]
    cd[pl.ds(0, 8), :] = jnp.where(first, -1.0, halo_r[0, 1])
    code = cd[pl.ds(8, GT), :]
    live = code >= 16.0

    def keep(k):
        return jnp.where(live & (code == cd[pl.ds(8 - k, GT), :]), 1.0, 0.0)

    zc[...] = (
        taps[0] * mx[pl.ds(8, GT), :] * keep(0)
        + taps[1] * mx[pl.ds(7, GT), :] * keep(1)
        + taps[2] * mx[pl.ds(6, GT), :] * keep(2)
    )
    gat[...] = (bcv[:, CH : 2 * CH] * zc[...]).astype(BF)

    @pl.loop(0, 2)
    def _(i):
        rows = rows_of(i, 256)
        zpart[0, rows, :] = nt(gat[rows, :], w0[...].reshape(D, 512)[:, 3 * CH :]).astype(BF)

    rs_y = rs_group(0)
    next(rs_y)
    next(ag1)
    next(ag2)
    next(rs_y)
    next(ag_dy)
    next(rs_y)
    next(ag1)
    next(ag2)
    next(rs_y)
    h2s[...] = tok_ref[...].astype(F32) + rs_result(0)
    h2 = h2s[...]
    r2 = lax.rsqrt(chip_sum(1, h2 * h2) * (1.0 / D) + EPS)
    hat2[...] = h2 * r2
    n2[rows_of(z), my_cols] = (hat2[...] * gain2).astype(BF)
    ag_n2 = ag_group(n2)
    next(ag_n2)
    next(ag2)
    next(ag_n2)
    next(ag1)
    next(ag_dy)
    next(ag_n2)
    next(ag2)
    next(ag_n2)

    @pl.loop(0, 2)
    def _(i):
        rows = rows_of(i, 256)
        ab = nn(n2[rows, :], w1[...].reshape(D, 2 * HP))
        a, b = ab[:, :HP], ab[:, HP:]
        s = jax.nn.sigmoid(a)
        silu = a * s
        uu[rows, :] = (silu * b).astype(BF)
        du = nn(dyf[rows, :], w2[...].reshape(D, HP))
        dab[rows, 0:HP] = (du * b * s * (1.0 + a * (1.0 - s))).astype(BF)
        dab[rows, HP : 2 * HP] = (du * silu).astype(BF)

    @pl.loop(0, 2)
    def _(i):
        rows = rows_of(i, 256)
        zpart[1, rows, :] = nt(dab[rows, :], w1[...].reshape(D, 2 * HP)).astype(BF)

    rs_n2 = rs_group(1)
    next(rs_n2)

    @pl.loop(0, 4)
    def _(i):
        cols = rows_of(i, 256)
        g1[i] = tn(n2[:, cols], dab[...]).astype(BF).reshape(4, 64, 2 * HP)

    next(rs_n2)
    rs1 = rs_plane(1)
    next(rs1)
    next(rs_n2)

    @pl.loop(0, 4)
    def _(i):
        cols = rows_of(i, 256)
        g2[i] = tn(dyf[:, cols], uu[...]).astype(BF).reshape(4, 64, HP)

    next(rs_n2)
    rs2 = rs_plane(2)
    dn2 = rs_result(1)
    small_out[...] = jnp.zeros((8, D), F32)
    small_out[pl.ds(1, 1), my_cols] = jnp.sum(dn2 * hat2[...], axis=0, keepdims=True)
    e2 = dn2 * gain2
    m2 = chip_sum(2, e2 * hat2[...]) * (1.0 / D)
    dh2s[...] = dy_ref[...].astype(F32) + r2 * (e2 - hat2[...] * m2)
    dhb[rows_of(z), my_cols] = dh2s[...].astype(BF)
    ag_dh = ag_group(dhb)
    next(ag_dh)
    next(rs2)
    next(rs1)
    next(ag_dh)

    @pl.loop(0, 2)
    def _(i):
        rows = rows_of(i, 256)
        zpart[2, rows, :] = nt(uu[rows, :], w2[...].reshape(D, HP)).astype(BF)

    rs_u = rs_group(2)
    next(ag_dh)
    next(rs_u)
    next(ag_dh)

    dg = nn(dhb[...], w0[...].reshape(D, 512)[:, 3 * CH :])
    dbcv[:, CH : 2 * CH] = (dg * zc[...]).astype(BF)
    dz = dg * bcv[:, CH : 2 * CH]
    code = cd[pl.ds(8, GT), :]
    live = code >= 16.0
    q0 = dz * keep(0)
    q1[pl.ds(0, GT), :] = dz * keep(1)
    q2[pl.ds(0, GT), :] = dz * keep(2)
    halo_s[1, 0] = q1[pl.ds(0, 8), :]
    halo_s[1, 1] = q2[pl.ds(0, 8), :]
    c = wire.send(halo_s.at[1], halo_r.at[1], before)
    small_out[pl.ds(2, 1), ch_cols] = jnp.sum(q0 * mx[pl.ds(8, GT), :], axis=0, keepdims=True)
    small_out[pl.ds(3, 1), ch_cols] = jnp.sum(q1[pl.ds(0, GT), :] * mx[pl.ds(7, GT), :], axis=0, keepdims=True)
    small_out[pl.ds(4, 1), ch_cols] = jnp.sum(q2[pl.ds(0, GT), :] * mx[pl.ds(6, GT), :], axis=0, keepdims=True)
    c.wait_recv()
    last = group == 15
    q1[pl.ds(GT, 8), :] = jnp.where(last, 0.0, halo_r[1, 0])
    q2[pl.ds(GT, 8), :] = jnp.where(last, 0.0, halo_r[1, 1])
    dm = taps[0] * q0 + taps[1] * q1[pl.ds(1, GT), :] + taps[2] * q2[pl.ds(2, GT), :]
    dbcv[:, 0:CH] = (dm * bcv[:, 2 * CH : 3 * CH]).astype(BF)
    dbcv[:, 2 * CH : 3 * CH] = (dm * bcv[:, 0:CH]).astype(BF)

    @pl.loop(0, 2)
    def _(i):
        rows = rows_of(i, 256)
        zpart[3, rows, :] = nt(dbcv[rows, :], w0[...].reshape(D, 512)[:, : 3 * CH]).astype(BF)

    rs_n1 = rs_group(3)
    next(rs_n1)
    next(rs1)
    next(rs2)

    @pl.loop(0, 4)
    def _(i):
        cols = rows_of(i, 256)
        g0[i, :, :, 0 : 3 * CH] = tn(n1[:, cols], dbcv[...]).astype(BF).reshape(4, 64, 3 * CH)
        g0[i, :, :, 3 * CH : 4 * CH] = tn(dhb[:, cols], gat[...]).astype(BF).reshape(4, 64, CH)

    rs0 = rs_plane(0)
    next(rs0)
    next(rs_n1)
    next(rs_u)
    next(rs_n1)
    next(rs0)
    next(rs2)
    next(rs_u)
    next(rs_n1)

    dn1 = rs_result(3)
    small_out[pl.ds(0, 1), my_cols] = jnp.sum(dn1 * hat1[...], axis=0, keepdims=True)
    e1 = dn1 * gain1
    m1 = chip_sum(3, e1 * hat1[...]) * (1.0 / D)
    tg_out[...] = dh2s[...] + r1 * (e1 - hat1[...] * m1)

    def all_sum(k, i, peers):
        red[k, i] = small_out[...]
        copies = [wire.send(red.at[k, i], red.at[k, i], peers[j]) for j in (1, 2, 3)]
        yield
        for c in copies:
            c.wait_recv()
        small_out[...] = (red[k, 0] + red[k, 1]) + (red[k, 2] + red[k, 3])
        yield

    sum_x = all_sum(0, x, xs)
    next(sum_x)
    next(rs1)
    next(rs0)
    next(sum_x)
    sum_y = all_sum(1, y, ys)
    next(sum_y)
    next(rs2)
    next(rs_u)
    mix_out[...] = (h2s[...] + rs_result(2)).astype(BF)
    next(rs0)
    next(sum_y)
    sum_z = all_sum(2, z, zs)
    next(sum_z)
    next(rs1)
    next(rs1)
    next(rs1)
    back1 = gather_grads(1)
    next(rs2)
    next(rs2)
    next(rs2)
    back2 = gather_grads(2)
    next(sum_z)
    red[3, core] = small_out[...]
    c = wire.send(red.at[3, core], red.at[3, core], peer)
    next(rs0)
    next(rs0)
    next(rs0)
    back0 = gather_grads(0)
    c.wait_recv()
    small_out[...] = red[3, 0] + red[3, 1]
    for copies, oa, out in ((back1, oa1, g1_out), (back2, oa2, g2_out), (back0, oa0, g0_out)):
        for c in copies:
            c.wait_recv()
        out[...] = oa[...].astype(F32)
    for gen in (ag0, ag1, ag2, ag_n1, ag_dy, ag_n2, ag_dh, rs0, rs1, rs2, rs_y, rs_n2, rs_u, rs_n1):
        assert next(gen, 0) == 0
    wire.finish()


def block(tokens, dy, code, vec, pack0, pack1, pack2):
    vmem = pl.BlockSpec(memory_space=pltpu.VMEM)
    plane = [pltpu.VMEM((4, 4, 64, w), BF) for w in WIDTHS]
    scratch = (
        plane
        + [pltpu.VMEM((4, 4, 64, w), BF) for w in WIDTHS]
        + [pltpu.VMEM((2, 6, 4, 16, w), BF) for w in WIDTHS]
        + [pltpu.VMEM((2, 6, 16, w), BF) for w in WIDTHS]
        + [pltpu.VMEM((4, 16, w), BF) for w in WIDTHS]
        + [
            pltpu.VMEM((4, TOK, CH), BF),
            pltpu.VMEM((GT, D), BF),
            pltpu.VMEM((GT, D), BF),
            pltpu.VMEM((GT, D), BF),
            pltpu.VMEM((GT, D), BF),
            pltpu.VMEM((4, GT, D), BF),
            pltpu.VMEM((4, GT, HALF), BF),
            pltpu.VMEM((4, GT, HALF), BF),
            pltpu.VMEM((4, 6, TOK // 2, HALF), BF),
            pltpu.VMEM((4, TOK, CH), F32),
            pltpu.VMEM((4, TOK, CH), F32),
            pltpu.VMEM((TOK, HALF), F32),
            pltpu.VMEM((TOK, HALF), F32),
            pltpu.VMEM((TOK, HALF), F32),
            pltpu.VMEM((TOK, HALF), F32),
            pltpu.VMEM((GT, 3 * CH), F32),
            pltpu.VMEM((GT, 3 * CH), BF),
            pltpu.VMEM((GT, CH), F32),
            pltpu.VMEM((GT, CH), BF),
            pltpu.VMEM((GT + 8, CH), F32),
            pltpu.VMEM((GT + 8, CH), F32),
            pltpu.VMEM((GT + 8, CH), F32),
            pltpu.VMEM((GT + 8, CH), F32),
            pltpu.VMEM((2, 2, 8, CH), F32),
            pltpu.VMEM((2, 2, 8, CH), F32),
            pltpu.VMEM((GT, HP), BF),
            pltpu.VMEM((GT, 2 * HP), BF),
            pltpu.VMEM((4, 4, 8, D), F32),
            pltpu.SemaphoreType.DMA((NCOPY,)),
            pltpu.SemaphoreType.DMA((NCOPY,)),
        ]
    )
    return pl.pallas_call(
        kernel,
        out_shape=[
            jax.ShapeDtypeStruct((TOK, HALF), BF),
            jax.ShapeDtypeStruct((TOK, HALF), F32),
            jax.ShapeDtypeStruct((8, D), F32),
        ]
        + [jax.ShapeDtypeStruct((4, 16, w), F32) for w in WIDTHS],
        in_specs=[vmem] * 7,
        out_specs=[vmem] * 6,
        scratch_shapes=scratch,
        compiler_params=pltpu.CompilerParams(
            collective_id=0, has_side_effects=True, vmem_limit_bytes=58 * 1024 * 1024
        ),
    )(tokens, dy, code, vec, pack0, pack1, pack2)


def local(
    tokens,
    segment_ids,
    valid_mask,
    norm1_gain,
    in_weight,
    conv_weight,
    out_weight,
    norm2_gain,
    gate_weight,
    up_weight,
    down_weight,
    out_cotangent,
):
    code = (segment_ids + 16 * valid_mask).astype(BF)
    code = jnp.broadcast_to(code[:, None], (TOK, CH))
    vec = jnp.concatenate(
        [norm1_gain[None], norm2_gain[None], conv_weight, jnp.zeros((3, D), BF)], axis=0
    ).astype(F32)

    def wide(w):
        return jnp.pad(w.reshape(16, 4, HID).transpose(1, 0, 2), ((0, 0), (0, 0), (0, HP - HID)))

    ins = in_weight.reshape(3, 16, 4, CH).transpose(2, 1, 0, 3).reshape(4, 16, 3 * CH)
    outs = out_weight.reshape(4, CH, 16).transpose(0, 2, 1)
    pack0 = jnp.concatenate([ins, outs], axis=2)
    pack1 = jnp.concatenate([wide(gate_weight), wide(up_weight)], axis=2)
    pack2 = jnp.pad(down_weight.reshape(4, HID, 16).transpose(0, 2, 1), ((0, 0), (0, 0), (0, HP - HID)))
    mixed, tokens_grad, small, p0, p1, p2 = block(tokens, out_cotangent, code, vec, pack0, pack1, pack2)
    grad_in = p0[:, :, : 3 * CH].reshape(4, 16, 3, CH).transpose(2, 1, 0, 3).reshape(3, 16, HALF)
    grad_out = p0[:, :, 3 * CH :].transpose(0, 2, 1).reshape(HALF, 16)
    grad_gate = p1[:, :, :HID].transpose(1, 0, 2).reshape(16, 4 * HID)
    grad_up = p1[:, :, HP : HP + HID].transpose(1, 0, 2).reshape(16, 4 * HID)
    grad_down = p2[:, :, :HID].transpose(0, 2, 1).reshape(4 * HID, 16)
    return (mixed, tokens_grad, small[0], grad_in, small[2:5], grad_out, small[1], grad_gate, grad_up, grad_down)


def solution(mesh):
    placed = (
        P("dp", "tensor"),
        P("dp"),
        P("dp"),
        P(),
        P(None, "dp", "tensor"),
        P(),
        P("tensor", "dp"),
        P(),
        P("dp", "tensor"),
        P("dp", "tensor"),
        P("tensor", "dp"),
        P("dp", "tensor"),
    )
    return jax.shard_map(
        local,
        mesh=mesh,
        in_specs=placed,
        out_specs=(
            P("dp", "tensor"),
            P("dp", "tensor"),
            P(),
            P(None, "dp", "tensor"),
            P(),
            P("tensor", "dp"),
            P(),
            P("dp", "tensor"),
            P("dp", "tensor"),
            P("tensor", "dp"),
        ),
        check_vma=False,
    )
```

```python
import jax
import jax.numpy as jnp
from jax import lax
from jax.experimental import pallas as pl
from jax.experimental.pallas import tpu as pltpu
from jax.sharding import PartitionSpec as P

D = 1024
EPS = 1e-05
R = 4
BF = jnp.bfloat16
F32 = jnp.float32
TOK = 128
GT = 512
HALF = 512
CH = 128
HID = 576
HP = 640
WIDTHS = (512, 2 * HP, HP)
SENDS = 48
RECEIVES = 186


def nn(a, b):
    return lax.dot_general(a, b, (((1,), (0,)), ((), ())), preferred_element_type=F32)


def nt(a, b):
    return lax.dot_general(a, b, (((1,), (1,)), ((), ())), preferred_element_type=F32)


def tn(a, b):
    return lax.dot_general(a, b, (((0,), (0,)), ((), ())), preferred_element_type=F32)


def add_into(dst, *others):
    total = dst[...].astype(F32)
    for other in others:
        total = total + other[...].astype(F32)
    dst[...] = total.astype(dst.dtype)


class Event:
    def __init__(self):
        self.time = float("inf")


class Copy(Event):
    def __init__(self, copy, time, end):
        self.copy, self.time, self.end, self.waited = copy, time, end, False


class Group(Event):
    def __init__(self, total):
        self.total, self.sem, self.time, self.waited = total, None, 0.0, False


class Room:
    def __init__(self, schedule, link, slack):
        self.schedule, self.link, self.slack = schedule, link, slack

    @property
    def time(self):
        return self.schedule.free.get(self.link, 0.0) - self.slack


class Schedule:
    RATE = 46.8e3
    CORE_RATE = 700e3
    LATENCY = 1.65
    FAR_LATENCY = 2.3
    CORE_LATENCY = 0.9
    ISSUE = 0.05

    def __init__(self, send_sems, recv_sems):
        self.send_sems, self.recv_sems = send_sems, recv_sems
        self.pool, self.received = [None] * SENDS, 0
        self.tasks, self.free, self.now = [], {}, 2.0

    def send(self, src, dst, device, *links, group=None):
        k = min(range(SENDS), key=lambda i: -1.0 if self.pool[i] is None else self.pool[i].end)
        if self.pool[k] is not None:
            self.pool[k].copy.wait_send()
            self.now = max(self.now, self.pool[k].end)
        sem = self.received if group is None or group.sem is None else group.sem
        if sem == self.received:
            self.received += 1
            assert sem < RECEIVES
        copy = pltpu.make_async_remote_copy(
            src_ref=src,
            dst_ref=dst,
            send_sem=self.send_sems.at[k],
            recv_sem=self.recv_sems.at[sem],
            device_id=device,
            device_id_type=pl.DeviceIdType.MESH,
        )
        copy.start()
        self.now += self.ISSUE
        size = jnp.dtype(src.dtype).itemsize
        for n in src.shape:
            size *= n
        end = self.now
        for link in links:
            begin = max(self.now, self.free.get(link, 0.0))
            self.free[link] = begin + size / (self.CORE_RATE if link == "c" else self.RATE)
            end = max(end, self.free[link])
        latency = self.CORE_LATENCY if "c" in links else self.LATENCY if len(links) == 1 else self.FAR_LATENCY
        self.pool[k] = Copy(copy, end + latency, end)
        if group is None:
            return self.pool[k]
        group.sem, group.time = sem, max(group.time, end + latency)
        group.copy = pltpu.make_async_remote_copy(
            src_ref=group.total,
            dst_ref=group.total,
            send_sem=self.send_sems.at[k],
            recv_sem=self.recv_sems.at[sem],
            device_id=device,
            device_id_type=pl.DeviceIdType.MESH,
        )
        return group

    def room(self, link, slack=0.8):
        return [Room(self, link, slack)]

    def work(self, us):
        self.now += us

    def done(self, event):
        event.time = self.now

    def add(self, rank, task):
        self.tasks.append([rank, task, ()])

    def run(self):
        while self.tasks:
            times = [max([0.0] + [e.time for e in t[2]]) for t in self.tasks]
            ready = [i for i, r in enumerate(times) if r <= self.now]
            if ready:
                i = min(ready, key=lambda i: (self.tasks[i][0], times[i]))
            else:
                i = min(range(len(times)), key=lambda i: (times[i], self.tasks[i][0]))
                self.now = times[i]
            task = self.tasks[i]
            for event in task[2]:
                if isinstance(event, (Copy, Group)) and not event.waited:
                    event.copy.wait_recv()
                    event.waited = True
                    self.now += 0.03
            try:
                task[2] = tuple(next(task[1]))
            except StopIteration:
                self.tasks.pop(i)
        for last in self.pool:
            if last is not None:
                last.copy.wait_send()


def ring_ag(s, axis, i, plus, minus, blk, two, issued=None):
    rest = Group(two)
    up, down = axis + "+", axis + "-"
    prev, nxt = (i + R - 1) % R, (i + 1) % R
    yield s.room(up)
    c1 = s.send(blk(i, 0), blk(i, 0), plus, up)
    yield s.room(down)
    c2 = s.send(blk(i, 1), blk(i, 1), minus, down)
    yield s.room(up)
    s.send(blk(i, 1), blk(i, 1), plus, up, group=rest)
    yield s.room(down)
    s.send(blk(i, 0), blk(i, 0), minus, down, group=rest)
    yield [c1]
    s.send(blk(prev, 0), blk(prev, 0), plus, up, group=rest)
    yield [c2]
    s.send(blk(nxt, 1), blk(nxt, 1), minus, down, group=rest)
    if issued is not None:
        s.done(issued)
    yield [rest]


def ring_rs(s, axis, i, plus, minus, blk, bufs, us):
    recv, rest = [bufs.at[k] for k in range(6)], Group(bufs.at[pl.ds(2, 4)])
    up, down = axis + "+", axis + "-"
    prev, nxt, far = (i + R - 1) % R, (i + 1) % R, (i + 2) % R
    yield s.room(up)
    c1 = s.send(blk(far, 0), recv[0], plus, up)
    yield s.room(down)
    c2 = s.send(blk(far, 1), recv[1], minus, down)
    yield s.room(up)
    s.send(blk(nxt, 1), recv[2], plus, up, group=rest)
    yield s.room(down)
    s.send(blk(prev, 0), recv[3], minus, down, group=rest)
    yield [c1]
    add_into(blk(nxt, 0), recv[0])
    s.work(us)
    s.send(blk(nxt, 0), recv[4], plus, up, group=rest)
    yield [c2]
    add_into(blk(prev, 1), recv[1])
    s.work(us)
    s.send(blk(prev, 1), recv[5], minus, down, group=rest)
    yield [rest]


def kernel(
    tok_ref,
    dy_ref,
    code_ref,
    vec_ref,
    pack0,
    pack1,
    pack2,
    mix_out,
    tg_out,
    small_out,
    g0_out,
    g1_out,
    g2_out,
    w0,
    w1,
    w2,
    g0,
    g1,
    g2,
    ra0,
    ra1,
    ra2,
    ra3,
    rb0,
    rb1,
    rb2,
    rb3,
    oa0,
    oa1,
    oa2,
    codes,
    tail_raw,
    tail_code,
    tail_s,
    tail_r,
    tail,
    n1,
    dyf,
    n2,
    dhb,
    zpart,
    zrc,
    zp,
    zr,
    zd,
    stat_s,
    stat_r,
    hat1,
    hat2,
    h2s,
    dh2s,
    bcv,
    dbcv,
    zc,
    gat,
    mx,
    cd,
    q0,
    q1,
    q2,
    halo_s,
    halo_r,
    uu,
    dab,
    red,
    send_sems,
    recv_sems,
):
    dp = lax.axis_index("dp")
    core = lax.axis_index("tensor")
    y, x, z = dp // 16, (dp // 4) % 4, dp % 4
    group = dp // 4

    def dev(yy, xx, zz):
        return (yy * 16 + xx * 4 + zz, core)

    def up(v, k=1):
        return (v + k) % R

    peer = (dp, 1 - core)
    xs = [None] + [dev(y, up(x, k), z) for k in (1, 2, 3)]
    ys = [None] + [dev(up(y, k), x, z) for k in (1, 2, 3)]
    zs = [None] + [dev(y, x, up(z, k)) for k in (1, 2, 3)]
    after = ((dp + 4) % 64, core)
    before = ((dp + 60) % 64, core)

    barrier = pltpu.get_barrier_semaphore()
    others = [peer, after, before] + xs[1:] + ys[1:] + zs[1:]
    for other in others:
        pl.semaphore_signal(barrier, inc=1, device_id=other, device_id_type=pl.DeviceIdType.MESH)
    pl.semaphore_wait(barrier, len(others))

    s = Schedule(send_sems, recv_sems)
    packs, ws, gs = (pack0, pack1, pack1, pack2), (w0, w1, w1, w2), (g0, g1, g1, g2)
    ras, rbs, oas = (ra0, ra1, ra2, ra3), (rb0, rb1, rb2, rb3), (oa0, oa1, oa1, oa2)
    outs = (g0_out, g1_out, g1_out, g2_out)
    lanes = (pl.ds(0, 512), pl.ds(0, HP), pl.ds(HP, HP), pl.ds(0, HP))
    my_cols = pl.ds(pl.multiple_of(core * HALF, HALF), HALF)
    peer_cols = pl.ds(pl.multiple_of((1 - core) * HALF, HALF), HALF)
    ch_cols = pl.ds(pl.multiple_of(core * HALF + z * CH, CH), CH)
    z_links = (None, ("z+",), ("z+", "z-"), ("z-",))
    links = {a: (None, (a + "+",), (a + "+", a + "-"), (a + "-",)) for a in "xyz"}

    def rows_of(j, count=TOK):
        return pl.ds(pl.multiple_of(j * count, count), count)

    def ag_plane(c, issued):
        w, ln = ws[c], lanes[c]

        def part(base, h):
            return pl.ds(base + 16 * h, 16)

        def side_a():
            yield from ring_ag(s, "x", x, xs[1], xs[3], lambda j, h: w.at[y, j, part(0, h), ln], w.at[y, x, :, ln])
            if c:
                yield [issued[c - 1][0]]
            yield from ring_ag(s, "y", y, ys[1], ys[3], lambda j, h: w.at[j, :, part(0, h), ln], w.at[y, :, :, ln], issued[c][0])

        def side_b():
            yield from ring_ag(s, "y", y, ys[1], ys[3], lambda j, h: w.at[j, x, part(32, h), ln], w.at[y, x, :, ln])
            if c:
                yield [issued[c - 1][1]]
            yield from ring_ag(s, "x", x, xs[1], xs[3], lambda j, h: w.at[:, j, part(32, h), ln], w.at[:, x, :, ln], issued[c][1])

        return side_a, side_b

    def rs_plane(c):
        g, ra, rb, ln, us = gs[c], ras[c], rbs[c], lanes[c], 0.12

        def part(base, h):
            return pl.ds(base + 16 * h, 16)

        def side_a():
            yield from ring_rs(
                s, "y", y, ys[1], ys[3], lambda j, h: g.at[j, :, part(0, h), ln], ra.at[0], us
            )
            for h, (u, v) in ((0, (3, 4)), (1, (2, 5))):
                add_into(g.at[y, :, part(0, h), ln], ra.at[0, u], ra.at[0, v])
                s.work(1.5 * us)
            yield from ring_rs(
                s, "x", x, xs[1], xs[3], lambda j, h: g.at[y, j, part(0, h), ln], rb.at[0], us / 3
            )
            for h, (u, v) in ((0, (3, 4)), (1, (2, 5))):
                add_into(g.at[y, x, part(0, h), ln], rb.at[0, u], rb.at[0, v])
                s.work(0.5 * us)

        def side_b():
            yield from ring_rs(
                s, "x", x, xs[1], xs[3], lambda j, h: g.at[:, j, part(32, h), ln], ra.at[1], us
            )
            for h, (u, v) in ((0, (3, 4)), (1, (2, 5))):
                add_into(g.at[:, x, part(32, h), ln], ra.at[1, u], ra.at[1, v])
                s.work(1.5 * us)
            yield from ring_rs(
                s, "y", y, ys[1], ys[3], lambda j, h: g.at[j, x, part(32, h), ln], rb.at[1], us / 3
            )
            for h, (u, v) in ((0, (3, 4)), (1, (2, 5))):
                add_into(g.at[y, x, part(32, h), ln], rb.at[1, u], rb.at[1, v])
                s.work(0.5 * us)

        return side_a, side_b

    prev, nxt, far = up(z, 3), up(z), up(z, 2)

    def ag_group(n, have, issued):
        def both(j, h, device, link, group=None):
            ref = n.at[half_rows(j, h), my_cols]
            return s.send(ref, ref, device, link, group=group)

        to_core = [Group(n.at[rows_of(j), my_cols]) for j in (z, prev, nxt, far)]

        def core_too(i, j, h):
            both(j, h, peer, "c", to_core[i])

        c1 = both(z, 0, zs[1], "z+")
        c2 = both(z, 1, zs[3], "z-")
        c3 = both(z, 1, zs[1], "z+")
        c4 = both(z, 0, zs[3], "z-")
        core_too(0, z, 0)
        core_too(0, z, 1)
        yield [to_core[0]]
        s.done(have[0])
        yield [c1]
        c5 = both(prev, 0, zs[1], "z+")
        core_too(1, prev, 0)
        yield [c2]
        c6 = both(nxt, 1, zs[3], "z-")
        s.done(issued)
        core_too(2, nxt, 1)
        yield [c3]
        core_too(1, prev, 1)
        yield [c4]
        core_too(2, nxt, 0)
        yield [to_core[1]]
        s.done(have[1])
        yield [to_core[2]]
        s.done(have[2])
        yield [c5]
        core_too(3, far, 0)
        yield [c6]
        core_too(3, far, 1)
        yield [to_core[3]]
        s.done(have[3])

    def half_rows(j, h):
        return pl.ds(pl.multiple_of(j * TOK + h * (TOK // 2), TOK // 2), TOK // 2)

    def share_core(k, j):
        return s.send(zpart.at[k, rows_of(j), peer_cols], zrc.at[k, rows_of(j)], peer, "c")

    def add_core(k, j):
        rows = rows_of(j)
        zp[k, rows] = (zpart[k, rows, my_cols].astype(F32) + zrc[k, rows].astype(F32)).astype(BF)
        s.work(0.15)

    def rs_group(k, part):
        def blk(j, h):
            return zp.at[k, half_rows(j, h)]

        recv = [zr.at[k, i] for i in range(6)]
        rest = Group(zr.at[k, pl.ds(2, 4)])
        order = (far, nxt, prev, z)
        copies = []
        for j in order:
            part(j)
            copies.append(share_core(k, j))
            yield []
        yield [copies[0]]
        add_core(k, far)
        c1 = s.send(blk(far, 0), recv[0], zs[1], "z+")
        c2 = s.send(blk(far, 1), recv[1], zs[3], "z-")
        yield [copies[1]]
        add_core(k, nxt)
        s.send(blk(nxt, 1), recv[2], zs[1], "z+", group=rest)
        yield [copies[2]]
        add_core(k, prev)
        s.send(blk(prev, 0), recv[3], zs[3], "z-", group=rest)
        yield [c1]
        add_into(blk(nxt, 0), recv[0])
        s.work(0.06)
        s.send(blk(nxt, 0), recv[4], zs[1], "z+", group=rest)
        yield [c2]
        add_into(blk(prev, 1), recv[1])
        s.work(0.06)
        s.send(blk(prev, 1), recv[5], zs[3], "z-", group=rest)
        yield [copies[3]]
        add_core(k, z)
        yield [rest]

    def rs_result(k):
        if k == 1:
            total = zp[k, rows_of(z)].astype(F32)
            for h in range(3):
                total = total + zd[h].astype(F32)
            return total

        def half(h, u, v):
            return zp[k, half_rows(z, h)].astype(F32) + zr[k, u].astype(F32) + zr[k, v].astype(F32)

        return jnp.concatenate([half(0, 3, 4), half(1, 2, 5)], axis=0)

    def chip_sum(k, values):
        stat_s[k] = jnp.broadcast_to(jnp.sum(values, axis=1, keepdims=True), (TOK, CH))
        return s.send(stat_s.at[k], stat_r.at[k], peer, "c")

    def chip_total(k):
        return (stat_s[k] + stat_r[k])[:, :1]

    def events(*dims):
        return [events(*dims[1:]) for _ in range(dims[0])] if dims else Event()

    dealt, full_w, issued = events(4), events(4, 2), events(4, 2)
    have_n1, have_n2, have_dy, have_dh = events(4), events(4), events(4), events(4)
    sent_n1, sent_n2, sent_dy, sent_dh = events(4)
    have_codes, have_halo, ffn, conv_back, sums = events(5)
    gain1 = vec_ref[pl.ds(0, 1), my_cols]
    gain2 = vec_ref[pl.ds(1, 1), my_cols]
    taps = [vec_ref[pl.ds(2 + k, 1), ch_cols] for k in range(3)]

    def deal(c):
        mine = pl.ds(pl.multiple_of(z * 16, 16), 16)
        slab = ws[c].at[y, x, mine, lanes[c]]
        group = Group(ws[c].at[y, x, pl.ds(0, 48), lanes[c]])
        for k in (1, 3, 2):
            s.send(packs[c].at[up(z, k), :, lanes[c]], slab, zs[k], *z_links[k], group=group)
        ws[c][y, x, mine, lanes[c]] = packs[c][z, :, lanes[c]]
        s.work(0.1)
        yield [group]
        s.done(dealt[c])

    def gather_side(c, h, side):
        yield [dealt[c]]
        yield from side()
        s.done(full_w[c][h])

    def first_norm():
        tok = tok_ref[...].astype(F32)
        copy = chip_sum(0, tok * tok)
        s.work(0.3)
        yield [copy]
        r1 = lax.rsqrt(chip_total(0) * (1.0 / D) + EPS)
        hat1[...] = tok_ref[...].astype(F32) * r1
        n1[rows_of(z), my_cols] = (hat1[...] * gain1).astype(BF)
        s.work(0.3)
        yield from ag_group(n1, have_n1, sent_n1)

    def halo():
        yield [
            s.send(tok_ref.at[pl.ds(TOK - 16, 16)], tail_raw, after, "x+"),
            s.send(code_ref, tail_code.at[z], after, "x+"),
        ]
        tok = tail_raw[...].astype(F32)
        tail_s[...] = jnp.broadcast_to(jnp.sum(tok * tok, axis=1, keepdims=True), (16, CH))
        yield [s.send(tail_s, tail_r, peer, "c")]
        scale = lax.rsqrt((tail_s[...] + tail_r[...])[:, :1] * (1.0 / D) + EPS)
        tail[z, :, my_cols] = (tail_raw[...].astype(F32) * scale * gain1).astype(BF)
        ref = tail.at[z, :, my_cols]
        group1, group2 = Group(tail.at[pl.ds(0, 3), :, my_cols]), Group(tail_code.at[pl.ds(0, 3)])
        for k in (1, 3, 2):
            s.send(ref, ref, zs[k], *z_links[k], group=group1)
            s.send(tail_code.at[z], tail_code.at[z], zs[k], *z_links[k], group=group2)
        s.work(0.1)
        yield [group1, group2]
        ref = tail.at[3, :, my_cols]
        yield [s.send(ref, ref, peer, "c")]
        n1[pl.ds(GT, 16), :] = tail[3]
        s.done(have_halo)

    def column(row):
        return jnp.transpose(jnp.broadcast_to(row, (CH, CH)))

    def share_codes():
        codes[z] = code_ref[...]
        group = Group(codes.at[pl.ds(0, 3)])
        for k in (1, 3, 2):
            s.send(code_ref, codes.at[z], zs[k], *z_links[k], group=group)
        yield [group]
        for j in range(4):
            cd[pl.ds(8 + j * TOK, TOK), :] = column(codes[j, 0:1])
        s.work(0.4)
        yield [have_halo]
        before_code = column(tail_code[3, 0:1])[TOK - 8 :]
        cd[pl.ds(0, 8), :] = jnp.where(group == 0, -1.0, before_code)
        s.work(0.1)
        s.done(have_codes)

    def share_dy():
        yield [sent_n1]
        dyf[rows_of(z), my_cols] = dy_ref[...]
        s.work(0.1)
        yield from ag_group(dyf, have_dy, sent_dy)

    def keep(k):
        code = cd[pl.ds(8, GT), :]
        return jnp.where((code >= 16.0) & (code == cd[pl.ds(8 - k, GT), :]), 1.0, 0.0)

    def ffn_block(j):
        rows = rows_of(j)
        ab = nn(n2[rows, :], w1[...].reshape(D, 2 * HP))
        a, b = ab[:, :HP], ab[:, HP:]
        sg = jax.nn.sigmoid(a)
        silu = a * sg
        uu[rows, :] = (silu * b).astype(BF)
        du = nn(dyf[rows, :], w2[...].reshape(D, HP))
        dab[rows, 0:HP] = (du * b * sg * (1.0 + a * (1.0 - sg))).astype(BF)
        dab[rows, HP : 2 * HP] = (du * silu).astype(BF)
        s.work(1.0)

    def y_part(j):
        rows = rows_of(j)
        zpart[0, rows, :] = nt(gat[rows, :], w0[...].reshape(D, 512)[:, 3 * CH :]).astype(BF)
        s.work(0.15)

    def n2_part(j):
        rows = rows_of(j)
        zpart[1, rows, :] = nt(dab[rows, :], w1[...].reshape(D, 2 * HP)).astype(BF)
        s.work(0.6)

    def u_part(j):
        rows = rows_of(j)
        zpart[2, rows, :] = nt(uu[rows, :], w2[...].reshape(D, HP)).astype(BF)
        s.work(0.35)

    def n1_part(j):
        rows = rows_of(j)
        zpart[3, rows, :] = nt(dbcv[rows, :], w0[...].reshape(D, 512)[:, : 3 * CH]).astype(BF)
        s.work(0.25)

    def main():
        yield have_n1 + full_w[0] + [have_halo]
        bcv[...] = nn(n1[...], w0[...].reshape(D, 512)[:, : 3 * CH])
        mixed = (bcv[:, 0:CH] * bcv[:, 2 * CH : 3 * CH]).astype(BF).astype(F32)
        mx[pl.ds(8, GT), :] = mixed[:GT]
        mx[pl.ds(0, 8), :] = mixed[GT + 8 :]
        s.work(1.0)
        yield [have_codes]
        zc[...] = (
            taps[0] * mx[pl.ds(8, GT), :] * keep(0)
            + taps[1] * mx[pl.ds(7, GT), :] * keep(1)
            + taps[2] * mx[pl.ds(6, GT), :] * keep(2)
        )
        gat[...] = (bcv[pl.ds(0, GT), CH : 2 * CH] * zc[...]).astype(BF)
        s.work(0.4)
        yield from rs_group(0, y_part)
        h2s[...] = tok_ref[...].astype(F32) + rs_result(0)
        h2 = h2s[...]
        copy = chip_sum(1, h2 * h2)
        s.work(0.4)
        yield [copy]
        r2 = lax.rsqrt(chip_total(1) * (1.0 / D) + EPS)
        hat2[...] = h2s[...] * r2
        n2[rows_of(z), my_cols] = (hat2[...] * gain2).astype(BF)
        s.work(0.3)
        s.add(1, ag_group(n2, have_n2, sent_n2))
        yield have_dy + full_w[1] + full_w[2] + full_w[3]
        last = Group(zd)
        for j, event, copy in ((z, have_n2[0], 0), (prev, have_n2[1], 3), (nxt, have_n2[2], 1), (far, have_n2[3], 2)):
            yield [event]
            ffn_block(j)
            if copy == 2:
                s.done(ffn)
            yield []
            n2_part(j)
            shared = share_core(1, j)
            s.add(1, send_block(j, copy, shared, last))
            yield []
        yield block_sent
        yield [last]
        dn2 = rs_result(1)
        small_out[...] = jnp.zeros((8, D), F32)
        small_out[pl.ds(1, 1), my_cols] = jnp.sum(dn2 * hat2[...], axis=0, keepdims=True)
        e2 = dn2 * gain2
        copy = chip_sum(2, e2 * hat2[...])
        s.work(0.4)
        yield [copy]
        m2 = chip_total(2) * (1.0 / D)
        r2 = lax.rsqrt(chip_total(1) * (1.0 / D) + EPS)
        e2 = rs_result(1) * gain2
        dh2s[...] = dy_ref[...].astype(F32) + r2 * (e2 - hat2[...] * m2)
        dhb[rows_of(z), my_cols] = dh2s[...].astype(BF)
        s.work(0.4)
        yield from ag_group(dhb, have_dh, sent_dh)

        dg = nn(dhb[...], w0[...].reshape(D, 512)[:, 3 * CH :])
        dbcv[:, CH : 2 * CH] = (dg * zc[...]).astype(BF)
        dz = dg * bcv[pl.ds(0, GT), CH : 2 * CH]
        q0[...] = dz * keep(0)
        q1[pl.ds(0, GT), :] = dz * keep(1)
        q2[pl.ds(0, GT), :] = dz * keep(2)
        halo_s[0] = q1[pl.ds(0, 8), :]
        halo_s[1] = q2[pl.ds(0, 8), :]
        s.work(0.6)
        copy = s.send(halo_s, halo_r, before, "x-")
        small_out[pl.ds(2, 1), ch_cols] = jnp.sum(q0[...] * mx[pl.ds(8, GT), :], axis=0, keepdims=True)
        small_out[pl.ds(3, 1), ch_cols] = jnp.sum(q1[pl.ds(0, GT), :] * mx[pl.ds(7, GT), :], axis=0, keepdims=True)
        small_out[pl.ds(4, 1), ch_cols] = jnp.sum(q2[pl.ds(0, GT), :] * mx[pl.ds(6, GT), :], axis=0, keepdims=True)
        s.work(0.3)
        yield [copy]
        last = group == 15
        q1[pl.ds(GT, 8), :] = jnp.where(last, 0.0, halo_r[0])
        q2[pl.ds(GT, 8), :] = jnp.where(last, 0.0, halo_r[1])
        dm = taps[0] * q0[...] + taps[1] * q1[pl.ds(1, GT), :] + taps[2] * q2[pl.ds(2, GT), :]
        dbcv[:, 0:CH] = (dm * bcv[pl.ds(0, GT), 2 * CH : 3 * CH]).astype(BF)
        dbcv[:, 2 * CH : 3 * CH] = (dm * bcv[pl.ds(0, GT), 0:CH]).astype(BF)
        s.work(0.4)
        s.done(conv_back)
        yield []

        yield from rs_group(3, n1_part)
        dn1 = rs_result(3)
        small_out[pl.ds(0, 1), my_cols] = jnp.sum(dn1 * hat1[...], axis=0, keepdims=True)
        e1 = dn1 * gain1
        copy = chip_sum(3, e1 * hat1[...])
        s.work(0.4)
        s.done(sums)
        yield [copy]
        m1 = chip_total(3) * (1.0 / D)
        r1 = lax.rsqrt(chip_total(0) * (1.0 / D) + EPS)
        e1 = rs_result(3) * gain1
        tg_out[...] = dh2s[...] + r1 * (e1 - hat1[...] * m1)
        s.work(0.4)

    def small_sums():
        yield [sums]
        for k, (axis, i, peers) in enumerate((("x", x, xs), ("y", y, ys), ("z", z, zs))):
            red[k, i] = small_out[...]
            group = Group(red.at[k, pl.ds(0, 3)])
            for j in (1, 3, 2):
                s.send(red.at[k, i], red.at[k, i], peers[j], *links[axis][j], group=group)
            yield [group]
            small_out[...] = (red[k, 0] + red[k, 1]) + (red[k, 2] + red[k, 3])
            s.work(0.1)
        red[3, core] = small_out[...]
        yield [s.send(red.at[3, core], red.at[3, core], peer, "c")]
        small_out[...] = red[3, 0] + red[3, 1]

    block_sent = events(4)

    def send_block(j, k, shared, last):
        yield [shared]
        add_core(1, j)
        if k:
            s.send(zp.at[1, rows_of(j)], zd.at[k - 1], zs[k], *z_links[k], group=last)
        s.done(block_sent[k])

    def hidden_out():
        yield [sent_dh]
        yield from rs_group(2, u_part)
        mix_out[...] = (h2s[...] + rs_result(2)).astype(BF)
        s.work(0.2)

    def make_half(h):
        def step(i):
            ln = lanes[1 + h]
            g1[i, :, :, ln] = tn(n2[:, pl.ds(i * 256, 256)], dab[:, ln]).astype(BF).reshape(4, 64, HP)
            s.work(0.4)

        return step

    def make_g2(i):
        g2[i] = tn(dyf[:, pl.ds(i * 256, 256)], uu[...]).astype(BF).reshape(4, 64, HP)
        s.work(0.4)

    def make_g0(i):
        cols = pl.ds(i * 256, 256)
        g0[i, :, :, 0 : 3 * CH] = tn(n1[pl.ds(0, GT), cols], dbcv[...]).astype(BF).reshape(4, 64, 3 * CH)
        g0[i, :, :, 3 * CH : 4 * CH] = tn(dhb[:, cols], gat[...]).astype(BF).reshape(4, 64, CH)
        s.work(0.35)

    made, summed = events(4), events(4, 2)

    def make(c, after_event, step):
        yield [after_event]
        for i in range(4):
            step(i)
            yield []
        s.done(made[c])

    def reduce_side(c, h, side):
        yield [made[c]]
        yield from side()
        s.done(summed[c][h])

    def hand_back(c):
        yield summed[c]
        ln = lanes[c]

        def rows(j):
            return gs[c].at[y, x, pl.ds(pl.multiple_of(j * 16, 16), 16), ln]

        group = Group(oas[c].at[pl.ds(0, 3), :, ln])
        for k in (1, 3, 2):
            s.send(rows(up(z, k)), oas[c].at[z, :, ln], zs[k], *z_links[k], group=group)
        oas[c][z, :, ln] = rows(z)[...]
        yield [group]
        outs[c][:, :, ln] = oas[c][:, :, ln].astype(F32)
        s.work(0.2)

    s.add(0, halo())
    s.add(0, deal(0))
    s.add(1, first_norm())
    for c in (1, 2, 3):
        s.add(1 + c, deal(c))
    s.add(4, share_codes())
    s.add(6, share_dy())
    for c in range(4):
        for h, side in enumerate(ag_plane(c, issued)):
            s.add(2 + c, gather_side(c, h, side))
    s.add(7, main())
    for c, after_event, step in ((1, ffn, make_half(0)), (2, ffn, make_half(1)), (3, ffn, make_g2), (0, conv_back, make_g0)):
        s.add(8 + c, make(c, after_event, step))
        for h, side in enumerate(rs_plane(c)):
            s.add(2 + c, reduce_side(c, h, side))
        s.add(4, hand_back(c))
    s.add(13, hidden_out())
    s.add(2, small_sums())
    s.run()


def block(tokens, dy, code, vec, pack0, pack1, pack2):
    vmem = pl.BlockSpec(memory_space=pltpu.VMEM)
    plane = [pltpu.VMEM((4, 4, 64, w), BF) for w in WIDTHS]
    scratch = (
        plane
        + [pltpu.VMEM((4, 4, 64, w), BF) for w in WIDTHS]
        + [pltpu.VMEM((2, 6, 4, 16, w), BF) for w in (512, HP, HP, HP)]
        + [pltpu.VMEM((2, 6, 16, w), BF) for w in (512, HP, HP, HP)]
        + [pltpu.VMEM((4, 16, w), BF) for w in WIDTHS]
        + [
            pltpu.VMEM((4, 8, CH), F32),
            pltpu.VMEM((16, HALF), BF),
            pltpu.VMEM((4, 8, CH), F32),
            pltpu.VMEM((16, CH), F32),
            pltpu.VMEM((16, CH), F32),
            pltpu.VMEM((4, 16, D), BF),
            pltpu.VMEM((GT + 16, D), BF),
            pltpu.VMEM((GT, D), BF),
            pltpu.VMEM((GT, D), BF),
            pltpu.VMEM((GT, D), BF),
            pltpu.VMEM((4, GT, D), BF),
            pltpu.VMEM((4, GT, HALF), BF),
            pltpu.VMEM((4, GT, HALF), BF),
            pltpu.VMEM((4, 6, TOK // 2, HALF), BF),
            pltpu.VMEM((3, TOK, HALF), BF),
            pltpu.VMEM((4, TOK, CH), F32),
            pltpu.VMEM((4, TOK, CH), F32),
            pltpu.VMEM((TOK, HALF), F32),
            pltpu.VMEM((TOK, HALF), F32),
            pltpu.VMEM((TOK, HALF), F32),
            pltpu.VMEM((TOK, HALF), F32),
            pltpu.VMEM((GT + 16, 3 * CH), F32),
            pltpu.VMEM((GT, 3 * CH), BF),
            pltpu.VMEM((GT, CH), F32),
            pltpu.VMEM((GT, CH), BF),
            pltpu.VMEM((GT + 8, CH), F32),
            pltpu.VMEM((GT + 8, CH), F32),
            pltpu.VMEM((GT, CH), F32),
            pltpu.VMEM((GT + 8, CH), F32),
            pltpu.VMEM((GT + 8, CH), F32),
            pltpu.VMEM((2, 8, CH), F32),
            pltpu.VMEM((2, 8, CH), F32),
            pltpu.VMEM((GT, HP), BF),
            pltpu.VMEM((GT, 2 * HP), BF),
            pltpu.VMEM((4, 4, 8, D), F32),
            pltpu.SemaphoreType.DMA((SENDS,)),
            pltpu.SemaphoreType.DMA((RECEIVES,)),
        ]
    )
    return pl.pallas_call(
        kernel,
        out_shape=[
            jax.ShapeDtypeStruct((TOK, HALF), BF),
            jax.ShapeDtypeStruct((TOK, HALF), F32),
            jax.ShapeDtypeStruct((8, D), F32),
        ]
        + [jax.ShapeDtypeStruct((4, 16, w), F32) for w in WIDTHS],
        in_specs=[vmem] * 7,
        out_specs=[vmem] * 6,
        scratch_shapes=scratch,
        compiler_params=pltpu.CompilerParams(
            collective_id=0, has_side_effects=True, vmem_limit_bytes=58 * 1024 * 1024
        ),
    )(tokens, dy, code, vec, pack0, pack1, pack2)


def local(
    tokens,
    segment_ids,
    valid_mask,
    norm1_gain,
    in_weight,
    conv_weight,
    out_weight,
    norm2_gain,
    gate_weight,
    up_weight,
    down_weight,
    out_cotangent,
):
    code = (segment_ids + 16 * valid_mask).astype(F32)
    code = jnp.broadcast_to(code[None], (8, CH))
    vec = jnp.concatenate(
        [norm1_gain[None], norm2_gain[None], conv_weight, jnp.zeros((3, D), BF)], axis=0
    ).astype(F32)

    def wide(w):
        return jnp.pad(w.reshape(16, 4, HID).transpose(1, 0, 2), ((0, 0), (0, 0), (0, HP - HID)))

    ins = in_weight.reshape(3, 16, 4, CH).transpose(2, 1, 0, 3).reshape(4, 16, 3 * CH)
    outs = out_weight.reshape(4, CH, 16).transpose(0, 2, 1)
    pack0 = jnp.concatenate([ins, outs], axis=2)
    pack1 = jnp.concatenate([wide(gate_weight), wide(up_weight)], axis=2)
    pack2 = jnp.pad(down_weight.reshape(4, HID, 16).transpose(0, 2, 1), ((0, 0), (0, 0), (0, HP - HID)))
    mixed, tokens_grad, small, p0, p1, p2 = block(tokens, out_cotangent, code, vec, pack0, pack1, pack2)
    grad_in = p0[:, :, : 3 * CH].reshape(4, 16, 3, CH).transpose(2, 1, 0, 3).reshape(3, 16, HALF)
    grad_out = p0[:, :, 3 * CH :].transpose(0, 2, 1).reshape(HALF, 16)
    grad_gate = p1[:, :, :HID].transpose(1, 0, 2).reshape(16, 4 * HID)
    grad_up = p1[:, :, HP : HP + HID].transpose(1, 0, 2).reshape(16, 4 * HID)
    grad_down = p2[:, :, :HID].transpose(0, 2, 1).reshape(4 * HID, 16)
    return (mixed, tokens_grad, small[0], grad_in, small[2:5], grad_out, small[1], grad_gate, grad_up, grad_down)


def solution(mesh):
    placed = (
        P("dp", "tensor"),
        P("dp"),
        P("dp"),
        P(),
        P(None, "dp", "tensor"),
        P(),
        P("tensor", "dp"),
        P(),
        P("dp", "tensor"),
        P("dp", "tensor"),
        P("tensor", "dp"),
        P("dp", "tensor"),
    )
    return jax.shard_map(
        local,
        mesh=mesh,
        in_specs=placed,
        out_specs=(
            P("dp", "tensor"),
            P("dp", "tensor"),
            P(),
            P(None, "dp", "tensor"),
            P(),
            P("tensor", "dp"),
            P(),
            P("dp", "tensor"),
            P("dp", "tensor"),
            P("tensor", "dp"),
        ),
        check_vma=False,
    )
```

```python
import jax
import jax.numpy as jnp
from jax import lax
from jax.experimental import pallas as pl
from jax.experimental.pallas import tpu as pltpu
from jax.sharding import PartitionSpec as P

D = 1024
EPS = 1e-05
R = 4
BF = jnp.bfloat16
F32 = jnp.float32
TOK = 128
GT = 512
HALF = 512
CH = 128
HID = 576
HP = 640
WIDTHS = (512, 2 * HP, HP)
SENDS = 48
RECEIVES = 186


def nn(a, b):
    return lax.dot_general(a, b, (((1,), (0,)), ((), ())), preferred_element_type=F32)


def nt(a, b):
    return lax.dot_general(a, b, (((1,), (1,)), ((), ())), preferred_element_type=F32)


def tn(a, b):
    return lax.dot_general(a, b, (((0,), (0,)), ((), ())), preferred_element_type=F32)


def add_into(dst, *others):
    total = dst[...].astype(F32)
    for other in others:
        total = total + other[...].astype(F32)
    dst[...] = total.astype(dst.dtype)


class Event:
    def __init__(self):
        self.time = float("inf")


class Copy(Event):
    def __init__(self, copy, time, end):
        self.copy, self.time, self.end, self.waited = copy, time, end, False

    def arrived(self):
        self.copy.wait_recv()


class Group(Event):
    def __init__(self, total):
        self.total, self.sem, self.time, self.waited = total, None, 0.0, False

    def arrived(self):
        send_sem, recv_sem, device = self.remake
        pltpu.make_async_remote_copy(
            src_ref=self.total,
            dst_ref=self.total,
            send_sem=send_sem,
            recv_sem=recv_sem,
            device_id=device,
            device_id_type=pl.DeviceIdType.MESH,
        ).wait_recv()


class Room:
    def __init__(self, schedule, link, slack):
        self.schedule, self.link, self.slack = schedule, link, slack

    @property
    def time(self):
        return self.schedule.free.get(self.link, 0.0) - self.slack


class Schedule:
    RATE = 46.8e3
    CORE_RATE = 700e3
    LATENCY = 1.65
    FAR_LATENCY = 2.3
    CORE_LATENCY = 0.9
    ISSUE = 0.05

    def __init__(self, send_sems, recv_sems):
        self.send_sems, self.recv_sems = send_sems, recv_sems
        self.pool, self.received = [None] * SENDS, 0
        self.tasks, self.free, self.now = [], {}, 2.0

    def send(self, src, dst, device, *links, group=None):
        k = min(range(SENDS), key=lambda i: -1.0 if self.pool[i] is None else self.pool[i].end)
        if self.pool[k] is not None:
            self.pool[k].copy.wait_send()
            self.now = max(self.now, self.pool[k].end)
        sem = self.received if group is None or group.sem is None else group.sem
        if sem == self.received:
            self.received += 1
            assert sem < RECEIVES
        copy = pltpu.make_async_remote_copy(
            src_ref=src,
            dst_ref=dst,
            send_sem=self.send_sems.at[k],
            recv_sem=self.recv_sems.at[sem],
            device_id=device,
            device_id_type=pl.DeviceIdType.MESH,
        )
        copy.start()
        self.now += self.ISSUE
        size = jnp.dtype(src.dtype).itemsize
        for n in src.shape:
            size *= n
        end = self.now
        for link in links:
            begin = max(self.now, self.free.get(link, 0.0))
            self.free[link] = begin + size / (self.CORE_RATE if link == "c" else self.RATE)
            end = max(end, self.free[link])
        latency = self.CORE_LATENCY if "c" in links else self.LATENCY if len(links) == 1 else self.FAR_LATENCY
        self.pool[k] = Copy(copy, end + latency, end)
        if group is None:
            return self.pool[k]
        group.sem, group.time = sem, max(group.time, end + latency)
        group.remake = (self.send_sems.at[k], self.recv_sems.at[sem], device)
        return group

    def room(self, link, slack=0.8):
        return [Room(self, link, slack)]

    def work(self, us):
        self.now += us

    def done(self, event):
        event.time = self.now

    def add(self, rank, task):
        self.tasks.append([rank, task, ()])

    def run(self):
        while self.tasks:
            times = [max([0.0] + [e.time for e in t[2]]) for t in self.tasks]
            ready = [i for i, r in enumerate(times) if r <= self.now]
            if ready:
                i = min(ready, key=lambda i: (self.tasks[i][0], times[i]))
            else:
                i = min(range(len(times)), key=lambda i: (times[i], self.tasks[i][0]))
                self.now = times[i]
            task = self.tasks[i]
            for event in task[2]:
                if isinstance(event, (Copy, Group)) and not event.waited:
                    event.arrived()
                    event.waited = True
                    self.now += 0.03
            try:
                task[2] = tuple(next(task[1]))
            except StopIteration:
                self.tasks.pop(i)
        for last in self.pool:
            if last is not None:
                last.copy.wait_send()


def ring_ag(s, axis, i, plus, minus, blk, two, issued=None):
    rest = Group(two)
    up, down = axis + "+", axis + "-"
    prev, nxt = (i + R - 1) % R, (i + 1) % R
    yield s.room(up)
    c1 = s.send(blk(i, 0), blk(i, 0), plus, up)
    yield s.room(down)
    c2 = s.send(blk(i, 1), blk(i, 1), minus, down)
    yield s.room(up)
    s.send(blk(i, 1), blk(i, 1), plus, up, group=rest)
    yield s.room(down)
    s.send(blk(i, 0), blk(i, 0), minus, down, group=rest)
    yield [c1]
    s.send(blk(prev, 0), blk(prev, 0), plus, up, group=rest)
    yield [c2]
    s.send(blk(nxt, 1), blk(nxt, 1), minus, down, group=rest)
    if issued is not None:
        s.done(issued)
    yield [rest]


def ring_rs(s, axis, i, plus, minus, blk, bufs, us):
    recv, rest = [bufs.at[k] for k in range(6)], Group(bufs.at[pl.ds(2, 4)])
    up, down = axis + "+", axis + "-"
    prev, nxt, far = (i + R - 1) % R, (i + 1) % R, (i + 2) % R
    yield s.room(up)
    c1 = s.send(blk(far, 0), recv[0], plus, up)
    yield s.room(down)
    c2 = s.send(blk(far, 1), recv[1], minus, down)
    yield s.room(up)
    s.send(blk(nxt, 1), recv[2], plus, up, group=rest)
    yield s.room(down)
    s.send(blk(prev, 0), recv[3], minus, down, group=rest)
    yield [c1]
    add_into(blk(nxt, 0), recv[0])
    s.work(us)
    s.send(blk(nxt, 0), recv[4], plus, up, group=rest)
    yield [c2]
    add_into(blk(prev, 1), recv[1])
    s.work(us)
    s.send(blk(prev, 1), recv[5], minus, down, group=rest)
    yield [rest]


def low_lanes():
    return lax.broadcasted_iota(jnp.int32, (16, CH), 1) < CH // 2


def half_tile(tile, odd):
    return jnp.where(low_lanes(), pltpu.roll(tile, CH // 2, 1) if odd else tile, 0.0)


def whole_tile(even, odd):
    return jnp.where(low_lanes(), even.astype(F32), pltpu.roll(odd.astype(F32), CH // 2, 1))


def kernel(
    tok_hbm,
    dy_hbm,
    seg_hbm,
    valid_hbm,
    gain1_hbm,
    gain2_hbm,
    conv_hbm,
    in_hbm,
    out_hbm,
    gate_hbm,
    up_hbm,
    down_hbm,
    mix_out,
    tg_out,
    small_out,
    g0_out,
    g1_out,
    g2_out,
    tok_ref,
    dy_ref,
    vec_ref,
    seg_ref,
    valid_ref,
    gain1_ref,
    gain2_ref,
    conv_ref,
    in_ref,
    out_ref,
    gate_ref,
    up_ref,
    down_ref,
    code_ref,
    pack0,
    pack1,
    pack2,
    w0,
    w1,
    w2,
    g0,
    g1,
    g2,
    ra0,
    ra1,
    ra2,
    ra3,
    rb0,
    rb1,
    rb2,
    rb3,
    oa0,
    oa1,
    oa2,
    codes,
    tail_raw,
    tail_code,
    tail_s,
    tail_r,
    tail,
    n1,
    dyf,
    n2,
    dhb,
    zpart,
    zrc,
    zp,
    zr,
    zd,
    stat_s,
    stat_r,
    hat1,
    hat2,
    h2s,
    dh2s,
    bcv,
    dbcv,
    zc,
    gat,
    mx,
    cd,
    q0,
    q1,
    q2,
    halo_s,
    halo_r,
    uu,
    dab,
    red,
    load_sems,
    send_sems,
    recv_sems,
):
    dp = lax.axis_index("dp")
    core = lax.axis_index("tensor")
    y, x, z = dp // 16, (dp // 4) % 4, dp % 4
    group = dp // 4

    def dev(yy, xx, zz):
        return (yy * 16 + xx * 4 + zz, core)

    def up(v, k=1):
        return (v + k) % R

    peer = (dp, 1 - core)
    xs = [None] + [dev(y, up(x, k), z) for k in (1, 2, 3)]
    ys = [None] + [dev(up(y, k), x, z) for k in (1, 2, 3)]
    zs = [None] + [dev(y, x, up(z, k)) for k in (1, 2, 3)]
    after = ((dp + 4) % 64, core)
    before = ((dp + 60) % 64, core)

    barrier = pltpu.get_barrier_semaphore()
    others = [peer, after, before] + xs[1:] + ys[1:] + zs[1:]
    for other in others:
        pl.semaphore_signal(barrier, inc=1, device_id=other, device_id_type=pl.DeviceIdType.MESH)
    loads = [
        pltpu.make_async_copy(src, dst, load_sems.at[k])
        for k, (src, dst) in enumerate(
            (
                (seg_hbm, seg_ref),
                (valid_hbm, valid_ref),
                (gain1_hbm, gain1_ref),
                (gain2_hbm, gain2_ref),
                (conv_hbm, conv_ref),
                (in_hbm, in_ref),
                (out_hbm, out_ref),
                (tok_hbm, tok_ref),
                (gate_hbm, gate_ref),
                (up_hbm, up_ref),
                (down_hbm, down_ref),
                (dy_hbm, dy_ref),
            )
        )
    ]
    for load in loads:
        load.start()
    for load in loads:
        load.wait()
    vec_ref[0] = gain1_ref[...].astype(F32)
    vec_ref[1] = gain2_ref[...].astype(F32)
    vec_ref[2:5] = conv_ref[...].astype(F32)
    code_ref[...] = jnp.broadcast_to((seg_ref[...] + 16 * valid_ref[...]).astype(F32)[None], (8, CH))
    for j in range(R):
        for k in range(3):
            pack0[j, :, k * CH : (k + 1) * CH] = in_ref[k, :, j * CH : (j + 1) * CH]
        pack0[j, :, 3 * CH :] = out_ref[:, j * CH : (j + 1) * CH]
        cols, tile = slice(j * HALF, (j + 1) * HALF), slice(2048 + j // 2 * CH, 2048 + (j // 2 + 1) * CH)
        for pack, k, ref in ((pack1, 0, gate_ref), (pack1, HP, up_ref), (pack2, 0, down_ref)):
            pack[j, :, k : k + HALF] = ref[:, cols]
            pack[j, :, k + HALF : k + HP] = half_tile(ref[:, tile].astype(F32), j % 2).astype(BF)
    pl.semaphore_wait(barrier, len(others))

    s = Schedule(send_sems, recv_sems)
    packs, ws, gs = (pack0, pack1, pack1, pack2), (w0, w1, w1, w2), (g0, g1, g1, g2)
    ras, rbs, oas = (ra0, ra1, ra2, ra3), (rb0, rb1, rb2, rb3), (oa0, oa1, oa1, oa2)
    outs = (g0_out, g1_out, g1_out, g2_out)
    lanes = (pl.ds(0, 512), pl.ds(0, HP), pl.ds(HP, HP), pl.ds(0, HP))
    my_cols = pl.ds(pl.multiple_of(core * HALF, HALF), HALF)
    peer_cols = pl.ds(pl.multiple_of((1 - core) * HALF, HALF), HALF)
    ch_cols = pl.ds(pl.multiple_of(core * HALF + z * CH, CH), CH)
    z_links = (None, ("z+",), ("z+", "z-"), ("z-",))
    links = {a: (None, (a + "+",), (a + "+", a + "-"), (a + "-",)) for a in "xyz"}

    def rows_of(j, count=TOK):
        return pl.ds(pl.multiple_of(j * count, count), count)

    def ag_plane(c, issued):
        w, ln = ws[c], lanes[c]

        def part(base, h):
            return pl.ds(base + 16 * h, 16)

        def side_a():
            yield from ring_ag(s, "x", x, xs[1], xs[3], lambda j, h: w.at[y, j, part(0, h), ln], w.at[y, x, :, ln])
            if c:
                yield [issued[c - 1][0]]
            yield from ring_ag(s, "y", y, ys[1], ys[3], lambda j, h: w.at[j, :, part(0, h), ln], w.at[y, :, :, ln], issued[c][0])

        def side_b():
            yield from ring_ag(s, "y", y, ys[1], ys[3], lambda j, h: w.at[j, x, part(32, h), ln], w.at[y, x, :, ln])
            if c:
                yield [issued[c - 1][1]]
            yield from ring_ag(s, "x", x, xs[1], xs[3], lambda j, h: w.at[:, j, part(32, h), ln], w.at[:, x, :, ln], issued[c][1])

        return side_a, side_b

    def rs_plane(c):
        g, ra, rb, ln, us = gs[c], ras[c], rbs[c], lanes[c], 0.12

        def part(base, h):
            return pl.ds(base + 16 * h, 16)

        def side_a():
            yield from ring_rs(
                s, "y", y, ys[1], ys[3], lambda j, h: g.at[j, :, part(0, h), ln], ra.at[0], us
            )
            for h, (u, v) in ((0, (3, 4)), (1, (2, 5))):
                add_into(g.at[y, :, part(0, h), ln], ra.at[0, u], ra.at[0, v])
                s.work(1.5 * us)
            yield from ring_rs(
                s, "x", x, xs[1], xs[3], lambda j, h: g.at[y, j, part(0, h), ln], rb.at[0], us / 3
            )
            for h, (u, v) in ((0, (3, 4)), (1, (2, 5))):
                add_into(g.at[y, x, part(0, h), ln], rb.at[0, u], rb.at[0, v])
                s.work(0.5 * us)

        def side_b():
            yield from ring_rs(
                s, "x", x, xs[1], xs[3], lambda j, h: g.at[:, j, part(32, h), ln], ra.at[1], us
            )
            for h, (u, v) in ((0, (3, 4)), (1, (2, 5))):
                add_into(g.at[:, x, part(32, h), ln], ra.at[1, u], ra.at[1, v])
                s.work(1.5 * us)
            yield from ring_rs(
                s, "y", y, ys[1], ys[3], lambda j, h: g.at[j, x, part(32, h), ln], rb.at[1], us / 3
            )
            for h, (u, v) in ((0, (3, 4)), (1, (2, 5))):
                add_into(g.at[y, x, part(32, h), ln], rb.at[1, u], rb.at[1, v])
                s.work(0.5 * us)

        return side_a, side_b

    prev, nxt, far = up(z, 3), up(z), up(z, 2)

    def ag_group(n, have, issued):
        def both(j, h, device, link, group=None):
            ref = n.at[half_rows(j, h), my_cols]
            return s.send(ref, ref, device, link, group=group)

        to_core = [Group(n.at[rows_of(j), my_cols]) for j in (z, prev, nxt, far)]

        def core_too(i, j, h):
            both(j, h, peer, "c", to_core[i])

        c1 = both(z, 0, zs[1], "z+")
        c2 = both(z, 1, zs[3], "z-")
        c3 = both(z, 1, zs[1], "z+")
        c4 = both(z, 0, zs[3], "z-")
        core_too(0, z, 0)
        core_too(0, z, 1)
        yield [to_core[0]]
        s.done(have[0])
        yield [c1]
        c5 = both(prev, 0, zs[1], "z+")
        core_too(1, prev, 0)
        yield [c2]
        c6 = both(nxt, 1, zs[3], "z-")
        s.done(issued)
        core_too(2, nxt, 1)
        yield [c3]
        core_too(1, prev, 1)
        yield [c4]
        core_too(2, nxt, 0)
        yield [to_core[1]]
        s.done(have[1])
        yield [to_core[2]]
        s.done(have[2])
        yield [c5]
        core_too(3, far, 0)
        yield [c6]
        core_too(3, far, 1)
        yield [to_core[3]]
        s.done(have[3])

    def half_rows(j, h):
        return pl.ds(pl.multiple_of(j * TOK + h * (TOK // 2), TOK // 2), TOK // 2)

    def share_core(k, j):
        return s.send(zpart.at[k, rows_of(j), peer_cols], zrc.at[k, rows_of(j)], peer, "c")

    def add_core(k, j):
        rows = rows_of(j)
        zp[k, rows] = (zpart[k, rows, my_cols].astype(F32) + zrc[k, rows].astype(F32)).astype(BF)
        s.work(0.15)

    def rs_group(k, part):
        def blk(j, h):
            return zp.at[k, half_rows(j, h)]

        recv = [zr.at[k, i] for i in range(6)]
        rest = Group(zr.at[k, pl.ds(2, 4)])
        order = (far, nxt, prev, z)
        copies = []
        for j in order:
            part(j)
            copies.append(share_core(k, j))
            yield []
        yield [copies[0]]
        add_core(k, far)
        c1 = s.send(blk(far, 0), recv[0], zs[1], "z+")
        c2 = s.send(blk(far, 1), recv[1], zs[3], "z-")
        yield [copies[1]]
        add_core(k, nxt)
        s.send(blk(nxt, 1), recv[2], zs[1], "z+", group=rest)
        yield [copies[2]]
        add_core(k, prev)
        s.send(blk(prev, 0), recv[3], zs[3], "z-", group=rest)
        yield [c1]
        add_into(blk(nxt, 0), recv[0])
        s.work(0.06)
        s.send(blk(nxt, 0), recv[4], zs[1], "z+", group=rest)
        yield [c2]
        add_into(blk(prev, 1), recv[1])
        s.work(0.06)
        s.send(blk(prev, 1), recv[5], zs[3], "z-", group=rest)
        yield [copies[3]]
        add_core(k, z)
        yield [rest]

    def rs_result(k):
        if k == 1:
            total = zp[k, rows_of(z)].astype(F32)
            for h in range(3):
                total = total + zd[h].astype(F32)
            return total

        def half(h, u, v):
            return zp[k, half_rows(z, h)].astype(F32) + zr[k, u].astype(F32) + zr[k, v].astype(F32)

        return jnp.concatenate([half(0, 3, 4), half(1, 2, 5)], axis=0)

    def chip_sum(k, values):
        stat_s[k] = jnp.broadcast_to(jnp.sum(values, axis=1, keepdims=True), (TOK, CH))
        return s.send(stat_s.at[k], stat_r.at[k], peer, "c")

    def chip_total(k):
        return (stat_s[k] + stat_r[k])[:, :1]

    def events(*dims):
        return [events(*dims[1:]) for _ in range(dims[0])] if dims else Event()

    dealt, full_w, issued = events(4), events(4, 2), events(4, 2)
    have_n1, have_n2, have_dy, have_dh = events(4), events(4), events(4), events(4)
    sent_n1, sent_n2, sent_dy, sent_dh = events(4)
    have_codes, have_halo, ffn, conv_back, sums = events(5)
    gain1 = vec_ref[pl.ds(0, 1), my_cols]
    gain2 = vec_ref[pl.ds(1, 1), my_cols]
    taps = [vec_ref[pl.ds(2 + k, 1), ch_cols] for k in range(3)]

    def deal(c):
        mine = pl.ds(pl.multiple_of(z * 16, 16), 16)
        slab = ws[c].at[y, x, mine, lanes[c]]
        group = Group(ws[c].at[y, x, pl.ds(0, 48), lanes[c]])
        for k in (1, 3, 2):
            s.send(packs[c].at[up(z, k), :, lanes[c]], slab, zs[k], *z_links[k], group=group)
        ws[c][y, x, mine, lanes[c]] = packs[c][z, :, lanes[c]]
        s.work(0.1)
        yield [group]
        s.done(dealt[c])

    def gather_side(c, h, side):
        yield [dealt[c]]
        yield from side()
        s.done(full_w[c][h])

    def first_norm():
        tok = tok_ref[...].astype(F32)
        copy = chip_sum(0, tok * tok)
        s.work(0.3)
        yield [copy]
        r1 = lax.rsqrt(chip_total(0) * (1.0 / D) + EPS)
        hat1[...] = tok_ref[...].astype(F32) * r1
        n1[rows_of(z), my_cols] = (hat1[...] * gain1).astype(BF)
        s.work(0.3)
        yield from ag_group(n1, have_n1, sent_n1)

    def halo():
        yield [
            s.send(tok_ref.at[pl.ds(TOK - 16, 16)], tail_raw, after, "x+"),
            s.send(code_ref, tail_code.at[z], after, "x+"),
        ]
        tok = tail_raw[...].astype(F32)
        tail_s[...] = jnp.broadcast_to(jnp.sum(tok * tok, axis=1, keepdims=True), (16, CH))
        yield [s.send(tail_s, tail_r, peer, "c")]
        scale = lax.rsqrt((tail_s[...] + tail_r[...])[:, :1] * (1.0 / D) + EPS)
        tail[z, :, my_cols] = (tail_raw[...].astype(F32) * scale * gain1).astype(BF)
        ref = tail.at[z, :, my_cols]
        group1, group2 = Group(tail.at[pl.ds(0, 3), :, my_cols]), Group(tail_code.at[pl.ds(0, 3)])
        for k in (1, 3, 2):
            s.send(ref, ref, zs[k], *z_links[k], group=group1)
            s.send(tail_code.at[z], tail_code.at[z], zs[k], *z_links[k], group=group2)
        s.work(0.1)
        yield [group1, group2]
        ref = tail.at[3, :, my_cols]
        yield [s.send(ref, ref, peer, "c")]
        n1[pl.ds(GT, 16), :] = tail[3]
        s.done(have_halo)

    def column(row):
        return jnp.transpose(jnp.broadcast_to(row, (CH, CH)))

    def share_codes():
        codes[z] = code_ref[...]
        group = Group(codes.at[pl.ds(0, 3)])
        for k in (1, 3, 2):
            s.send(code_ref, codes.at[z], zs[k], *z_links[k], group=group)
        yield [group]
        for j in range(4):
            cd[pl.ds(8 + j * TOK, TOK), :] = column(codes[j, 0:1])
        s.work(0.4)
        yield [have_halo]
        before_code = column(tail_code[3, 0:1])[TOK - 8 :]
        cd[pl.ds(0, 8), :] = jnp.where(group == 0, -1.0, before_code)
        s.work(0.1)
        s.done(have_codes)

    def share_dy():
        yield [sent_n1]
        dyf[rows_of(z), my_cols] = dy_ref[...]
        s.work(0.1)
        yield from ag_group(dyf, have_dy, sent_dy)

    def keep(k):
        code = cd[pl.ds(8, GT), :]
        return jnp.where((code >= 16.0) & (code == cd[pl.ds(8 - k, GT), :]), 1.0, 0.0)

    def ffn_block(j):
        rows = rows_of(j)
        ab = nn(n2[rows, :], w1[...].reshape(D, 2 * HP))
        a, b = ab[:, :HP], ab[:, HP:]
        sg = jax.nn.sigmoid(a)
        silu = a * sg
        uu[rows, :] = (silu * b).astype(BF)
        du = nn(dyf[rows, :], w2[...].reshape(D, HP))
        dab[rows, 0:HP] = (du * b * sg * (1.0 + a * (1.0 - sg))).astype(BF)
        dab[rows, HP : 2 * HP] = (du * silu).astype(BF)
        s.work(1.0)

    def y_part(j):
        rows = rows_of(j)
        zpart[0, rows, :] = nt(gat[rows, :], w0[...].reshape(D, 512)[:, 3 * CH :]).astype(BF)
        s.work(0.15)

    def n2_part(j):
        rows = rows_of(j)
        zpart[1, rows, :] = nt(dab[rows, :], w1[...].reshape(D, 2 * HP)).astype(BF)
        s.work(0.6)

    def u_part(j):
        rows = rows_of(j)
        zpart[2, rows, :] = nt(uu[rows, :], w2[...].reshape(D, HP)).astype(BF)
        s.work(0.35)

    def n1_part(j):
        rows = rows_of(j)
        zpart[3, rows, :] = nt(dbcv[rows, :], w0[...].reshape(D, 512)[:, : 3 * CH]).astype(BF)
        s.work(0.25)

    def main():
        yield have_n1 + full_w[0] + [have_halo]
        bcv[...] = nn(n1[...], w0[...].reshape(D, 512)[:, : 3 * CH])
        mixed = (bcv[:, 0:CH] * bcv[:, 2 * CH : 3 * CH]).astype(BF).astype(F32)
        mx[pl.ds(8, GT), :] = mixed[:GT]
        mx[pl.ds(0, 8), :] = mixed[GT + 8 :]
        s.work(1.0)
        yield [have_codes]
        zc[...] = (
            taps[0] * mx[pl.ds(8, GT), :] * keep(0)
            + taps[1] * mx[pl.ds(7, GT), :] * keep(1)
            + taps[2] * mx[pl.ds(6, GT), :] * keep(2)
        )
        gat[...] = (bcv[pl.ds(0, GT), CH : 2 * CH] * zc[...]).astype(BF)
        s.work(0.4)
        yield from rs_group(0, y_part)
        h2s[...] = tok_ref[...].astype(F32) + rs_result(0)
        h2 = h2s[...]
        copy = chip_sum(1, h2 * h2)
        s.work(0.4)
        yield [copy]
        r2 = lax.rsqrt(chip_total(1) * (1.0 / D) + EPS)
        hat2[...] = h2s[...] * r2
        n2[rows_of(z), my_cols] = (hat2[...] * gain2).astype(BF)
        s.work(0.3)
        s.add(1, ag_group(n2, have_n2, sent_n2))
        yield have_dy + full_w[1] + full_w[2] + full_w[3]
        last = Group(zd)
        for j, event, copy in ((z, have_n2[0], 0), (prev, have_n2[1], 3), (nxt, have_n2[2], 1), (far, have_n2[3], 2)):
            yield [event]
            ffn_block(j)
            if copy == 2:
                s.done(ffn)
            yield []
            n2_part(j)
            shared = share_core(1, j)
            s.add(1, send_block(j, copy, shared, last))
            yield []
        yield block_sent
        yield [last]
        dn2 = rs_result(1)
        small_out[...] = jnp.zeros((8, D), F32)
        small_out[pl.ds(1, 1), my_cols] = jnp.sum(dn2 * hat2[...], axis=0, keepdims=True)
        e2 = dn2 * gain2
        copy = chip_sum(2, e2 * hat2[...])
        s.work(0.4)
        yield [copy]
        m2 = chip_total(2) * (1.0 / D)
        r2 = lax.rsqrt(chip_total(1) * (1.0 / D) + EPS)
        e2 = rs_result(1) * gain2
        dh2s[...] = dy_ref[...].astype(F32) + r2 * (e2 - hat2[...] * m2)
        dhb[rows_of(z), my_cols] = dh2s[...].astype(BF)
        s.work(0.4)
        yield from ag_group(dhb, have_dh, sent_dh)

        dg = nn(dhb[...], w0[...].reshape(D, 512)[:, 3 * CH :])
        dbcv[:, CH : 2 * CH] = (dg * zc[...]).astype(BF)
        dz = dg * bcv[pl.ds(0, GT), CH : 2 * CH]
        q0[...] = dz * keep(0)
        q1[pl.ds(0, GT), :] = dz * keep(1)
        q2[pl.ds(0, GT), :] = dz * keep(2)
        halo_s[0] = q1[pl.ds(0, 8), :]
        halo_s[1] = q2[pl.ds(0, 8), :]
        s.work(0.6)
        copy = s.send(halo_s, halo_r, before, "x-")
        small_out[pl.ds(2, 1), ch_cols] = jnp.sum(q0[...] * mx[pl.ds(8, GT), :], axis=0, keepdims=True)
        small_out[pl.ds(3, 1), ch_cols] = jnp.sum(q1[pl.ds(0, GT), :] * mx[pl.ds(7, GT), :], axis=0, keepdims=True)
        small_out[pl.ds(4, 1), ch_cols] = jnp.sum(q2[pl.ds(0, GT), :] * mx[pl.ds(6, GT), :], axis=0, keepdims=True)
        s.work(0.3)
        yield [copy]
        last = group == 15
        q1[pl.ds(GT, 8), :] = jnp.where(last, 0.0, halo_r[0])
        q2[pl.ds(GT, 8), :] = jnp.where(last, 0.0, halo_r[1])
        dm = taps[0] * q0[...] + taps[1] * q1[pl.ds(1, GT), :] + taps[2] * q2[pl.ds(2, GT), :]
        dbcv[:, 0:CH] = (dm * bcv[pl.ds(0, GT), 2 * CH : 3 * CH]).astype(BF)
        dbcv[:, 2 * CH : 3 * CH] = (dm * bcv[pl.ds(0, GT), 0:CH]).astype(BF)
        s.work(0.4)
        s.done(conv_back)
        yield []

        yield from rs_group(3, n1_part)
        dn1 = rs_result(3)
        small_out[pl.ds(0, 1), my_cols] = jnp.sum(dn1 * hat1[...], axis=0, keepdims=True)
        e1 = dn1 * gain1
        copy = chip_sum(3, e1 * hat1[...])
        s.work(0.4)
        s.done(sums)
        yield [copy]
        m1 = chip_total(3) * (1.0 / D)
        r1 = lax.rsqrt(chip_total(0) * (1.0 / D) + EPS)
        e1 = rs_result(3) * gain1
        tg_out[...] = dh2s[...] + r1 * (e1 - hat1[...] * m1)
        s.work(0.4)

    def small_sums():
        yield [sums]
        for k, (axis, i, peers) in enumerate((("x", x, xs), ("y", y, ys), ("z", z, zs))):
            red[k, i] = small_out[...]
            group = Group(red.at[k, pl.ds(0, 3)])
            for j in (1, 3, 2):
                s.send(red.at[k, i], red.at[k, i], peers[j], *links[axis][j], group=group)
            yield [group]
            small_out[...] = (red[k, 0] + red[k, 1]) + (red[k, 2] + red[k, 3])
            s.work(0.1)
        red[3, core] = small_out[...]
        yield [s.send(red.at[3, core], red.at[3, core], peer, "c")]
        small_out[...] = red[3, 0] + red[3, 1]

    block_sent = events(4)

    def send_block(j, k, shared, last):
        yield [shared]
        add_core(1, j)
        if k:
            s.send(zp.at[1, rows_of(j)], zd.at[k - 1], zs[k], *z_links[k], group=last)
        s.done(block_sent[k])

    def hidden_out():
        yield [sent_dh]
        yield from rs_group(2, u_part)
        mix_out[...] = (h2s[...] + rs_result(2)).astype(BF)
        s.work(0.2)

    def make_half(h):
        def step(i):
            ln = lanes[1 + h]
            g1[i, :, :, ln] = tn(n2[:, pl.ds(i * 256, 256)], dab[:, ln]).astype(BF).reshape(4, 64, HP)
            s.work(0.4)

        return step

    def make_g2(i):
        g2[i] = tn(dyf[:, pl.ds(i * 256, 256)], uu[...]).astype(BF).reshape(4, 64, HP)
        s.work(0.4)

    def make_g0(i):
        cols = pl.ds(i * 256, 256)
        g0[i, :, :, 0 : 3 * CH] = tn(n1[pl.ds(0, GT), cols], dbcv[...]).astype(BF).reshape(4, 64, 3 * CH)
        g0[i, :, :, 3 * CH : 4 * CH] = tn(dhb[:, cols], gat[...]).astype(BF).reshape(4, 64, CH)
        s.work(0.35)

    made, summed = events(4), events(4, 2)

    def make(c, after_event, step):
        yield [after_event]
        for i in range(4):
            step(i)
            yield []
        s.done(made[c])

    def reduce_side(c, h, side):
        yield [made[c]]
        yield from side()
        s.done(summed[c][h])

    def hand_back(c):
        yield summed[c]
        ln = lanes[c]

        def rows(j):
            return gs[c].at[y, x, pl.ds(pl.multiple_of(j * 16, 16), 16), ln]

        group = Group(oas[c].at[pl.ds(0, 3), :, ln])
        for k in (1, 3, 2):
            s.send(rows(up(z, k)), oas[c].at[z, :, ln], zs[k], *z_links[k], group=group)
        oas[c][z, :, ln] = rows(z)[...]
        yield [group]
        outs[c][:, :, ln] = oas[c][:, :, ln]
        s.work(0.2)

    s.add(0, halo())
    s.add(0, deal(0))
    s.add(1, first_norm())
    for c in (1, 2, 3):
        s.add(1 + c, deal(c))
    s.add(4, share_codes())
    s.add(6, share_dy())
    for c in range(4):
        for h, side in enumerate(ag_plane(c, issued)):
            s.add(2 + c, gather_side(c, h, side))
    s.add(7, main())
    for c, after_event, step in ((1, ffn, make_half(0)), (2, ffn, make_half(1)), (3, ffn, make_g2), (0, conv_back, make_g0)):
        s.add(8 + c, make(c, after_event, step))
        for h, side in enumerate(rs_plane(c)):
            s.add(2 + c, reduce_side(c, h, side))
        s.add(4, hand_back(c))
    s.add(13, hidden_out())
    s.add(2, small_sums())
    s.run()


def finish(mix, tg, small, p0, p1, p2, o_mix, o_tg, o_gain1, o_in, o_conv, o_out, o_gain2, o_gate, o_up, o_down):
    o_mix[...] = mix[...]
    o_tg[...] = tg[...]
    o_gain1[...] = small[0]
    o_gain2[...] = small[1]
    o_conv[...] = small[2:5]
    for j in range(R):
        for k in range(3):
            o_in[k, :, j * CH : (j + 1) * CH] = p0[j, :, k * CH : (k + 1) * CH].astype(F32)
        o_out[:, j * CH : (j + 1) * CH] = p0[j, :, 3 * CH :].astype(F32)
        cols = slice(j * HALF, (j + 1) * HALF)
        o_gate[:, cols] = p1[j, :, 0:HALF].astype(F32)
        o_up[:, cols] = p1[j, :, HP : HP + HALF].astype(F32)
        o_down[:, cols] = p2[j, :, 0:HALF].astype(F32)
    for t in range(2):
        tile = slice(2048 + t * CH, 2048 + (t + 1) * CH)
        o_gate[:, tile] = whole_tile(p1[2 * t, :, HALF:HP], p1[2 * t + 1, :, HALF:HP])
        o_up[:, tile] = whole_tile(p1[2 * t, :, HP + HALF :], p1[2 * t + 1, :, HP + HALF :])
        o_down[:, tile] = whole_tile(p2[2 * t, :, HALF:HP], p2[2 * t + 1, :, HALF:HP])


def block(tokens, dy, seg, valid, gain1, gain2, conv, in_weight, out_weight, gate, up, down):
    vmem = pl.BlockSpec(memory_space=pltpu.VMEM)
    loaded = [
        pltpu.VMEM((TOK, HALF), BF),
        pltpu.VMEM((TOK, HALF), BF),
        pltpu.VMEM((8, D), F32),
        pltpu.VMEM((TOK,), jnp.int32),
        pltpu.VMEM((TOK,), jnp.int32),
        pltpu.VMEM((D,), BF),
        pltpu.VMEM((D,), BF),
        pltpu.VMEM((3, D), BF),
        pltpu.VMEM((3, 16, HALF), BF),
        pltpu.VMEM((16, HALF), BF),
        pltpu.VMEM((16, R * HID), BF),
        pltpu.VMEM((16, R * HID), BF),
        pltpu.VMEM((16, R * HID), BF),
        pltpu.VMEM((8, CH), F32),
    ] + [pltpu.VMEM((R, 16, w), BF) for w in WIDTHS]
    plane = [pltpu.VMEM((4, 4, 64, w), BF) for w in WIDTHS]
    scratch = (
        loaded
        + plane
        + [pltpu.VMEM((4, 4, 64, w), BF) for w in WIDTHS]
        + [pltpu.VMEM((2, 6, 4, 16, w), BF) for w in (512, HP, HP, HP)]
        + [pltpu.VMEM((2, 6, 16, w), BF) for w in (512, HP, HP, HP)]
        + [pltpu.VMEM((4, 16, w), BF) for w in WIDTHS]
        + [
            pltpu.VMEM((4, 8, CH), F32),
            pltpu.VMEM((16, HALF), BF),
            pltpu.VMEM((4, 8, CH), F32),
            pltpu.VMEM((16, CH), F32),
            pltpu.VMEM((16, CH), F32),
            pltpu.VMEM((4, 16, D), BF),
            pltpu.VMEM((GT + 16, D), BF),
            pltpu.VMEM((GT, D), BF),
            pltpu.VMEM((GT, D), BF),
            pltpu.VMEM((GT, D), BF),
            pltpu.VMEM((4, GT, D), BF),
            pltpu.VMEM((4, GT, HALF), BF),
            pltpu.VMEM((4, GT, HALF), BF),
            pltpu.VMEM((4, 6, TOK // 2, HALF), BF),
            pltpu.VMEM((3, TOK, HALF), BF),
            pltpu.VMEM((4, TOK, CH), F32),
            pltpu.VMEM((4, TOK, CH), F32),
            pltpu.VMEM((TOK, HALF), F32),
            pltpu.VMEM((TOK, HALF), F32),
            pltpu.VMEM((TOK, HALF), F32),
            pltpu.VMEM((TOK, HALF), F32),
            pltpu.VMEM((GT + 16, 3 * CH), F32),
            pltpu.VMEM((GT, 3 * CH), BF),
            pltpu.VMEM((GT, CH), F32),
            pltpu.VMEM((GT, CH), BF),
            pltpu.VMEM((GT + 8, CH), F32),
            pltpu.VMEM((GT + 8, CH), F32),
            pltpu.VMEM((GT, CH), F32),
            pltpu.VMEM((GT + 8, CH), F32),
            pltpu.VMEM((GT + 8, CH), F32),
            pltpu.VMEM((2, 8, CH), F32),
            pltpu.VMEM((2, 8, CH), F32),
            pltpu.VMEM((GT, HP), BF),
            pltpu.VMEM((GT, 2 * HP), BF),
            pltpu.VMEM((4, 4, 8, D), F32),
            pltpu.SemaphoreType.DMA((12,)),
            pltpu.SemaphoreType.DMA((SENDS,)),
            pltpu.SemaphoreType.DMA((RECEIVES,)),
        ]
    )
    packed = pl.pallas_call(
        kernel,
        out_shape=[
            jax.ShapeDtypeStruct((TOK, HALF), BF),
            jax.ShapeDtypeStruct((TOK, HALF), F32),
            jax.ShapeDtypeStruct((8, D), F32),
        ]
        + [jax.ShapeDtypeStruct((R, 16, w), BF) for w in WIDTHS],
        in_specs=[pl.BlockSpec(memory_space=pl.ANY)] * 12,
        out_specs=[vmem] * 6,
        scratch_shapes=scratch,
        compiler_params=pltpu.CompilerParams(
            collective_id=0, has_side_effects=True, vmem_limit_bytes=58 * 1024 * 1024
        ),
    )(tokens, dy, seg, valid, gain1, gain2, conv, in_weight, out_weight, gate, up, down)
    return pl.pallas_call(
        finish,
        out_shape=[
            jax.ShapeDtypeStruct((TOK, HALF), BF),
            jax.ShapeDtypeStruct((TOK, HALF), F32),
            jax.ShapeDtypeStruct((D,), F32),
            jax.ShapeDtypeStruct((3, 16, HALF), F32),
            jax.ShapeDtypeStruct((3, D), F32),
            jax.ShapeDtypeStruct((16, HALF), F32),
            jax.ShapeDtypeStruct((D,), F32),
            jax.ShapeDtypeStruct((16, R * HID), F32),
            jax.ShapeDtypeStruct((16, R * HID), F32),
            jax.ShapeDtypeStruct((16, R * HID), F32),
        ],
        in_specs=[vmem] * 6,
        out_specs=[vmem] * 10,
    )(*packed)


def local(
    tokens,
    segment_ids,
    valid_mask,
    norm1_gain,
    in_weight,
    conv_weight,
    out_weight,
    norm2_gain,
    gate_weight,
    up_weight,
    down_weight,
    out_cotangent,
):
    outs = list(
        block(
            tokens,
            out_cotangent,
            segment_ids,
            valid_mask,
            norm1_gain,
            norm2_gain,
            conv_weight,
            in_weight,
            out_weight.T,
            gate_weight,
            up_weight,
            down_weight.T,
        )
    )
    outs[5], outs[9] = outs[5].T, outs[9].T
    return tuple(outs)


def solution(mesh):
    placed = (
        P("dp", "tensor"),
        P("dp"),
        P("dp"),
        P(),
        P(None, "dp", "tensor"),
        P(),
        P("tensor", "dp"),
        P(),
        P("dp", "tensor"),
        P("dp", "tensor"),
        P("tensor", "dp"),
        P("dp", "tensor"),
    )
    return jax.shard_map(
        local,
        mesh=mesh,
        in_specs=placed,
        out_specs=(
            P("dp", "tensor"),
            P("dp", "tensor"),
            P(),
            P(None, "dp", "tensor"),
            P(),
            P("tensor", "dp"),
            P(),
            P("dp", "tensor"),
            P("dp", "tensor"),
            P("tensor", "dp"),
        ),
        check_vma=False,
    )
```

```python
import jax
import jax.numpy as jnp
from jax import lax
from jax.experimental import pallas as pl
from jax.experimental.pallas import tpu as pltpu
from jax.sharding import PartitionSpec as P

D = 1024
EPS = 1e-05
R = 4
BF = jnp.bfloat16
F32 = jnp.float32
TOK = 128
GT = 512
HALF = 512
CH = 128
HID = 576
HP = 640
WIDTHS = (512, 2 * HP, HP)
BVC = (0, 2, 1)
SENDS = 48
RECEIVES = 200


def nn(a, b):
    return lax.dot_general(a, b, (((1,), (0,)), ((), ())), preferred_element_type=F32)


def nt(a, b):
    return lax.dot_general(a, b, (((1,), (1,)), ((), ())), preferred_element_type=F32)


def tn(a, b):
    return lax.dot_general(a, b, (((0,), (0,)), ((), ())), preferred_element_type=F32)


def add_into(dst, *others):
    total = dst[...].astype(F32)
    for other in others:
        total = total + other[...].astype(F32)
    dst[...] = total.astype(dst.dtype)


class Event:
    def __init__(self):
        self.time = float("inf")


class Copy(Event):
    def __init__(self, copy, time, end):
        self.copy, self.time, self.end, self.waited = copy, time, end, False

    def arrived(self):
        self.copy.wait_recv()


class Group(Event):
    def __init__(self, total):
        self.total, self.sem, self.time, self.waited = total, None, 0.0, False

    def arrived(self):
        send_sem, recv_sem, device = self.remake
        pltpu.make_async_remote_copy(
            src_ref=self.total,
            dst_ref=self.total,
            send_sem=send_sem,
            recv_sem=recv_sem,
            device_id=device,
            device_id_type=pl.DeviceIdType.MESH,
        ).wait_recv()


class Room:
    def __init__(self, schedule, link, slack):
        self.schedule, self.link, self.slack = schedule, link, slack

    @property
    def time(self):
        if self.link in self.schedule.quiet:
            return float("inf")
        return self.schedule.free.get(self.link, 0.0) - self.slack


class Schedule:
    RATE = 38.0e3
    CORE_RATE = 700e3
    LATENCY = 2.6
    FAR_LATENCY = 3.6
    CORE_LATENCY = 1.7
    ISSUE = 0.05

    def __init__(self, send_sems, recv_sems):
        self.send_sems, self.recv_sems = send_sems, recv_sems
        self.pool, self.received, self.quiet = [None] * SENDS, 0, ()
        self.tasks, self.free, self.now = [], {}, 3.7

    def send(self, src, dst, device, *links, group=None):
        k = min(range(SENDS), key=lambda i: -1.0 if self.pool[i] is None else self.pool[i].end)
        if self.pool[k] is not None:
            self.pool[k].copy.wait_send()
            self.now = max(self.now, self.pool[k].end)
        sem = self.received if group is None or group.sem is None else group.sem
        if sem == self.received:
            self.received += 1
            assert sem < RECEIVES
        copy = pltpu.make_async_remote_copy(
            src_ref=src,
            dst_ref=dst,
            send_sem=self.send_sems.at[k],
            recv_sem=self.recv_sems.at[sem],
            device_id=device,
            device_id_type=pl.DeviceIdType.MESH,
        )
        copy.start()
        self.now += self.ISSUE
        size = jnp.dtype(src.dtype).itemsize
        for n in src.shape:
            size *= n
        end = self.now
        for link in links:
            begin = max(self.now, self.free.get(link, 0.0))
            self.free[link] = begin + size / (self.CORE_RATE if link == "c" else self.RATE)
            end = max(end, self.free[link])
        latency = self.CORE_LATENCY if "c" in links else self.LATENCY if len(links) == 1 else self.FAR_LATENCY
        self.pool[k] = Copy(copy, end + latency, end)
        if group is None:
            return self.pool[k]
        group.sem, group.time = sem, max(group.time, end + latency)
        group.remake = (self.send_sems.at[k], self.recv_sems.at[sem], device)
        return group

    def room(self, link, slack=12.0):
        return [Room(self, link, slack)]

    def work(self, us):
        self.now += us

    def done(self, event):
        event.time = self.now

    def add(self, rank, task):
        self.tasks.append([rank, task, ()])

    def run(self):
        while self.tasks:
            times = [max([0.0] + [e.time for e in t[2]]) for t in self.tasks]
            ready = [i for i, r in enumerate(times) if r <= self.now]
            if ready:
                i = min(ready, key=lambda i: (self.tasks[i][0], times[i]))
            else:
                i = min(range(len(times)), key=lambda i: (times[i], self.tasks[i][0]))
                self.now = times[i]
            task = self.tasks[i]
            for event in task[2]:
                if isinstance(event, (Copy, Group)) and not event.waited:
                    event.arrived()
                    event.waited = True
                    self.now += 0.03
            try:
                task[2] = tuple(next(task[1]))
            except StopIteration:
                self.tasks.pop(i)
        for last in self.pool:
            if last is not None:
                last.copy.wait_send()


def ring_ag(s, axis, i, plus, minus, blk, two, issued=None):
    rest = Group(two)
    up, down = axis + "+", axis + "-"
    prev, nxt = (i + R - 1) % R, (i + 1) % R
    yield s.room(up)
    c1 = s.send(blk(i, 0), blk(i, 0), plus, up)
    yield s.room(down)
    c2 = s.send(blk(i, 1), blk(i, 1), minus, down)
    yield s.room(up)
    s.send(blk(i, 1), blk(i, 1), plus, up, group=rest)
    yield s.room(down)
    s.send(blk(i, 0), blk(i, 0), minus, down, group=rest)
    yield [c1]
    s.send(blk(prev, 0), blk(prev, 0), plus, up, group=rest)
    yield [c2]
    s.send(blk(nxt, 1), blk(nxt, 1), minus, down, group=rest)
    if issued is not None:
        s.done(issued)
    yield [rest]


def ring_rs(s, axis, i, plus, minus, blk, bufs, us):
    recv, rest = [bufs.at[k] for k in range(6)], Group(bufs.at[pl.ds(2, 4)])
    up, down = axis + "+", axis + "-"
    prev, nxt, far = (i + R - 1) % R, (i + 1) % R, (i + 2) % R
    yield s.room(up)
    c1 = s.send(blk(far, 0), recv[0], plus, up)
    yield s.room(down)
    c2 = s.send(blk(far, 1), recv[1], minus, down)
    yield s.room(up)
    s.send(blk(nxt, 1), recv[2], plus, up, group=rest)
    yield s.room(down)
    s.send(blk(prev, 0), recv[3], minus, down, group=rest)
    yield [c1]
    add_into(blk(nxt, 0), recv[0])
    s.work(us)
    s.send(blk(nxt, 0), recv[4], plus, up, group=rest)
    yield [c2]
    add_into(blk(prev, 1), recv[1])
    s.work(us)
    s.send(blk(prev, 1), recv[5], minus, down, group=rest)
    yield [rest]


def low_lanes():
    return lax.broadcasted_iota(jnp.int32, (16, CH), 1) < CH // 2


def half_tile(tile, odd):
    return jnp.where(low_lanes(), pltpu.roll(tile, CH // 2, 1) if odd else tile, 0.0)


def whole_tile(even, odd):
    return jnp.where(low_lanes(), even.astype(F32), pltpu.roll(odd.astype(F32), CH // 2, 1))


def kernel(
    tok_hbm,
    dy_hbm,
    seg_hbm,
    valid_hbm,
    gain1_hbm,
    gain2_hbm,
    conv_hbm,
    in_hbm,
    out_hbm,
    gate_hbm,
    up_hbm,
    down_hbm,
    mix_out,
    tg_out,
    small_sum,
    g0_out,
    g1_out,
    g2_out,
    tok_ref,
    dy_ref,
    vec_ref,
    seg_ref,
    valid_ref,
    gain1_ref,
    gain2_ref,
    conv_ref,
    in_ref,
    out_ref,
    gate_ref,
    up_ref,
    down_ref,
    code_ref,
    pack0,
    pack1,
    pack2,
    w0,
    w1,
    w2,
    g0,
    g1,
    g2,
    ra0,
    ra1,
    ra2,
    ra3,
    ra4,
    rb0,
    rb1,
    rb2,
    rb3,
    rb4,
    oa0,
    oa1,
    oa2,
    codes,
    tail_raw,
    tail_code,
    tail_s,
    tail_r,
    tail,
    n1,
    dyf,
    n2,
    dhb,
    zpart,
    zrc,
    zp,
    zr,
    zd,
    stat_s,
    stat_r,
    hat1,
    hat2,
    h2s,
    dh2s,
    bcv,
    dbcv,
    zc,
    gat,
    mx,
    cd,
    q0,
    q1,
    q2,
    halo_s,
    halo_r,
    uu,
    dab,
    red,
    redc,
    small_out,
    load_sems,
    send_sems,
    recv_sems,
):
    dp = lax.axis_index("dp")
    core = lax.axis_index("tensor")
    y, x, z = dp // 16, (dp // 4) % 4, dp % 4
    group = dp // 4

    def dev(yy, xx, zz):
        return (yy * 16 + xx * 4 + zz, core)

    def up(v, k=1):
        return (v + k) % R

    peer = (dp, 1 - core)
    xs = [None] + [dev(y, up(x, k), z) for k in (1, 2, 3)]
    ys = [None] + [dev(up(y, k), x, z) for k in (1, 2, 3)]
    zs = [None] + [dev(y, x, up(z, k)) for k in (1, 2, 3)]
    after = ((dp + 4) % 64, core)
    before = ((dp + 60) % 64, core)

    barrier = pltpu.get_barrier_semaphore()
    others = [peer, after, before] + xs[1:] + ys[1:] + zs[1:]
    for other in others:
        pl.semaphore_signal(barrier, inc=1, device_id=other, device_id_type=pl.DeviceIdType.MESH)
    loads = [
        pltpu.make_async_copy(src, dst, load_sems.at[k])
        for k, (src, dst) in enumerate(
            (
                (seg_hbm, seg_ref),
                (valid_hbm, valid_ref),
                (gain1_hbm, gain1_ref),
                (gain2_hbm, gain2_ref),
                (conv_hbm, conv_ref),
                (in_hbm, in_ref),
                (out_hbm, out_ref),
                (tok_hbm, tok_ref),
                (gate_hbm, gate_ref),
                (up_hbm, up_ref),
                (down_hbm, down_ref),
                (dy_hbm, dy_ref),
            )
        )
    ]
    for load in loads:
        load.start()
    for load in loads:
        load.wait()
    vec_ref[0] = gain1_ref[...].astype(F32)
    vec_ref[1] = gain2_ref[...].astype(F32)
    vec_ref[2:5] = conv_ref[...].astype(F32)
    code_ref[...] = jnp.broadcast_to((seg_ref[...] + 16 * valid_ref[...]).astype(F32)[None], (8, CH))
    for j in range(R):
        for k in range(3):
            pack0[j, :, k * CH : (k + 1) * CH] = in_ref[BVC[k], :, j * CH : (j + 1) * CH]
        pack0[j, :, 3 * CH :] = out_ref[:, j * CH : (j + 1) * CH]
        cols, tile = slice(j * HALF, (j + 1) * HALF), slice(2048 + j // 2 * CH, 2048 + (j // 2 + 1) * CH)
        for pack, k, ref in ((pack1, 0, gate_ref), (pack1, HP, up_ref), (pack2, 0, down_ref)):
            pack[j, :, k : k + HALF] = ref[:, cols]
            pack[j, :, k + HALF : k + HP] = half_tile(ref[:, tile].astype(F32), j % 2).astype(BF)
    pl.semaphore_wait(barrier, len(others))

    s = Schedule(send_sems, recv_sems)
    packs, ws, gs = (pack0, pack1, pack1, pack2), (w0, w1, w1, w2), (g0, g1, g1, g2, g0)
    ras, rbs, oas = (ra0, ra1, ra2, ra3, ra4), (rb0, rb1, rb2, rb3, rb4), (oa0, oa1, oa1, oa2, oa0)
    outs = (g0_out, g1_out, g1_out, g2_out, g0_out)
    lanes = (pl.ds(0, 512), pl.ds(0, HP), pl.ds(HP, HP), pl.ds(0, HP))
    grad_lanes = (pl.ds(2 * CH, 2 * CH),) + lanes[1:] + (pl.ds(0, 2 * CH),)
    my_cols = pl.ds(pl.multiple_of(core * HALF, HALF), HALF)
    peer_cols = pl.ds(pl.multiple_of((1 - core) * HALF, HALF), HALF)
    ch_cols = pl.ds(pl.multiple_of(core * HALF + z * CH, CH), CH)
    z_links = (None, ("z+",), ("z+", "z-"), ("z-",))
    links = {a: (None, (a + "+",), (a + "+", a + "-"), (a + "-",)) for a in "xyz"}

    def rows_of(j, count=TOK):
        return pl.ds(pl.multiple_of(j * count, count), count)

    def ag_plane(c, issued):
        w, ln = ws[c], lanes[c]

        def part(base, h):
            return pl.ds(base + 16 * h, 16)

        def side_a():
            yield from ring_ag(s, "x", x, xs[1], xs[3], lambda j, h: w.at[y, j, part(0, h), ln], w.at[y, x, :, ln])
            if c:
                yield [issued[c - 1][0]]
            yield from ring_ag(s, "y", y, ys[1], ys[3], lambda j, h: w.at[j, :, part(0, h), ln], w.at[y, :, :, ln], issued[c][0])

        def side_b():
            yield from ring_ag(s, "y", y, ys[1], ys[3], lambda j, h: w.at[j, x, part(32, h), ln], w.at[y, x, :, ln])
            if c:
                yield [issued[c - 1][1]]
            yield from ring_ag(s, "x", x, xs[1], xs[3], lambda j, h: w.at[:, j, part(32, h), ln], w.at[:, x, :, ln], issued[c][1])

        return side_a, side_b

    def rs_plane(c):
        g, ra, rb, ln, us = gs[c], ras[c], rbs[c], grad_lanes[c], 0.12

        def part(base, h):
            return pl.ds(base + 16 * h, 16)

        def side_a():
            yield from ring_rs(
                s, "y", y, ys[1], ys[3], lambda j, h: g.at[j, :, part(0, h), ln], ra.at[0], us
            )
            for h, (u, v) in ((0, (3, 4)), (1, (2, 5))):
                add_into(g.at[y, :, part(0, h), ln], ra.at[0, u], ra.at[0, v])
                s.work(1.5 * us)
            yield from ring_rs(
                s, "x", x, xs[1], xs[3], lambda j, h: g.at[y, j, part(0, h), ln], rb.at[0], us / 3
            )
            for h, (u, v) in ((0, (3, 4)), (1, (2, 5))):
                add_into(g.at[y, x, part(0, h), ln], rb.at[0, u], rb.at[0, v])
                s.work(0.5 * us)

        def side_b():
            yield from ring_rs(
                s, "x", x, xs[1], xs[3], lambda j, h: g.at[:, j, part(32, h), ln], ra.at[1], us
            )
            for h, (u, v) in ((0, (3, 4)), (1, (2, 5))):
                add_into(g.at[:, x, part(32, h), ln], ra.at[1, u], ra.at[1, v])
                s.work(1.5 * us)
            yield from ring_rs(
                s, "y", y, ys[1], ys[3], lambda j, h: g.at[j, x, part(32, h), ln], rb.at[1], us / 3
            )
            for h, (u, v) in ((0, (3, 4)), (1, (2, 5))):
                add_into(g.at[y, x, part(32, h), ln], rb.at[1, u], rb.at[1, v])
                s.work(0.5 * us)

        return side_a, side_b

    prev, nxt, far = up(z, 3), up(z), up(z, 2)

    def ag_group(n, have, issued):
        def both(j, h, device, link, group=None):
            ref = n.at[half_rows(j, h), my_cols]
            return s.send(ref, ref, device, link, group=group)

        to_core = [Group(n.at[rows_of(j), my_cols]) for j in (z, prev, nxt, far)]

        def core_too(i, j, h):
            both(j, h, peer, "c", to_core[i])

        c1 = both(z, 0, zs[1], "z+")
        c2 = both(z, 1, zs[3], "z-")
        c3 = both(z, 1, zs[1], "z+")
        c4 = both(z, 0, zs[3], "z-")
        core_too(0, z, 0)
        core_too(0, z, 1)
        yield [to_core[0]]
        s.done(have[0])
        yield [c1]
        c5 = both(prev, 0, zs[1], "z+")
        core_too(1, prev, 0)
        yield [c2]
        c6 = both(nxt, 1, zs[3], "z-")
        s.done(issued)
        core_too(2, nxt, 1)
        yield [c3]
        core_too(1, prev, 1)
        yield [c4]
        core_too(2, nxt, 0)
        if n is dhb:
            s.quiet = ("x-", "y-")
        yield [to_core[1]]
        s.done(have[1])
        yield [to_core[2]]
        s.done(have[2])
        yield [c5]
        core_too(3, far, 0)
        yield [c6]
        core_too(3, far, 1)
        yield [to_core[3]]
        s.done(have[3])

    def half_rows(j, h):
        return pl.ds(pl.multiple_of(j * TOK + h * (TOK // 2), TOK // 2), TOK // 2)

    def share_core(k, j):
        return s.send(zpart.at[k, rows_of(j), peer_cols], zrc.at[k, rows_of(j)], peer, "c")

    def add_core(k, j):
        rows = rows_of(j)
        zp[k, rows] = (zpart[k, rows, my_cols].astype(F32) + zrc[k, rows].astype(F32)).astype(BF)
        s.work(0.15)

    def rs_group(k, part):
        def blk(j, h):
            return zp.at[k, half_rows(j, h)]

        recv = [zr.at[k, i] for i in range(6)]
        rest = Group(zr.at[k, pl.ds(2, 4)])
        order = (far, nxt, prev, z)
        copies = []
        for j in order:
            part(j)
            copies.append(share_core(k, j))
            yield []
        yield [copies[0]]
        add_core(k, far)
        c1 = s.send(blk(far, 0), recv[0], zs[1], "z+")
        c2 = s.send(blk(far, 1), recv[1], zs[3], "z-")
        yield [copies[1]]
        add_core(k, nxt)
        s.send(blk(nxt, 1), recv[2], zs[1], "z+", group=rest)
        yield [copies[2]]
        add_core(k, prev)
        s.send(blk(prev, 0), recv[3], zs[3], "z-", group=rest)
        yield [c1]
        add_into(blk(nxt, 0), recv[0])
        s.work(0.06)
        s.send(blk(nxt, 0), recv[4], zs[1], "z+", group=rest)
        yield [c2]
        add_into(blk(prev, 1), recv[1])
        s.work(0.06)
        s.send(blk(prev, 1), recv[5], zs[3], "z-", group=rest)
        yield [copies[3]]
        add_core(k, z)
        yield [rest]

    def rs_result(k):
        if k == 1:
            total = zp[k, rows_of(z)].astype(F32)
            for h in range(3):
                total = total + zd[h].astype(F32)
            return total

        def half(h, u, v):
            return zp[k, half_rows(z, h)].astype(F32) + zr[k, u].astype(F32) + zr[k, v].astype(F32)

        return jnp.concatenate([half(0, 3, 4), half(1, 2, 5)], axis=0)

    def chip_sum(k, values):
        stat_s[k] = jnp.broadcast_to(jnp.sum(values, axis=1, keepdims=True), (TOK, CH))
        return s.send(stat_s.at[k], stat_r.at[k], peer, "c")

    def chip_total(k):
        return (stat_s[k] + stat_r[k])[:, :1]

    def events(*dims):
        return [events(*dims[1:]) for _ in range(dims[0])] if dims else Event()

    dealt, full_w, issued = events(4), events(4, 2), events(4, 2)
    have_n1, have_n2, have_dy, have_dh = events(4), events(4), events(4), events(4)
    sent_n1, sent_n2, sent_dy, sent_dh = events(4)
    have_codes, have_halo, ffn, c_back, conv_back, sums = events(6)
    gain1 = vec_ref[pl.ds(0, 1), my_cols]
    gain2 = vec_ref[pl.ds(1, 1), my_cols]
    taps = [vec_ref[pl.ds(2 + k, 1), ch_cols] for k in range(3)]

    def deal(c):
        mine = pl.ds(pl.multiple_of(z * 16, 16), 16)
        slab = ws[c].at[y, x, mine, lanes[c]]
        group = Group(ws[c].at[y, x, pl.ds(0, 48), lanes[c]])
        for k in (1, 3, 2):
            s.send(packs[c].at[up(z, k), :, lanes[c]], slab, zs[k], *z_links[k], group=group)
        ws[c][y, x, mine, lanes[c]] = packs[c][z, :, lanes[c]]
        s.work(0.1)
        yield [group]
        s.done(dealt[c])

    def gather_side(c, h, side):
        yield [dealt[c]]
        yield from side()
        s.done(full_w[c][h])

    def first_norm():
        tok = tok_ref[...].astype(F32)
        copy = chip_sum(0, tok * tok)
        s.work(0.3)
        yield [copy]
        r1 = lax.rsqrt(chip_total(0) * (1.0 / D) + EPS)
        hat1[...] = tok_ref[...].astype(F32) * r1
        n1[rows_of(z), my_cols] = (hat1[...] * gain1).astype(BF)
        s.work(0.3)
        yield from ag_group(n1, have_n1, sent_n1)

    def halo():
        yield [
            s.send(tok_ref.at[pl.ds(TOK - 16, 16)], tail_raw, after, "x+", "y+"),
            s.send(code_ref, tail_code.at[z], after, "x+", "y+"),
        ]
        tok = tail_raw[...].astype(F32)
        tail_s[...] = jnp.broadcast_to(jnp.sum(tok * tok, axis=1, keepdims=True), (16, CH))
        yield [s.send(tail_s, tail_r, peer, "c")]
        scale = lax.rsqrt((tail_s[...] + tail_r[...])[:, :1] * (1.0 / D) + EPS)
        tail[z, :, my_cols] = (tail_raw[...].astype(F32) * scale * gain1).astype(BF)
        ref = tail.at[z, :, my_cols]
        group1, group2 = Group(tail.at[pl.ds(0, 3), :, my_cols]), Group(tail_code.at[pl.ds(0, 3)])
        for k in (1, 3, 2):
            s.send(ref, ref, zs[k], *z_links[k], group=group1)
            s.send(tail_code.at[z], tail_code.at[z], zs[k], *z_links[k], group=group2)
        s.work(0.1)
        yield [group1, group2]
        ref = tail.at[3, :, my_cols]
        yield [s.send(ref, ref, peer, "c")]
        n1[pl.ds(GT, 16), :] = tail[3]
        s.done(have_halo)

    def column(row):
        return jnp.transpose(jnp.broadcast_to(row, (CH, CH)))

    def share_codes():
        codes[z] = code_ref[...]
        group = Group(codes.at[pl.ds(0, 3)])
        for k in (1, 3, 2):
            s.send(code_ref, codes.at[z], zs[k], *z_links[k], group=group)
        yield [group]
        for j in range(4):
            cd[pl.ds(8 + j * TOK, TOK), :] = column(codes[j, 0:1])
        s.work(0.4)
        yield [have_halo]
        before_code = column(tail_code[3, 0:1])[TOK - 8 :]
        cd[pl.ds(0, 8), :] = jnp.where(group == 0, -1.0, before_code)
        s.work(0.1)
        s.done(have_codes)

    def share_dy():
        yield [sent_n1]
        dyf[rows_of(z), my_cols] = dy_ref[...]
        s.work(0.1)
        yield from ag_group(dyf, have_dy, sent_dy)

    def keep(k):
        code = cd[pl.ds(8, GT), :]
        return jnp.where((code >= 16.0) & (code == cd[pl.ds(8 - k, GT), :]), 1.0, 0.0)

    def ffn_block(j):
        rows = rows_of(j)
        ab = nn(n2[rows, :], w1[...].reshape(D, 2 * HP))
        a, b = ab[:, :HP], ab[:, HP:]
        sg = jax.nn.sigmoid(a)
        silu = a * sg
        uu[rows, :] = (silu * b).astype(BF)
        du = nn(dyf[rows, :], w2[...].reshape(D, HP))
        dab[rows, 0:HP] = (du * b * sg * (1.0 + a * (1.0 - sg))).astype(BF)
        dab[rows, HP : 2 * HP] = (du * silu).astype(BF)
        s.work(0.9)

    def y_part(j):
        rows = rows_of(j)
        zpart[0, rows, :] = nt(gat[rows, :], w0[...].reshape(D, 512)[:, 3 * CH :]).astype(BF)
        s.work(0.15)

    def n2_part(j):
        rows = rows_of(j)
        part = nt(dab[rows, :], w1[...].reshape(D, 2 * HP))
        zpart[1, rows, :] = part.astype(BF)
        small_out[pl.ds(1, 1), :] += jnp.sum(part * n2[rows, :].astype(F32), axis=0, keepdims=True)
        s.work(0.9)

    def u_part(j):
        rows = rows_of(j)
        zpart[2, rows, :] = nt(uu[rows, :], w2[...].reshape(D, HP)).astype(BF)
        s.work(0.35)

    def n1_part(j):
        rows = rows_of(j)
        part = nt(dbcv[rows, :], w0[...].reshape(D, 512)[:, : 3 * CH])
        zpart[3, rows, :] = part.astype(BF)
        small_out[pl.ds(0, 1), :] += jnp.sum(part * n1[rows, :].astype(F32), axis=0, keepdims=True)
        s.work(0.35)
        if j is z:
            s.done(sums)

    def main():
        yield have_n1 + full_w[0] + [have_halo]
        bcv[...] = nn(n1[...], w0[...].reshape(D, 512)[:, : 3 * CH])
        mixed = (bcv[:, 0:CH] * bcv[:, CH : 2 * CH]).astype(BF).astype(F32)
        mx[pl.ds(8, GT), :] = mixed[:GT]
        mx[pl.ds(0, 8), :] = mixed[GT + 8 :]
        s.work(1.0)
        yield [have_codes]
        zc[...] = (
            taps[0] * mx[pl.ds(8, GT), :] * keep(0)
            + taps[1] * mx[pl.ds(7, GT), :] * keep(1)
            + taps[2] * mx[pl.ds(6, GT), :] * keep(2)
        )
        gat[...] = (bcv[pl.ds(0, GT), 2 * CH : 3 * CH] * zc[...]).astype(BF)
        s.work(0.4)
        yield from rs_group(0, y_part)
        h2s[...] = tok_ref[...].astype(F32) + rs_result(0)
        h2 = h2s[...]
        copy = chip_sum(1, h2 * h2)
        s.work(0.4)
        yield [copy]
        r2 = lax.rsqrt(chip_total(1) * (1.0 / D) + EPS)
        hat2[...] = h2s[...] * r2
        n2[rows_of(z), my_cols] = (hat2[...] * gain2).astype(BF)
        s.work(0.3)
        s.add(1, ag_group(n2, have_n2, sent_n2))
        yield have_dy + full_w[1] + full_w[2] + full_w[3]
        last = Group(zd)
        small_out[...] = jnp.zeros((8, D), F32)
        for j, event, copy in ((z, have_n2[0], 0), (prev, have_n2[1], 3), (nxt, have_n2[2], 1), (far, have_n2[3], 2)):
            yield [event]
            ffn_block(j)
            if copy == 2:
                s.done(ffn)
            yield []
            n2_part(j)
            shared = share_core(1, j)
            s.add(1, send_block(j, copy, shared, last))
            yield []
        yield block_sent
        yield [last]
        dn2 = rs_result(1)
        e2 = dn2 * gain2
        copy = chip_sum(2, e2 * hat2[...])
        s.work(0.4)
        yield [copy]
        m2 = chip_total(2) * (1.0 / D)
        r2 = lax.rsqrt(chip_total(1) * (1.0 / D) + EPS)
        e2 = rs_result(1) * gain2
        dh2s[...] = dy_ref[...].astype(F32) + r2 * (e2 - hat2[...] * m2)
        dhb[rows_of(z), my_cols] = dh2s[...].astype(BF)
        s.work(0.4)
        yield from ag_group(dhb, have_dh, sent_dh)

        dg = nn(dhb[...], w0[...].reshape(D, 512)[:, 3 * CH :])
        dbcv[:, 2 * CH : 3 * CH] = (dg * zc[...]).astype(BF)
        dz = dg * bcv[pl.ds(0, GT), 2 * CH : 3 * CH]
        q0[...] = dz * keep(0)
        q1[pl.ds(0, GT), :] = dz * keep(1)
        q2[pl.ds(0, GT), :] = dz * keep(2)
        halo_s[0] = q1[pl.ds(0, 8), :]
        halo_s[1] = q2[pl.ds(0, 8), :]
        s.work(0.6)
        s.quiet = ()
        copy = s.send(halo_s, halo_r, before, "x-", "y-")
        s.done(c_back)
        small_out[pl.ds(2, 1), ch_cols] = jnp.sum(q0[...] * mx[pl.ds(8, GT), :], axis=0, keepdims=True)
        small_out[pl.ds(3, 1), ch_cols] = jnp.sum(q1[pl.ds(0, GT), :] * mx[pl.ds(7, GT), :], axis=0, keepdims=True)
        small_out[pl.ds(4, 1), ch_cols] = jnp.sum(q2[pl.ds(0, GT), :] * mx[pl.ds(6, GT), :], axis=0, keepdims=True)
        s.work(0.3)
        yield [copy]
        last = group == 15
        q1[pl.ds(GT, 8), :] = jnp.where(last, 0.0, halo_r[0])
        q2[pl.ds(GT, 8), :] = jnp.where(last, 0.0, halo_r[1])
        dm = taps[0] * q0[...] + taps[1] * q1[pl.ds(1, GT), :] + taps[2] * q2[pl.ds(2, GT), :]
        dbcv[:, 0:CH] = (dm * bcv[pl.ds(0, GT), CH : 2 * CH]).astype(BF)
        dbcv[:, CH : 2 * CH] = (dm * bcv[pl.ds(0, GT), 0:CH]).astype(BF)
        s.work(0.4)
        s.done(conv_back)
        yield []

        yield from rs_group(3, n1_part)
        dn1 = rs_result(3)
        e1 = dn1 * gain1
        copy = chip_sum(3, e1 * hat1[...])
        s.work(0.4)
        yield [copy]
        m1 = chip_total(3) * (1.0 / D)
        r1 = lax.rsqrt(chip_total(0) * (1.0 / D) + EPS)
        e1 = rs_result(3) * gain1
        tg_out[...] = dh2s[...] + r1 * (e1 - hat1[...] * m1)
        s.work(0.4)

    def small_sums():
        yield [sums]
        yield [s.send(small_out.at[:, peer_cols], redc.at[2], peer, "c")]
        half = small_out[:, my_cols] + redc[2]
        for k, (axis, i, peers) in enumerate((("x", x, xs), ("y", y, ys), ("z", z, zs))):
            red[k, i] = half
            group = Group(red.at[k, pl.ds(0, 3)])
            for j in (2, 1, 3):
                s.send(red.at[k, i], red.at[k, i], peers[j], *links[axis][j], group=group)
            yield [group]
            half = (red[k, 0] + red[k, 1]) + (red[k, 2] + red[k, 3])
            s.work(0.1)
        redc[core] = half
        yield [s.send(redc.at[core], redc.at[core], peer, "c")]
        for h in range(2):
            cols = pl.ds(h * HALF, HALF)
            small_sum[0:2, cols] = redc[h, 0:2] / vec_ref[0:2, cols]
            small_sum[2:8, cols] = redc[h, 2:8]

    block_sent = events(4)

    def send_block(j, k, shared, last):
        yield [shared]
        add_core(1, j)
        if k:
            s.send(zp.at[1, rows_of(j)], zd.at[k - 1], zs[k], *z_links[k], group=last)
        s.done(block_sent[k])

    def hidden_out():
        yield [sent_dh]
        yield from rs_group(2, u_part)
        mix_out[...] = (h2s[...] + rs_result(2)).astype(BF)
        s.work(0.2)

    def make_half(h):
        def step(i):
            ln = lanes[1 + h]
            g1[i, :, :, ln] = tn(n2[:, pl.ds(i * 256, 256)], dab[:, ln]).astype(BF).reshape(4, 64, HP)
            s.work(0.3)

        return step

    def make_g2(i):
        g2[i] = tn(dyf[:, pl.ds(i * 256, 256)], uu[...]).astype(BF).reshape(4, 64, HP)
        s.work(0.4)

    def make_g0(i):
        cols = pl.ds(i * 256, 256)
        g0[i, :, :, 2 * CH : 3 * CH] = tn(n1[pl.ds(0, GT), cols], dbcv[:, 2 * CH :]).astype(BF).reshape(4, 64, CH)
        g0[i, :, :, 3 * CH :] = tn(dhb[:, cols], gat[...]).astype(BF).reshape(4, 64, CH)
        s.work(0.2)

    def make_g4(i):
        cols = pl.ds(i * 256, 256)
        g0[i, :, :, 0 : 2 * CH] = tn(n1[pl.ds(0, GT), cols], dbcv[:, 0 : 2 * CH]).astype(BF).reshape(4, 64, 2 * CH)
        s.work(0.2)

    made, summed = events(5), events(5, 2)

    def make(c, after_event, step):
        yield [after_event]
        for i in range(4):
            step(i)
            yield []
        s.done(made[c])

    def reduce_side(c, h, side):
        yield [made[c]]
        yield from side()
        s.done(summed[c][h])

    def hand_back(c):
        yield summed[c]
        ln = grad_lanes[c]

        def rows(j):
            return gs[c].at[y, x, pl.ds(pl.multiple_of(j * 16, 16), 16), ln]

        group = Group(oas[c].at[pl.ds(0, 3), :, ln])
        for k in (1, 3, 2):
            s.send(rows(up(z, k)), oas[c].at[z, :, ln], zs[k], *z_links[k], group=group)
        oas[c][z, :, ln] = rows(z)[...]
        yield [group]
        outs[c][:, :, ln] = oas[c][:, :, ln]
        s.work(0.2)

    s.add(0, halo())
    s.add(0, deal(0))
    s.add(1, first_norm())
    for c in (1, 2, 3):
        s.add(1 + c, deal(c))
    s.add(4, share_codes())
    s.add(6, share_dy())
    for c in range(4):
        for h, side in enumerate(ag_plane(c, issued)):
            s.add(2 + c, gather_side(c, h, side))
    s.add(7, main())
    for c, rank, after_event, step in (
        (1, 3, ffn, make_half(0)),
        (2, 4, ffn, make_half(1)),
        (3, 5, ffn, make_g2),
        (0, 2, c_back, make_g0),
        (4, 1, conv_back, make_g4),
    ):
        s.add(7 + rank, make(c, after_event, step))
        for h, side in enumerate(rs_plane(c)):
            s.add(rank, reduce_side(c, h, side))
        s.add(rank, hand_back(c))
    s.add(13, hidden_out())
    s.add(2, small_sums())
    s.run()


def finish(mix, tg, small, p0, p1, p2, o_mix, o_tg, o_gain1, o_in, o_conv, o_out, o_gain2, o_gate, o_up, o_down):
    o_mix[...] = mix[...]
    o_tg[...] = tg[...]
    o_gain1[...] = small[0]
    o_gain2[...] = small[1]
    o_conv[...] = small[2:5]
    for j in range(R):
        for k in range(3):
            o_in[BVC[k], :, j * CH : (j + 1) * CH] = p0[j, :, k * CH : (k + 1) * CH].astype(F32)
        o_out[:, j * CH : (j + 1) * CH] = p0[j, :, 3 * CH :].astype(F32)
        cols = slice(j * HALF, (j + 1) * HALF)
        o_gate[:, cols] = p1[j, :, 0:HALF].astype(F32)
        o_up[:, cols] = p1[j, :, HP : HP + HALF].astype(F32)
        o_down[:, cols] = p2[j, :, 0:HALF].astype(F32)
    for t in range(2):
        tile = slice(2048 + t * CH, 2048 + (t + 1) * CH)
        o_gate[:, tile] = whole_tile(p1[2 * t, :, HALF:HP], p1[2 * t + 1, :, HALF:HP])
        o_up[:, tile] = whole_tile(p1[2 * t, :, HP + HALF :], p1[2 * t + 1, :, HP + HALF :])
        o_down[:, tile] = whole_tile(p2[2 * t, :, HALF:HP], p2[2 * t + 1, :, HALF:HP])


def block(tokens, dy, seg, valid, gain1, gain2, conv, in_weight, out_weight, gate, up, down):
    vmem = pl.BlockSpec(memory_space=pltpu.VMEM)
    loaded = [
        pltpu.VMEM((TOK, HALF), BF),
        pltpu.VMEM((TOK, HALF), BF),
        pltpu.VMEM((8, D), F32),
        pltpu.VMEM((TOK,), jnp.int32),
        pltpu.VMEM((TOK,), jnp.int32),
        pltpu.VMEM((D,), BF),
        pltpu.VMEM((D,), BF),
        pltpu.VMEM((3, D), BF),
        pltpu.VMEM((3, 16, HALF), BF),
        pltpu.VMEM((16, HALF), BF),
        pltpu.VMEM((16, R * HID), BF),
        pltpu.VMEM((16, R * HID), BF),
        pltpu.VMEM((16, R * HID), BF),
        pltpu.VMEM((8, CH), F32),
    ] + [pltpu.VMEM((R, 16, w), BF) for w in WIDTHS]
    plane = [pltpu.VMEM((4, 4, 64, w), BF) for w in WIDTHS]
    scratch = (
        loaded
        + plane
        + [pltpu.VMEM((4, 4, 64, w), BF) for w in WIDTHS]
        + [pltpu.VMEM((2, 6, 4, 16, w), BF) for w in (2 * CH, HP, HP, HP, 2 * CH)]
        + [pltpu.VMEM((2, 6, 16, w), BF) for w in (2 * CH, HP, HP, HP, 2 * CH)]
        + [pltpu.VMEM((4, 16, w), BF) for w in WIDTHS]
        + [
            pltpu.VMEM((4, 8, CH), F32),
            pltpu.VMEM((16, HALF), BF),
            pltpu.VMEM((4, 8, CH), F32),
            pltpu.VMEM((16, CH), F32),
            pltpu.VMEM((16, CH), F32),
            pltpu.VMEM((4, 16, D), BF),
            pltpu.VMEM((GT + 16, D), BF),
            pltpu.VMEM((GT, D), BF),
            pltpu.VMEM((GT, D), BF),
            pltpu.VMEM((GT, D), BF),
            pltpu.VMEM((4, GT, D), BF),
            pltpu.VMEM((4, GT, HALF), BF),
            pltpu.VMEM((4, GT, HALF), BF),
            pltpu.VMEM((4, 6, TOK // 2, HALF), BF),
            pltpu.VMEM((3, TOK, HALF), BF),
            pltpu.VMEM((4, TOK, CH), F32),
            pltpu.VMEM((4, TOK, CH), F32),
            pltpu.VMEM((TOK, HALF), F32),
            pltpu.VMEM((TOK, HALF), F32),
            pltpu.VMEM((TOK, HALF), F32),
            pltpu.VMEM((TOK, HALF), F32),
            pltpu.VMEM((GT + 16, 3 * CH), F32),
            pltpu.VMEM((GT, 3 * CH), BF),
            pltpu.VMEM((GT, CH), F32),
            pltpu.VMEM((GT, CH), BF),
            pltpu.VMEM((GT + 8, CH), F32),
            pltpu.VMEM((GT + 8, CH), F32),
            pltpu.VMEM((GT, CH), F32),
            pltpu.VMEM((GT + 8, CH), F32),
            pltpu.VMEM((GT + 8, CH), F32),
            pltpu.VMEM((2, 8, CH), F32),
            pltpu.VMEM((2, 8, CH), F32),
            pltpu.VMEM((GT, HP), BF),
            pltpu.VMEM((GT, 2 * HP), BF),
            pltpu.VMEM((3, R, 8, HALF), F32),
            pltpu.VMEM((3, 8, HALF), F32),
            pltpu.VMEM((8, D), F32),
            pltpu.SemaphoreType.DMA((12,)),
            pltpu.SemaphoreType.DMA((SENDS,)),
            pltpu.SemaphoreType.DMA((RECEIVES,)),
        ]
    )
    packed = pl.pallas_call(
        kernel,
        out_shape=[
            jax.ShapeDtypeStruct((TOK, HALF), BF),
            jax.ShapeDtypeStruct((TOK, HALF), F32),
            jax.ShapeDtypeStruct((8, D), F32),
        ]
        + [jax.ShapeDtypeStruct((R, 16, w), BF) for w in WIDTHS],
        in_specs=[pl.BlockSpec(memory_space=pl.ANY)] * 12,
        out_specs=[vmem] * 6,
        scratch_shapes=scratch,
        compiler_params=pltpu.CompilerParams(
            collective_id=0, has_side_effects=True, vmem_limit_bytes=58 * 1024 * 1024
        ),
    )(tokens, dy, seg, valid, gain1, gain2, conv, in_weight, out_weight, gate, up, down)
    return pl.pallas_call(
        finish,
        out_shape=[
            jax.ShapeDtypeStruct((TOK, HALF), BF),
            jax.ShapeDtypeStruct((TOK, HALF), F32),
            jax.ShapeDtypeStruct((D,), F32),
            jax.ShapeDtypeStruct((3, 16, HALF), F32),
            jax.ShapeDtypeStruct((3, D), F32),
            jax.ShapeDtypeStruct((16, HALF), F32),
            jax.ShapeDtypeStruct((D,), F32),
            jax.ShapeDtypeStruct((16, R * HID), F32),
            jax.ShapeDtypeStruct((16, R * HID), F32),
            jax.ShapeDtypeStruct((16, R * HID), F32),
        ],
        in_specs=[vmem] * 6,
        out_specs=[vmem] * 10,
    )(*packed)


def local(
    tokens,
    segment_ids,
    valid_mask,
    norm1_gain,
    in_weight,
    conv_weight,
    out_weight,
    norm2_gain,
    gate_weight,
    up_weight,
    down_weight,
    out_cotangent,
):
    outs = list(
        block(
            tokens,
            out_cotangent,
            segment_ids,
            valid_mask,
            norm1_gain,
            norm2_gain,
            conv_weight,
            in_weight,
            out_weight.T,
            gate_weight,
            up_weight,
            down_weight.T,
        )
    )
    outs[5], outs[9] = outs[5].T, outs[9].T
    return tuple(outs)


def solution(mesh):
    placed = (
        P("dp", "tensor"),
        P("dp"),
        P("dp"),
        P(),
        P(None, "dp", "tensor"),
        P(),
        P("tensor", "dp"),
        P(),
        P("dp", "tensor"),
        P("dp", "tensor"),
        P("tensor", "dp"),
        P("dp", "tensor"),
    )
    return jax.shard_map(
        local,
        mesh=mesh,
        in_specs=placed,
        out_specs=(
            P("dp", "tensor"),
            P("dp", "tensor"),
            P(),
            P(None, "dp", "tensor"),
            P(),
            P("tensor", "dp"),
            P(),
            P("dp", "tensor"),
            P("dp", "tensor"),
            P("tensor", "dp"),
        ),
        check_vma=False,
    )
```

```python
import jax
import jax.numpy as jnp
from jax import lax
from jax.experimental import pallas as pl
from jax.experimental.pallas import tpu as pltpu
from jax.sharding import PartitionSpec as P

D = 1024
EPS = 1e-05
R = 4
BF = jnp.bfloat16
F32 = jnp.float32
TOK = 128
GT = 512
HALF = 512
CH = 128
HID = 576
HP = 640
GW = 1152
WIDTHS = (512, GW, HP)
BVC = (0, 2, 1)
SENDS = 48
RECEIVES = 200


def nn(a, b):
    return lax.dot_general(a, b, (((1,), (0,)), ((), ())), preferred_element_type=F32)


def nt(a, b):
    return lax.dot_general(a, b, (((1,), (1,)), ((), ())), preferred_element_type=F32)


def tn(a, b):
    return lax.dot_general(a, b, (((0,), (0,)), ((), ())), preferred_element_type=F32)


def add_into(dst, *others):
    total = dst[...].astype(F32)
    for other in others:
        total = total + other[...].astype(F32)
    dst[...] = total.astype(dst.dtype)


class Event:
    def __init__(self):
        self.time = float("inf")


class Copy(Event):
    def __init__(self, copy, time, end):
        self.copy, self.time, self.end, self.waited = copy, time, end, False

    def arrived(self):
        self.copy.wait_recv()


class Group(Event):
    def __init__(self, total):
        self.total, self.sem, self.time, self.waited = total, None, 0.0, False

    def arrived(self):
        send_sem, recv_sem, device = self.remake
        pltpu.make_async_remote_copy(
            src_ref=self.total,
            dst_ref=self.total,
            send_sem=send_sem,
            recv_sem=recv_sem,
            device_id=device,
            device_id_type=pl.DeviceIdType.MESH,
        ).wait_recv()


class Room:
    def __init__(self, schedule, link, slack):
        self.schedule, self.link, self.slack = schedule, link, slack

    @property
    def time(self):
        if self.link in self.schedule.quiet:
            return float("inf")
        return self.schedule.free.get(self.link, 0.0) - self.slack


class Schedule:
    RATE = 33.0e3
    CORE_RATE = 700e3
    LATENCY = 2.6
    FAR_LATENCY = 3.6
    CORE_LATENCY = 1.7
    ISSUE = 0.05

    def __init__(self, send_sems, recv_sems):
        self.send_sems, self.recv_sems = send_sems, recv_sems
        self.pool, self.received, self.quiet = [None] * SENDS, 0, ()
        self.tasks, self.free, self.now = [], {}, 3.7

    def send(self, src, dst, device, *links, group=None):
        k = min(range(SENDS), key=lambda i: -1.0 if self.pool[i] is None else self.pool[i].end)
        if self.pool[k] is not None:
            self.pool[k].copy.wait_send()
            self.now = max(self.now, self.pool[k].end)
        sem = self.received if group is None or group.sem is None else group.sem
        if sem == self.received:
            self.received += 1
            assert sem < RECEIVES
        copy = pltpu.make_async_remote_copy(
            src_ref=src,
            dst_ref=dst,
            send_sem=self.send_sems.at[k],
            recv_sem=self.recv_sems.at[sem],
            device_id=device,
            device_id_type=pl.DeviceIdType.MESH,
        )
        copy.start()
        self.now += self.ISSUE
        size = jnp.dtype(src.dtype).itemsize
        for n in src.shape:
            size *= n
        end = self.now
        for link in links:
            begin = max(self.now, self.free.get(link, 0.0))
            self.free[link] = begin + size / (self.CORE_RATE if link == "c" else self.RATE)
            end = max(end, self.free[link])
        latency = self.CORE_LATENCY if "c" in links else self.LATENCY if len(links) == 1 else self.FAR_LATENCY
        self.pool[k] = Copy(copy, end + latency, end)
        if group is None:
            return self.pool[k]
        group.sem, group.time = sem, max(group.time, end + latency)
        group.remake = (self.send_sems.at[k], self.recv_sems.at[sem], device)
        return group

    def room(self, link, slack=12.0):
        return [Room(self, link, slack)]

    def work(self, us):
        self.now += us

    def done(self, event):
        event.time = self.now

    def add(self, rank, task):
        self.tasks.append([rank, task, ()])

    def run(self):
        while self.tasks:
            times = [max([0.0] + [e.time for e in t[2]]) for t in self.tasks]
            ready = [i for i, r in enumerate(times) if r <= self.now]
            if ready:
                i = min(ready, key=lambda i: (self.tasks[i][0], times[i]))
            else:
                i = min(range(len(times)), key=lambda i: (times[i], self.tasks[i][0]))
                self.now = times[i]
            task = self.tasks[i]
            for event in task[2]:
                if isinstance(event, (Copy, Group)) and not event.waited:
                    event.arrived()
                    event.waited = True
                    self.now += 0.03
            try:
                task[2] = tuple(next(task[1]))
            except StopIteration:
                self.tasks.pop(i)
        for last in self.pool:
            if last is not None:
                last.copy.wait_send()


def ring_ag(s, axis, i, plus, minus, blk, two, issued=None):
    rest = Group(two)
    up, down = axis + "+", axis + "-"
    prev, nxt = (i + R - 1) % R, (i + 1) % R
    yield s.room(up)
    c1 = s.send(blk(i, 0), blk(i, 0), plus, up)
    yield s.room(down)
    c2 = s.send(blk(i, 1), blk(i, 1), minus, down)
    yield s.room(up)
    s.send(blk(i, 1), blk(i, 1), plus, up, group=rest)
    yield s.room(down)
    s.send(blk(i, 0), blk(i, 0), minus, down, group=rest)
    yield [c1]
    s.send(blk(prev, 0), blk(prev, 0), plus, up, group=rest)
    yield [c2]
    s.send(blk(nxt, 1), blk(nxt, 1), minus, down, group=rest)
    if issued is not None:
        s.done(issued)
    yield [rest]


def ring_rs(s, axis, i, plus, minus, blk, bufs, us):
    recv, rest = [bufs.at[k] for k in range(6)], Group(bufs.at[pl.ds(2, 4)])
    up, down = axis + "+", axis + "-"
    prev, nxt, far = (i + R - 1) % R, (i + 1) % R, (i + 2) % R
    yield s.room(up)
    c1 = s.send(blk(far, 0), recv[0], plus, up)
    yield s.room(down)
    c2 = s.send(blk(far, 1), recv[1], minus, down)
    yield s.room(up)
    s.send(blk(nxt, 1), recv[2], plus, up, group=rest)
    yield s.room(down)
    s.send(blk(prev, 0), recv[3], minus, down, group=rest)
    yield [c1]
    add_into(blk(nxt, 0), recv[0])
    s.work(us)
    s.send(blk(nxt, 0), recv[4], plus, up, group=rest)
    yield [c2]
    add_into(blk(prev, 1), recv[1])
    s.work(us)
    s.send(blk(prev, 1), recv[5], minus, down, group=rest)
    yield [rest]


def low_lanes():
    return lax.broadcasted_iota(jnp.int32, (16, CH), 1) < CH // 2


def half_tile(tile, odd):
    return jnp.where(low_lanes(), pltpu.roll(tile, CH // 2, 1) if odd else tile, 0.0)


def whole_tile(even, odd):
    return jnp.where(low_lanes(), even.astype(F32), pltpu.roll(odd.astype(F32), CH // 2, 1))


def kernel(
    tok_hbm,
    dy_hbm,
    seg_hbm,
    valid_hbm,
    gain1_hbm,
    gain2_hbm,
    conv_hbm,
    in_hbm,
    out_hbm,
    gate_hbm,
    up_hbm,
    down_hbm,
    mix_out,
    tg_out,
    small_sum,
    g0_out,
    g1_out,
    g2_out,
    tok_ref,
    dy_ref,
    vec_ref,
    seg_ref,
    valid_ref,
    gain1_ref,
    gain2_ref,
    conv_ref,
    in_ref,
    out_ref,
    gate_ref,
    up_ref,
    down_ref,
    code_ref,
    pack0,
    pack1,
    pack2,
    w0,
    w1,
    w2,
    g0,
    g1,
    g2,
    ra0,
    ra1,
    ra2,
    ra3,
    ra4,
    rb0,
    rb1,
    rb2,
    rb3,
    rb4,
    oa0,
    oa1,
    oa2,
    codes,
    tail_raw,
    tail_code,
    tail_s,
    tail_r,
    tail,
    n1,
    dyf,
    n2,
    dhb,
    zpart,
    zrc,
    zp,
    zr,
    zd,
    stat_s,
    stat_r,
    hat1,
    hat2,
    h2s,
    dh2s,
    bcv,
    dbcv,
    zc,
    gat,
    mx,
    cd,
    q0,
    q1,
    q2,
    halo_s,
    halo_r,
    uu,
    dab,
    red,
    redc,
    small_out,
    load_sems,
    send_sems,
    recv_sems,
):
    dp = lax.axis_index("dp")
    core = lax.axis_index("tensor")
    y, x, z = dp // 16, (dp // 4) % 4, dp % 4
    group = dp // 4

    def dev(yy, xx, zz):
        return (yy * 16 + xx * 4 + zz, core)

    def up(v, k=1):
        return (v + k) % R

    peer = (dp, 1 - core)
    xs = [None] + [dev(y, up(x, k), z) for k in (1, 2, 3)]
    ys = [None] + [dev(up(y, k), x, z) for k in (1, 2, 3)]
    zs = [None] + [dev(y, x, up(z, k)) for k in (1, 2, 3)]
    after = ((dp + 4) % 64, core)
    before = ((dp + 60) % 64, core)

    barrier = pltpu.get_barrier_semaphore()
    others = [peer, after, before] + xs[1:] + ys[1:] + zs[1:]
    for other in others:
        pl.semaphore_signal(barrier, inc=1, device_id=other, device_id_type=pl.DeviceIdType.MESH)
    loads = [
        pltpu.make_async_copy(src, dst, load_sems.at[k])
        for k, (src, dst) in enumerate(
            (
                (seg_hbm, seg_ref),
                (valid_hbm, valid_ref),
                (gain1_hbm, gain1_ref),
                (gain2_hbm, gain2_ref),
                (conv_hbm, conv_ref),
                (in_hbm, in_ref),
                (out_hbm, out_ref),
                (tok_hbm, tok_ref),
                (gate_hbm, gate_ref),
                (up_hbm, up_ref),
                (down_hbm, down_ref),
                (dy_hbm, dy_ref),
            )
        )
    ]
    for load in loads:
        load.start()
    for load in loads:
        load.wait()
    vec_ref[0] = gain1_ref[...].astype(F32)
    vec_ref[1] = gain2_ref[...].astype(F32)
    vec_ref[2:5] = conv_ref[...].astype(F32)
    code_ref[...] = jnp.broadcast_to((seg_ref[...] + 16 * valid_ref[...]).astype(F32)[None], (8, CH))
    for j in range(R):
        for k in range(3):
            pack0[j, :, k * CH : (k + 1) * CH] = in_ref[BVC[k], :, j * CH : (j + 1) * CH]
        pack0[j, :, 3 * CH :] = out_ref[:, j * CH : (j + 1) * CH]
        cols, tile = slice(j * HALF, (j + 1) * HALF), slice(2048 + j // 2 * CH, 2048 + (j // 2 + 1) * CH)
        pack1[j, :, 0:HALF] = gate_ref[:, cols]
        pack1[j, :, HALF : 2 * HALF] = up_ref[:, cols]
        gate_half, up_half, down_half = [
            half_tile(ref[:, tile].astype(F32), j % 2) for ref in (gate_ref, up_ref, down_ref)
        ]
        pack1[j, :, 2 * HALF :] = (gate_half + pltpu.roll(up_half, CH // 2, 1)).astype(BF)
        pack2[j, :, 0:HALF] = down_ref[:, cols]
        pack2[j, :, HALF:HP] = down_half.astype(BF)
    pl.semaphore_wait(barrier, len(others))

    s = Schedule(send_sems, recv_sems)
    packs, ws, gs = (pack0, pack1, pack1, pack2), (w0, w1, w1, w2), (g0, g1, g1, g2, g0)
    ras, rbs, oas = (ra0, ra1, ra2, ra3, ra4), (rb0, rb1, rb2, rb3, rb4), (oa0, oa1, oa1, oa2, oa0)
    outs = (g0_out, g1_out, g1_out, g2_out, g0_out)
    lanes = (pl.ds(0, 512), pl.ds(0, 512), pl.ds(512, HP), pl.ds(0, HP))
    grad_lanes = (pl.ds(2 * CH, 2 * CH),) + lanes[1:] + (pl.ds(0, 2 * CH),)
    my_cols = pl.ds(pl.multiple_of(core * HALF, HALF), HALF)
    peer_cols = pl.ds(pl.multiple_of((1 - core) * HALF, HALF), HALF)
    ch_cols = pl.ds(pl.multiple_of(core * HALF + z * CH, CH), CH)
    z_links = (None, ("z+",), ("z+", "z-"), ("z-",))
    links = {a: (None, (a + "+",), (a + "+", a + "-"), (a + "-",)) for a in "xyz"}

    def rows_of(j, count=TOK):
        return pl.ds(pl.multiple_of(j * count, count), count)

    def ag_plane(c, issued):
        w, ln = ws[c], lanes[c]

        def part(base, h):
            return pl.ds(base + 16 * h, 16)

        def side_a():
            yield from ring_ag(s, "x", x, xs[1], xs[3], lambda j, h: w.at[y, j, part(0, h), ln], w.at[y, x, :, ln])
            if c:
                yield [issued[c - 1][0]]
            yield from ring_ag(s, "y", y, ys[1], ys[3], lambda j, h: w.at[j, :, part(0, h), ln], w.at[y, :, :, ln], issued[c][0])

        def side_b():
            yield from ring_ag(s, "y", y, ys[1], ys[3], lambda j, h: w.at[j, x, part(32, h), ln], w.at[y, x, :, ln])
            if c:
                yield [issued[c - 1][1]]
            yield from ring_ag(s, "x", x, xs[1], xs[3], lambda j, h: w.at[:, j, part(32, h), ln], w.at[:, x, :, ln], issued[c][1])

        return side_a, side_b

    def rs_plane(c):
        g, ra, rb, ln, us = gs[c], ras[c], rbs[c], grad_lanes[c], 0.12

        def part(base, h):
            return pl.ds(base + 16 * h, 16)

        def side_a():
            yield from ring_rs(
                s, "y", y, ys[1], ys[3], lambda j, h: g.at[j, :, part(0, h), ln], ra.at[0], us
            )
            for h, (u, v) in ((0, (3, 4)), (1, (2, 5))):
                add_into(g.at[y, :, part(0, h), ln], ra.at[0, u], ra.at[0, v])
                s.work(1.5 * us)
            yield from ring_rs(
                s, "x", x, xs[1], xs[3], lambda j, h: g.at[y, j, part(0, h), ln], rb.at[0], us / 3
            )
            for h, (u, v) in ((0, (3, 4)), (1, (2, 5))):
                add_into(g.at[y, x, part(0, h), ln], rb.at[0, u], rb.at[0, v])
                s.work(0.5 * us)

        def side_b():
            yield from ring_rs(
                s, "x", x, xs[1], xs[3], lambda j, h: g.at[:, j, part(32, h), ln], ra.at[1], us
            )
            for h, (u, v) in ((0, (3, 4)), (1, (2, 5))):
                add_into(g.at[:, x, part(32, h), ln], ra.at[1, u], ra.at[1, v])
                s.work(1.5 * us)
            yield from ring_rs(
                s, "y", y, ys[1], ys[3], lambda j, h: g.at[j, x, part(32, h), ln], rb.at[1], us / 3
            )
            for h, (u, v) in ((0, (3, 4)), (1, (2, 5))):
                add_into(g.at[y, x, part(32, h), ln], rb.at[1, u], rb.at[1, v])
                s.work(0.5 * us)

        return side_a, side_b

    prev, nxt, far = up(z, 3), up(z), up(z, 2)

    def ag_group(n, have, issued):
        def both(j, h, device, link, group=None):
            ref = n.at[half_rows(j, h), my_cols]
            return s.send(ref, ref, device, link, group=group)

        to_core = [Group(n.at[rows_of(j), my_cols]) for j in (z, prev, nxt, far)]

        def core_too(i, j, h):
            both(j, h, peer, "c", to_core[i])

        c1 = both(z, 0, zs[1], "z+")
        c2 = both(z, 1, zs[3], "z-")
        c3 = both(z, 1, zs[1], "z+")
        c4 = both(z, 0, zs[3], "z-")
        core_too(0, z, 0)
        core_too(0, z, 1)
        yield [to_core[0]]
        s.done(have[0])
        yield [c1]
        c5 = both(prev, 0, zs[1], "z+")
        core_too(1, prev, 0)
        yield [c2]
        c6 = both(nxt, 1, zs[3], "z-")
        s.done(issued)
        core_too(2, nxt, 1)
        yield [c3]
        core_too(1, prev, 1)
        yield [c4]
        core_too(2, nxt, 0)
        if n is dhb:
            s.quiet = ("x-", "y-")
        yield [to_core[1]]
        s.done(have[1])
        yield [to_core[2]]
        s.done(have[2])
        yield [c5]
        core_too(3, far, 0)
        yield [c6]
        core_too(3, far, 1)
        yield [to_core[3]]
        s.done(have[3])

    def half_rows(j, h):
        return pl.ds(pl.multiple_of(j * TOK + h * (TOK // 2), TOK // 2), TOK // 2)

    def share_core(k, j):
        return s.send(zpart.at[k, rows_of(j), peer_cols], zrc.at[k, rows_of(j)], peer, "c")

    def add_core(k, j):
        rows = rows_of(j)
        zp[k, rows] = (zpart[k, rows, my_cols].astype(F32) + zrc[k, rows].astype(F32)).astype(BF)
        s.work(0.15)

    def rs_group(k, part):
        def blk(j, h):
            return zp.at[k, half_rows(j, h)]

        recv = [zr.at[k, i] for i in range(6)]
        rest = Group(zr.at[k, pl.ds(2, 4)])
        order = (far, nxt, prev, z)
        copies = []
        for j in order:
            part(j)
            copies.append(share_core(k, j))
            yield []
        yield [copies[0]]
        add_core(k, far)
        c1 = s.send(blk(far, 0), recv[0], zs[1], "z+")
        c2 = s.send(blk(far, 1), recv[1], zs[3], "z-")
        yield [copies[1]]
        add_core(k, nxt)
        s.send(blk(nxt, 1), recv[2], zs[1], "z+", group=rest)
        yield [copies[2]]
        add_core(k, prev)
        s.send(blk(prev, 0), recv[3], zs[3], "z-", group=rest)
        yield [c1]
        add_into(blk(nxt, 0), recv[0])
        s.work(0.06)
        s.send(blk(nxt, 0), recv[4], zs[1], "z+", group=rest)
        yield [c2]
        add_into(blk(prev, 1), recv[1])
        s.work(0.06)
        s.send(blk(prev, 1), recv[5], zs[3], "z-", group=rest)
        yield [copies[3]]
        add_core(k, z)
        yield [rest]

    def rs_result(k):
        if k == 1:
            total = zp[k, rows_of(z)].astype(F32)
            for h in range(3):
                total = total + zd[h].astype(F32)
            return total

        def half(h, u, v):
            return zp[k, half_rows(z, h)].astype(F32) + zr[k, u].astype(F32) + zr[k, v].astype(F32)

        return jnp.concatenate([half(0, 3, 4), half(1, 2, 5)], axis=0)

    def chip_sum(k, values):
        stat_s[k] = jnp.broadcast_to(jnp.sum(values, axis=1, keepdims=True), (TOK, CH))
        return s.send(stat_s.at[k], stat_r.at[k], peer, "c")

    def chip_total(k):
        return (stat_s[k] + stat_r[k])[:, :1]

    def events(*dims):
        return [events(*dims[1:]) for _ in range(dims[0])] if dims else Event()

    dealt, full_w, issued = events(4), events(4, 2), events(4, 2)
    have_n1, have_n2, have_dy, have_dh = events(4), events(4), events(4), events(4)
    sent_n1, sent_n2, sent_dy, sent_dh = events(4)
    have_codes, have_halo, ffn, c_back, conv_back, sums = events(6)
    gain1 = vec_ref[pl.ds(0, 1), my_cols]
    gain2 = vec_ref[pl.ds(1, 1), my_cols]
    taps = [vec_ref[pl.ds(2 + k, 1), ch_cols] for k in range(3)]

    def deal(c):
        mine = pl.ds(pl.multiple_of(z * 16, 16), 16)
        slab = ws[c].at[y, x, mine, lanes[c]]
        group = Group(ws[c].at[y, x, pl.ds(0, 48), lanes[c]])
        for k in (1, 3, 2):
            s.send(packs[c].at[up(z, k), :, lanes[c]], slab, zs[k], *z_links[k], group=group)
        ws[c][y, x, mine, lanes[c]] = packs[c][z, :, lanes[c]]
        s.work(0.1)
        yield [group]
        s.done(dealt[c])

    def gather_side(c, h, side):
        yield [dealt[c]]
        yield from side()
        s.done(full_w[c][h])

    def first_norm():
        tok = tok_ref[...].astype(F32)
        copy = chip_sum(0, tok * tok)
        s.work(0.3)
        yield [copy]
        r1 = lax.rsqrt(chip_total(0) * (1.0 / D) + EPS)
        hat1[...] = tok_ref[...].astype(F32) * r1
        n1[rows_of(z), my_cols] = (hat1[...] * gain1).astype(BF)
        s.work(0.3)
        yield from ag_group(n1, have_n1, sent_n1)

    def halo():
        yield [
            s.send(tok_ref.at[pl.ds(TOK - 16, 16)], tail_raw, after, "x+", "y+"),
            s.send(code_ref, tail_code.at[z], after, "x+", "y+"),
        ]
        tok = tail_raw[...].astype(F32)
        tail_s[...] = jnp.broadcast_to(jnp.sum(tok * tok, axis=1, keepdims=True), (16, CH))
        yield [s.send(tail_s, tail_r, peer, "c")]
        scale = lax.rsqrt((tail_s[...] + tail_r[...])[:, :1] * (1.0 / D) + EPS)
        tail[z, :, my_cols] = (tail_raw[...].astype(F32) * scale * gain1).astype(BF)
        ref = tail.at[z, :, my_cols]
        group1, group2 = Group(tail.at[pl.ds(0, 3), :, my_cols]), Group(tail_code.at[pl.ds(0, 3)])
        for k in (1, 3, 2):
            s.send(ref, ref, zs[k], *z_links[k], group=group1)
            s.send(tail_code.at[z], tail_code.at[z], zs[k], *z_links[k], group=group2)
        s.work(0.1)
        yield [group1, group2]
        ref = tail.at[3, :, my_cols]
        yield [s.send(ref, ref, peer, "c")]
        n1[pl.ds(GT, 16), :] = tail[3]
        s.done(have_halo)

    def column(row):
        return jnp.transpose(jnp.broadcast_to(row, (CH, CH)))

    def share_codes():
        codes[z] = code_ref[...]
        group = Group(codes.at[pl.ds(0, 3)])
        for k in (1, 3, 2):
            s.send(code_ref, codes.at[z], zs[k], *z_links[k], group=group)
        yield [group]
        for j in range(4):
            cd[pl.ds(8 + j * TOK, TOK), :] = column(codes[j, 0:1])
        s.work(0.4)
        yield [have_halo]
        before_code = column(tail_code[3, 0:1])[TOK - 8 :]
        cd[pl.ds(0, 8), :] = jnp.where(group == 0, -1.0, before_code)
        s.work(0.1)
        s.done(have_codes)

    def share_dy():
        yield [sent_n1]
        dyf[rows_of(z), my_cols] = dy_ref[...]
        s.work(0.1)
        yield from ag_group(dyf, have_dy, sent_dy)

    def keep(k):
        code = cd[pl.ds(8, GT), :]
        return jnp.where((code >= 16.0) & (code == cd[pl.ds(8 - k, GT), :]), 1.0, 0.0)

    def ffn_block(j):
        rows = rows_of(j)
        ab = nn(n2[rows, :], w1[...].reshape(D, GW))
        du = nn(dyf[rows, :], w2[...].reshape(D, HP))

        def act(a, b, du):
            sg = jax.nn.sigmoid(a)
            silu = a * sg
            return silu * b, du * b * sg * (1.0 + a * (1.0 - sg)), du * silu

        u, da, db = act(ab[:, :HALF], ab[:, HALF : 2 * HALF], du[:, :HALF])
        uu[rows, 0:HALF] = u.astype(BF)
        dab[rows, 0:HALF] = da.astype(BF)
        dab[rows, HALF : 2 * HALF] = db.astype(BF)
        tile = ab[:, 2 * HALF :]
        low = lax.broadcasted_iota(jnp.int32, (TOK, CH), 1) < CH // 2
        u, da, db = [jnp.where(low, v, 0.0) for v in act(tile, pltpu.roll(tile, CH // 2, 1), du[:, HALF:])]
        uu[rows, HALF:HP] = u.astype(BF)
        dab[rows, 2 * HALF :] = (da + pltpu.roll(db, CH // 2, 1)).astype(BF)
        s.work(0.9)

    def y_part(j):
        rows = rows_of(j)
        zpart[0, rows, :] = nt(gat[rows, :], w0[...].reshape(D, 512)[:, 3 * CH :]).astype(BF)
        s.work(0.15)

    def n2_part(j):
        rows = rows_of(j)
        part = nt(dab[rows, :], w1[...].reshape(D, GW))
        zpart[1, rows, :] = part.astype(BF)
        small_out[pl.ds(1, 1), :] += jnp.sum(part * n2[rows, :].astype(F32), axis=0, keepdims=True)
        s.work(0.9)

    def u_part(j):
        rows = rows_of(j)
        zpart[2, rows, :] = nt(uu[rows, :], w2[...].reshape(D, HP)).astype(BF)
        s.work(0.35)

    def n1_part(j):
        rows = rows_of(j)
        part = nt(dbcv[rows, :], w0[...].reshape(D, 512)[:, : 3 * CH])
        zpart[3, rows, :] = part.astype(BF)
        small_out[pl.ds(0, 1), :] += jnp.sum(part * n1[rows, :].astype(F32), axis=0, keepdims=True)
        s.work(0.35)
        if j is z:
            s.done(sums)

    def main():
        yield have_n1 + full_w[0] + [have_halo]
        bcv[...] = nn(n1[...], w0[...].reshape(D, 512)[:, : 3 * CH])
        mixed = (bcv[:, 0:CH] * bcv[:, CH : 2 * CH]).astype(BF).astype(F32)
        mx[pl.ds(8, GT), :] = mixed[:GT]
        mx[pl.ds(0, 8), :] = mixed[GT + 8 :]
        s.work(1.0)
        yield [have_codes]
        zc[...] = (
            taps[0] * mx[pl.ds(8, GT), :] * keep(0)
            + taps[1] * mx[pl.ds(7, GT), :] * keep(1)
            + taps[2] * mx[pl.ds(6, GT), :] * keep(2)
        )
        gat[...] = (bcv[pl.ds(0, GT), 2 * CH : 3 * CH] * zc[...]).astype(BF)
        s.work(0.4)
        yield from rs_group(0, y_part)
        h2s[...] = tok_ref[...].astype(F32) + rs_result(0)
        h2 = h2s[...]
        copy = chip_sum(1, h2 * h2)
        s.work(0.4)
        yield [copy]
        r2 = lax.rsqrt(chip_total(1) * (1.0 / D) + EPS)
        hat2[...] = h2s[...] * r2
        n2[rows_of(z), my_cols] = (hat2[...] * gain2).astype(BF)
        s.work(0.3)
        s.add(1, ag_group(n2, have_n2, sent_n2))
        yield have_dy + full_w[1] + full_w[2] + full_w[3]
        last = Group(zd)
        small_out[...] = jnp.zeros((8, D), F32)
        for j, event, copy in ((z, have_n2[0], 0), (prev, have_n2[1], 3), (nxt, have_n2[2], 1), (far, have_n2[3], 2)):
            yield [event]
            ffn_block(j)
            if copy == 2:
                s.done(ffn)
            yield []
            n2_part(j)
            shared = share_core(1, j)
            s.add(1, send_block(j, copy, shared, last))
            yield []
        yield block_sent
        yield [last]
        dn2 = rs_result(1)
        e2 = dn2 * gain2
        copy = chip_sum(2, e2 * hat2[...])
        s.work(0.4)
        yield [copy]
        m2 = chip_total(2) * (1.0 / D)
        r2 = lax.rsqrt(chip_total(1) * (1.0 / D) + EPS)
        e2 = rs_result(1) * gain2
        dh2s[...] = dy_ref[...].astype(F32) + r2 * (e2 - hat2[...] * m2)
        dhb[rows_of(z), my_cols] = dh2s[...].astype(BF)
        s.work(0.4)
        yield from ag_group(dhb, have_dh, sent_dh)

        dg = nn(dhb[...], w0[...].reshape(D, 512)[:, 3 * CH :])
        dbcv[:, 2 * CH : 3 * CH] = (dg * zc[...]).astype(BF)
        dz = dg * bcv[pl.ds(0, GT), 2 * CH : 3 * CH]
        q0[...] = dz * keep(0)
        q1[pl.ds(0, GT), :] = dz * keep(1)
        q2[pl.ds(0, GT), :] = dz * keep(2)
        halo_s[0] = q1[pl.ds(0, 8), :]
        halo_s[1] = q2[pl.ds(0, 8), :]
        s.work(0.6)
        s.quiet = ()
        copy = s.send(halo_s, halo_r, before, "x-", "y-")
        s.done(c_back)
        small_out[pl.ds(2, 1), ch_cols] = jnp.sum(q0[...] * mx[pl.ds(8, GT), :], axis=0, keepdims=True)
        small_out[pl.ds(3, 1), ch_cols] = jnp.sum(q1[pl.ds(0, GT), :] * mx[pl.ds(7, GT), :], axis=0, keepdims=True)
        small_out[pl.ds(4, 1), ch_cols] = jnp.sum(q2[pl.ds(0, GT), :] * mx[pl.ds(6, GT), :], axis=0, keepdims=True)
        s.work(0.3)
        yield [copy]
        last = group == 15
        q1[pl.ds(GT, 8), :] = jnp.where(last, 0.0, halo_r[0])
        q2[pl.ds(GT, 8), :] = jnp.where(last, 0.0, halo_r[1])
        dm = taps[0] * q0[...] + taps[1] * q1[pl.ds(1, GT), :] + taps[2] * q2[pl.ds(2, GT), :]
        dbcv[:, 0:CH] = (dm * bcv[pl.ds(0, GT), CH : 2 * CH]).astype(BF)
        dbcv[:, CH : 2 * CH] = (dm * bcv[pl.ds(0, GT), 0:CH]).astype(BF)
        s.work(0.4)
        s.done(conv_back)
        yield []

        yield from rs_group(3, n1_part)
        dn1 = rs_result(3)
        e1 = dn1 * gain1
        copy = chip_sum(3, e1 * hat1[...])
        s.work(0.4)
        yield [copy]
        m1 = chip_total(3) * (1.0 / D)
        r1 = lax.rsqrt(chip_total(0) * (1.0 / D) + EPS)
        e1 = rs_result(3) * gain1
        tg_out[...] = dh2s[...] + r1 * (e1 - hat1[...] * m1)
        s.work(0.4)

    def small_sums():
        yield [sums]
        yield [s.send(small_out.at[:, peer_cols], redc.at[2], peer, "c")]
        half = small_out[:, my_cols] + redc[2]
        for k, (axis, i, peers) in enumerate((("x", x, xs), ("y", y, ys), ("z", z, zs))):
            red[k, i] = half
            group = Group(red.at[k, pl.ds(0, 3)])
            for j in (2, 1, 3):
                s.send(red.at[k, i], red.at[k, i], peers[j], *links[axis][j], group=group)
            yield [group]
            half = (red[k, 0] + red[k, 1]) + (red[k, 2] + red[k, 3])
            s.work(0.1)
        redc[core] = half
        yield [s.send(redc.at[core], redc.at[core], peer, "c")]
        for h in range(2):
            cols = pl.ds(h * HALF, HALF)
            small_sum[0:2, cols] = redc[h, 0:2] / vec_ref[0:2, cols]
            small_sum[2:8, cols] = redc[h, 2:8]

    block_sent = events(4)

    def send_block(j, k, shared, last):
        yield [shared]
        add_core(1, j)
        if k:
            s.send(zp.at[1, rows_of(j)], zd.at[k - 1], zs[k], *z_links[k], group=last)
        s.done(block_sent[k])

    def hidden_out():
        yield [sent_dh]
        yield from rs_group(2, u_part)
        mix_out[...] = (h2s[...] + rs_result(2)).astype(BF)
        s.work(0.2)

    def make_half(h):
        def step(i):
            ln = lanes[1 + h]
            g1[i, :, :, ln] = tn(n2[:, pl.ds(i * 256, 256)], dab[:, ln]).astype(BF).reshape(4, 64, ln.size)
            s.work(0.3)

        return step

    def make_g2(i):
        g2[i] = tn(dyf[:, pl.ds(i * 256, 256)], uu[...]).astype(BF).reshape(4, 64, HP)
        s.work(0.4)

    def make_g0(i):
        cols = pl.ds(i * 256, 256)
        g0[i, :, :, 2 * CH : 3 * CH] = tn(n1[pl.ds(0, GT), cols], dbcv[:, 2 * CH :]).astype(BF).reshape(4, 64, CH)
        g0[i, :, :, 3 * CH :] = tn(dhb[:, cols], gat[...]).astype(BF).reshape(4, 64, CH)
        s.work(0.2)

    def make_g4(i):
        cols = pl.ds(i * 256, 256)
        g0[i, :, :, 0 : 2 * CH] = tn(n1[pl.ds(0, GT), cols], dbcv[:, 0 : 2 * CH]).astype(BF).reshape(4, 64, 2 * CH)
        s.work(0.2)

    made, summed = events(5), events(5, 2)

    def make(c, after_event, step):
        yield [after_event]
        for i in range(4):
            step(i)
            yield []
        s.done(made[c])

    def reduce_side(c, h, side):
        yield [made[c]]
        yield from side()
        s.done(summed[c][h])

    def hand_back(c):
        yield summed[c]
        ln = grad_lanes[c]

        def rows(j):
            return gs[c].at[y, x, pl.ds(pl.multiple_of(j * 16, 16), 16), ln]

        group = Group(oas[c].at[pl.ds(0, 3), :, ln])
        for k in (1, 3, 2):
            s.send(rows(up(z, k)), oas[c].at[z, :, ln], zs[k], *z_links[k], group=group)
        oas[c][z, :, ln] = rows(z)[...]
        yield [group]
        outs[c][:, :, ln] = oas[c][:, :, ln]
        s.work(0.2)

    s.add(0, halo())
    s.add(0, deal(0))
    s.add(1, first_norm())
    for c in (1, 2, 3):
        s.add(1 + c, deal(c))
    s.add(4, share_codes())
    s.add(6, share_dy())
    for c in range(4):
        for h, side in enumerate(ag_plane(c, issued)):
            s.add(2 + c, gather_side(c, h, side))
    s.add(7, main())
    for c, rank, after_event, step in (
        (1, 3, ffn, make_half(0)),
        (2, 4, ffn, make_half(1)),
        (3, 5, ffn, make_g2),
        (0, 2, c_back, make_g0),
        (4, 1, conv_back, make_g4),
    ):
        s.add(7 + rank, make(c, after_event, step))
        for h, side in enumerate(rs_plane(c)):
            s.add(rank, reduce_side(c, h, side))
        s.add(rank, hand_back(c))
    s.add(13, hidden_out())
    s.add(2, small_sums())
    s.run()


def finish(mix, tg, small, p0, p1, p2, o_mix, o_tg, o_gain1, o_in, o_conv, o_out, o_gain2, o_gate, o_up, o_down):
    o_mix[...] = mix[...]
    o_tg[...] = tg[...]
    o_gain1[...] = small[0]
    o_gain2[...] = small[1]
    o_conv[...] = small[2:5]
    for j in range(R):
        for k in range(3):
            o_in[BVC[k], :, j * CH : (j + 1) * CH] = p0[j, :, k * CH : (k + 1) * CH].astype(F32)
        o_out[:, j * CH : (j + 1) * CH] = p0[j, :, 3 * CH :].astype(F32)
        cols = slice(j * HALF, (j + 1) * HALF)
        o_gate[:, cols] = p1[j, :, 0:HALF].astype(F32)
        o_up[:, cols] = p1[j, :, HALF : 2 * HALF].astype(F32)
        o_down[:, cols] = p2[j, :, 0:HALF].astype(F32)
    for t in range(2):
        tile = slice(2048 + t * CH, 2048 + (t + 1) * CH)
        even, odd = [p1[2 * t + k, :, 2 * HALF :].astype(F32) for k in range(2)]
        o_gate[:, tile] = whole_tile(even, odd)
        o_up[:, tile] = jnp.where(low_lanes(), pltpu.roll(even, CH // 2, 1), odd)
        o_down[:, tile] = whole_tile(p2[2 * t, :, HALF:HP], p2[2 * t + 1, :, HALF:HP])


def block(tokens, dy, seg, valid, gain1, gain2, conv, in_weight, out_weight, gate, up, down):
    vmem = pl.BlockSpec(memory_space=pltpu.VMEM)
    loaded = [
        pltpu.VMEM((TOK, HALF), BF),
        pltpu.VMEM((TOK, HALF), BF),
        pltpu.VMEM((8, D), F32),
        pltpu.VMEM((TOK,), jnp.int32),
        pltpu.VMEM((TOK,), jnp.int32),
        pltpu.VMEM((D,), BF),
        pltpu.VMEM((D,), BF),
        pltpu.VMEM((3, D), BF),
        pltpu.VMEM((3, 16, HALF), BF),
        pltpu.VMEM((16, HALF), BF),
        pltpu.VMEM((16, R * HID), BF),
        pltpu.VMEM((16, R * HID), BF),
        pltpu.VMEM((16, R * HID), BF),
        pltpu.VMEM((8, CH), F32),
    ] + [pltpu.VMEM((R, 16, w), BF) for w in WIDTHS]
    plane = [pltpu.VMEM((4, 4, 64, w), BF) for w in WIDTHS]
    scratch = (
        loaded
        + plane
        + [pltpu.VMEM((4, 4, 64, w), BF) for w in WIDTHS]
        + [pltpu.VMEM((2, 6, 4, 16, w), BF) for w in (2 * CH, 512, HP, HP, 2 * CH)]
        + [pltpu.VMEM((2, 6, 16, w), BF) for w in (2 * CH, 512, HP, HP, 2 * CH)]
        + [pltpu.VMEM((4, 16, w), BF) for w in WIDTHS]
        + [
            pltpu.VMEM((4, 8, CH), F32),
            pltpu.VMEM((16, HALF), BF),
            pltpu.VMEM((4, 8, CH), F32),
            pltpu.VMEM((16, CH), F32),
            pltpu.VMEM((16, CH), F32),
            pltpu.VMEM((4, 16, D), BF),
            pltpu.VMEM((GT + 16, D), BF),
            pltpu.VMEM((GT, D), BF),
            pltpu.VMEM((GT, D), BF),
            pltpu.VMEM((GT, D), BF),
            pltpu.VMEM((4, GT, D), BF),
            pltpu.VMEM((4, GT, HALF), BF),
            pltpu.VMEM((4, GT, HALF), BF),
            pltpu.VMEM((4, 6, TOK // 2, HALF), BF),
            pltpu.VMEM((3, TOK, HALF), BF),
            pltpu.VMEM((4, TOK, CH), F32),
            pltpu.VMEM((4, TOK, CH), F32),
            pltpu.VMEM((TOK, HALF), F32),
            pltpu.VMEM((TOK, HALF), F32),
            pltpu.VMEM((TOK, HALF), F32),
            pltpu.VMEM((TOK, HALF), F32),
            pltpu.VMEM((GT + 16, 3 * CH), F32),
            pltpu.VMEM((GT, 3 * CH), BF),
            pltpu.VMEM((GT, CH), F32),
            pltpu.VMEM((GT, CH), BF),
            pltpu.VMEM((GT + 8, CH), F32),
            pltpu.VMEM((GT + 8, CH), F32),
            pltpu.VMEM((GT, CH), F32),
            pltpu.VMEM((GT + 8, CH), F32),
            pltpu.VMEM((GT + 8, CH), F32),
            pltpu.VMEM((2, 8, CH), F32),
            pltpu.VMEM((2, 8, CH), F32),
            pltpu.VMEM((GT, HP), BF),
            pltpu.VMEM((GT, GW), BF),
            pltpu.VMEM((3, R, 8, HALF), F32),
            pltpu.VMEM((3, 8, HALF), F32),
            pltpu.VMEM((8, D), F32),
            pltpu.SemaphoreType.DMA((12,)),
            pltpu.SemaphoreType.DMA((SENDS,)),
            pltpu.SemaphoreType.DMA((RECEIVES,)),
        ]
    )
    packed = pl.pallas_call(
        kernel,
        out_shape=[
            jax.ShapeDtypeStruct((TOK, HALF), BF),
            jax.ShapeDtypeStruct((TOK, HALF), F32),
            jax.ShapeDtypeStruct((8, D), F32),
        ]
        + [jax.ShapeDtypeStruct((R, 16, w), BF) for w in WIDTHS],
        in_specs=[pl.BlockSpec(memory_space=pl.ANY)] * 12,
        out_specs=[vmem] * 6,
        scratch_shapes=scratch,
        compiler_params=pltpu.CompilerParams(
            collective_id=0, has_side_effects=True, vmem_limit_bytes=58 * 1024 * 1024
        ),
    )(tokens, dy, seg, valid, gain1, gain2, conv, in_weight, out_weight, gate, up, down)
    return pl.pallas_call(
        finish,
        out_shape=[
            jax.ShapeDtypeStruct((TOK, HALF), BF),
            jax.ShapeDtypeStruct((TOK, HALF), F32),
            jax.ShapeDtypeStruct((D,), F32),
            jax.ShapeDtypeStruct((3, 16, HALF), F32),
            jax.ShapeDtypeStruct((3, D), F32),
            jax.ShapeDtypeStruct((16, HALF), F32),
            jax.ShapeDtypeStruct((D,), F32),
            jax.ShapeDtypeStruct((16, R * HID), F32),
            jax.ShapeDtypeStruct((16, R * HID), F32),
            jax.ShapeDtypeStruct((16, R * HID), F32),
        ],
        in_specs=[vmem] * 6,
        out_specs=[vmem] * 10,
    )(*packed)


def local(
    tokens,
    segment_ids,
    valid_mask,
    norm1_gain,
    in_weight,
    conv_weight,
    out_weight,
    norm2_gain,
    gate_weight,
    up_weight,
    down_weight,
    out_cotangent,
):
    outs = list(
        block(
            tokens,
            out_cotangent,
            segment_ids,
            valid_mask,
            norm1_gain,
            norm2_gain,
            conv_weight,
            in_weight,
            out_weight.T,
            gate_weight,
            up_weight,
            down_weight.T,
        )
    )
    outs[5], outs[9] = outs[5].T, outs[9].T
    return tuple(outs)


def solution(mesh):
    placed = (
        P("dp", "tensor"),
        P("dp"),
        P("dp"),
        P(),
        P(None, "dp", "tensor"),
        P(),
        P("tensor", "dp"),
        P(),
        P("dp", "tensor"),
        P("dp", "tensor"),
        P("tensor", "dp"),
        P("dp", "tensor"),
    )
    return jax.shard_map(
        local,
        mesh=mesh,
        in_specs=placed,
        out_specs=(
            P("dp", "tensor"),
            P("dp", "tensor"),
            P(),
            P(None, "dp", "tensor"),
            P(),
            P("tensor", "dp"),
            P(),
            P("dp", "tensor"),
            P("dp", "tensor"),
            P("tensor", "dp"),
        ),
        check_vma=False,
    )
```
